32 devices in a mesh: groups: 2 (over y), tm: 4 (over z), zoom: 2 (over x), pol: 2 (over core).
Axes of the slice: x: 2, y: 2, z: 4, core: 2. Of those that a mesh axis runs over, the one named last changes fastest.
Arguments:
- voltages: bfloat16 [2, 4, 7464960], P('pol', 'groups', ('tm', 'zoom')), parts along dimension 1, may hold values from -6 to 6
- section1_taps: float32 [12, 512], replicated, may hold values from -0.078125 to 0.078125
- section2_taps: float32 [5, 3456], replicated, may hold values from -0.046875 to 0.046875
- band_starts: int32 [4], P('groups'), parts along dimension 0, may hold values from 0 to 511
- band_widths: int32 [4], P('groups'), parts along dimension 0, may hold values from 1 to 20, 24 in all
Outputs:
- fine: float32 [2, 2, 4, 1, 58320], P('pol', 'zoom', 'groups', None, 'tm'), parts along dimension 2
The draws below stay inside these ranges and needn't reach their ends.
There are 2 independent parts, one for each index of `groups`. The reference program is written for one: setup_inputs(seed, part) draws one part's arguments, and reference() takes and returns one part's arrays. A program takes and returns all parts, laid end to end along the dimension named above; an argument that names none is the same for every part. Nothing has to cross between parts.
Inputs may be any that keep to these rules, and one draw needn't show every extreme that they name: `band_widths`: the 2 widths sum to 24, and one band has exactly 20 coarse channels.
All inputs are finite; a program needn't handle non-finite values.
Results may differ from the reference program's by a relative error of at most 0.0069.
Values may be sent and summed in bfloat16 or wider, within the bound.
A program may use at most 192 MiB of HBM per device.

```python
import math
import jax
import jax.numpy as jnp
import numpy as np
from jax import lax

CHAN = 512
HOP = 432
TAPS1 = 12
TAPS2 = 5
FA = 27
FB = 128
FINE = 3456
KEEP = 2916
EDGE = 128
FSPEC = 1
NB = 2
WMAX = 20
LIVE_TOTAL = 24
SPEC_ALL = 17280
SAMPLES = 7464960
POLS = 2


def levels(own_key, extent, shards, smallest, largest):
    factor_of, own = 1.0, jax.random.fold_in(own_key, 6)
    for dim, shards_of in shards:
        heights = jnp.exp(jax.random.uniform(jax.random.fold_in(own, dim), (shards_of,), jnp.float32, smallest / len(shards), largest / len(shards)))
        factor_of = factor_of * jnp.repeat(heights, extent[dim] // shards_of).reshape([-1 if axis == dim else 1 for axis in range(len(extent))])
    return factor_of


def split_up(count, total, bound, skew):
    loads = [(1 << 20) // math.isqrt(standing ** skew) + 1 for standing in range(2, count + 1)]
    surplus, counts = total - bound - (count - 1), [1] * (count - 1)
    while surplus > 0:
        free = [i for i in range(count - 1) if counts[i] < bound]
        whole, remaining = sum([loads[i] for i in free]), surplus
        for i in free:
            more = min(bound - counts[i], max(1, remaining * loads[i] // whole), surplus)
            counts[i] = counts[i] + more
            surplus = surplus - more
    return np.array([bound] + counts)


def uneven(key, amount, total, bound, lean):
    if amount == 2:
        one = jax.random.randint(key, (), max(1, total - bound), min(bound, total - 1) + 1)
        return jnp.stack([one, total - one])
    lengths = jnp.asarray(split_up(amount, total, bound, lean), jnp.int32)
    couples = (amount - 1) // 2
    donor, taker = lengths[1:1 + 2 * couples:2], lengths[2:2 + 2 * couples:2]
    slack = jnp.minimum(donor - 1, bound - taker)
    moved = jax.random.randint(jax.random.fold_in(key, 1), (couples,), 0, 1 << 20) % (slack + 1)
    lengths = lengths.at[1:1 + 2 * couples:2].set(donor - moved).at[2:2 + 2 * couples:2].set(taker + moved)
    return lengths[jax.random.permutation(jax.random.fold_in(key, 2), amount)]


def scatter_about(stream_key, extent, width, bound, cuts=(), held_as=jnp.bfloat16):
    array = width * jax.random.normal(stream_key, extent, jnp.float32)
    if cuts:
        array = array * levels(stream_key, extent, cuts, -0.22, 0.18)
    return jnp.clip(array, -bound, bound).astype(held_as)


def setup_inputs(seed: int = 0, part: int = 0) -> dict:
    key_list = jax.random.split(jax.random.key(seed), 6)
    part_splits = jax.random.split(jax.random.fold_in(key_list[5], part), 6)
    return {
        "voltages": scatter_about(part_splits[0], (POLS, 2, SAMPLES), 1.0, 6.0, ((0, 2), (2, 8))),
        "section1_taps": scatter_about(key_list[1], (TAPS1, CHAN), (TAPS1 * CHAN) ** -0.5, 0.078125, (), jnp.float32),
        "section2_taps": scatter_about(key_list[2], (TAPS2, FINE), (TAPS2 * FINE) ** -0.5, 0.046875, (), jnp.float32),
        "band_starts": jax.random.randint(part_splits[3], (NB,), 0, CHAN).astype(jnp.int32),
        "band_widths": uneven(part_splits[4], NB, LIVE_TOTAL, WMAX, 2).astype(jnp.int32),
    }


def angle_table(rows, cols, length):
    product = (jnp.arange(rows, dtype=jnp.int32)[:, None] * jnp.arange(cols, dtype=jnp.int32)[None, :]) % length
    return product.astype(jnp.float32) * (2.0 * math.pi / length)


def rotation_block(length):
    angles = angle_table(length, length, length)
    cosine_tab = jnp.cos(angles).astype(jnp.bfloat16)
    sine_tab = jnp.sin(angles).astype(jnp.bfloat16)
    return jnp.stack([jnp.stack([cosine_tab, sine_tab]), jnp.stack([-sine_tab, cosine_tab])])


def joined_table(length):
    angles = angle_table(length, length, length)
    cosine_tab = jnp.cos(angles).astype(jnp.bfloat16)
    sine_tab = jnp.sin(angles).astype(jnp.bfloat16)
    top_rows = jnp.concatenate([cosine_tab, -sine_tab], axis=1)
    bottom_rows = jnp.concatenate([sine_tab, cosine_tab], axis=1)
    return jnp.concatenate([top_rows, bottom_rows], axis=0)


def bin_index(radix_a, radix_b, keep_len, edge_len):
    fine_len = radix_a * radix_b
    offsets = (np.arange(keep_len + 2 * edge_len) - keep_len // 2 - edge_len) % fine_len
    base = (offsets % radix_a) * (2 * radix_b) + offsets // radix_a
    return base, base + radix_b


def frame_view(segment, spectra, chan_len, hop_len):
    pieces = -(-chan_len // hop_len)
    framed = segment[:, :(spectra + pieces - 1) * hop_len].reshape(segment.shape[0], spectra + pieces - 1, hop_len)
    joined = jnp.concatenate([framed[:, offset:offset + spectra] for offset in range(pieces)], axis=2)
    return joined[:, :, :chan_len]


def weighted_frames(signal, taps, spectra, hop_len):
    chan_len = taps.shape[1]
    running = jnp.zeros((2, spectra, chan_len), jnp.float32)
    for tap_index in range(taps.shape[0]):
        frames = frame_view(signal[:, tap_index * chan_len:], spectra, chan_len, hop_len)
        running = running + taps[tap_index][None, None, :] * frames.astype(jnp.float32)
    return running.astype(jnp.bfloat16)


def fine_spectra(series, section2_taps, radix_a, radix_b, keep_len, edge_len):
    tap_count, fine_len = section2_taps.shape
    items = series.shape[1]
    row_count = series.shape[2] // fine_len
    spectra = row_count - tap_count + 1
    row_blocks = series.reshape(2, items, row_count, fine_len)
    running = jnp.zeros((2, items, spectra, fine_len), jnp.float32)
    for tap_index in range(tap_count):
        running = running + section2_taps[tap_index] * row_blocks[:, :, tap_index:tap_index + spectra].astype(jnp.float32)
    weighted = running.astype(jnp.bfloat16).reshape(2, items, spectra, radix_a, radix_b)
    partial_value = jnp.einsum("pqkm,qcfmb->pcfkb", rotation_block(radix_a).astype(jnp.float32), weighted.astype(jnp.float32), precision=lax.Precision.HIGHEST)
    angles = angle_table(radix_a, radix_b, fine_len)
    cosine_tab = jnp.cos(angles)
    sine_tab = jnp.sin(angles)
    real_part = partial_value[0] * cosine_tab + partial_value[1] * sine_tab
    imag_part = partial_value[1] * cosine_tab - partial_value[0] * sine_tab
    twiddled = jnp.concatenate([real_part, imag_part], axis=-1).astype(jnp.bfloat16)
    spectrum = jnp.einsum("cfkm,mj->cfkj", twiddled.astype(jnp.float32), joined_table(radix_b).astype(jnp.float32), precision=lax.Precision.HIGHEST)
    flattened = spectrum.reshape(items, spectra, radix_a * 2 * radix_b)
    real_index, imag_index = bin_index(radix_a, radix_b, keep_len, edge_len)
    return jnp.stack([jnp.take(flattened, real_index, axis=2), jnp.take(flattened, imag_index, axis=2)])


def stitch_bands(extended, upper_rim, lower_rim, slot_ids, band_width, keep_len, edge_len):
    centre = extended[..., edge_len:edge_len + keep_len]
    live = (slot_ids < band_width).astype(jnp.float32)[None, :, None, None]
    upper_ok = (slot_ids + 1 < band_width).astype(jnp.float32)[None, :, None, None]
    lower_ok = ((slot_ids >= 1) & (slot_ids < band_width)).astype(jnp.float32)[None, :, None, None]
    ramp = (jnp.arange(edge_len, dtype=jnp.float32) + 0.5) / (2.0 * edge_len)
    upper_weight = ramp * upper_ok
    lower_weight = ramp[::-1] * lower_ok
    low_part = centre[..., :edge_len] * (1.0 - lower_weight) + lower_rim * lower_weight
    high_part = centre[..., keep_len - edge_len:] * (1.0 - upper_weight) + upper_rim * upper_weight
    joined = jnp.concatenate([low_part, centre[..., edge_len:keep_len - edge_len], high_part], axis=-1)
    return joined * live


def reference(voltages, section1_taps, section2_taps, band_starts, band_widths):
    chan_len = section1_taps.shape[1]
    pieces = -(-chan_len // HOP)
    rotation = rotation_block(chan_len).astype(jnp.float32)
    slot_ids = jnp.arange(WMAX, dtype=jnp.int32)
    results = []
    for pol_index in range(POLS):
        signal = jnp.pad(voltages[pol_index], ((0, 0), (0, TAPS1 * chan_len + pieces * HOP)))
        weighted = weighted_frames(signal, section1_taps, SPEC_ALL, HOP)
        coarse = jnp.einsum("pqkn,qsn->pks", rotation, weighted.astype(jnp.float32), precision=lax.Precision.HIGHEST).astype(jnp.bfloat16)

        def one_band(pair):
            start, band_width = pair
            channels = ((start + slot_ids) % chan_len).astype(jnp.int32)
            series = jnp.take(coarse, channels, axis=1)
            extended = fine_spectra(series, section2_taps, FA, FB, KEEP, EDGE)
            zero_rim = jnp.zeros_like(extended[:, :1, :, :EDGE])
            upper_rim = jnp.concatenate([extended[:, 1:, :, :EDGE], zero_rim], axis=1)
            lower_rim = jnp.concatenate([zero_rim, extended[:, :-1, :, KEEP + EDGE:]], axis=1)
            stitched = stitch_bands(extended, upper_rim, lower_rim, slot_ids, band_width, KEEP, EDGE)
            return jnp.transpose(stitched, (0, 2, 1, 3)).reshape(2, FSPEC, WMAX * KEEP)

        results.append(lax.map(one_band, (band_starts, band_widths)))
    return jnp.stack(results)
```

```python
import functools
import math

import jax
import jax.numpy as jnp
import numpy as np
from jax import lax
from jax.experimental import pallas as pl
from jax.experimental.pallas import tpu as pltpu
from jax.sharding import PartitionSpec as P

HOP = 432
FA = 27
FB = 128
KEEP = 2916
EDGE = 128
CH_DEV = 5
LIVE_DEV = 3


def shifted(value, axis, steps):
    count = lax.axis_size(axis)
    initial, last = (max(0, -steps), min(count, count - steps))
    return lax.ppermute(value, axis, [(source, source + steps) for source in range(initial, last)])


def angle_table(rows, cols, length):
    product = (
        jnp.arange(rows, dtype=jnp.int32)[:, None]
        * jnp.arange(cols, dtype=jnp.int32)[None, :]
        % length
    )
    return product.astype(jnp.float32) * (2.0 * math.pi / length)


def rotation_block(length):
    angles = angle_table(length, length, length)
    cosine_tab = jnp.cos(angles).astype(jnp.bfloat16)
    sine_tab = jnp.sin(angles).astype(jnp.bfloat16)
    return jnp.stack([jnp.stack([cosine_tab, sine_tab]), jnp.stack([-sine_tab, cosine_tab])])


def frame_view(segment, spectra, chan_len, hop_len):
    pieces = -(-chan_len // hop_len)
    framed = segment[:, : (spectra + pieces - 1) * hop_len].reshape(
        segment.shape[0], spectra + pieces - 1, hop_len
    )
    joined = jnp.concatenate(
        [framed[:, offset : offset + spectra] for offset in range(pieces)], axis=2
    )
    return joined[:, :, :chan_len]


def weighted_frames(signal, taps, spectra, hop_len):
    chan_len = taps.shape[1]
    running = jnp.zeros((2, spectra, chan_len), jnp.float32)
    for tap_index in range(taps.shape[0]):
        frames = frame_view(signal[:, tap_index * chan_len :], spectra, chan_len, hop_len)
        running = running + taps[tap_index][None, None, :] * frames.astype(jnp.float32)
    return running.astype(jnp.bfloat16)


def natural_order(series, section2_taps, radix_a, radix_b):
    tap_count, fine_len = section2_taps.shape
    items = series.shape[1]
    row_count = series.shape[2] // fine_len
    spectra = row_count - tap_count + 1
    row_blocks = series.reshape(2, items, row_count, fine_len)
    running = jnp.zeros((2, items, spectra, fine_len), jnp.float32)
    for tap_index in range(tap_count):
        running = running + section2_taps[tap_index] * row_blocks[
            :, :, tap_index : tap_index + spectra
        ].astype(jnp.float32)
    weighted = running.astype(jnp.bfloat16).reshape(2, items, spectra, radix_a, radix_b)
    return weighted, np.arange(radix_b)


def phase_order(received, section2_taps, radix_a, radix_b):
    tap_count, fine_len = section2_taps.shape
    sources, _, lines, rows = received.shape
    items = lines // GROUP
    short = fine_len // GROUP
    row_count = sources * rows // short
    spectra = row_count - tap_count + 1
    lanes = jnp.transpose(received, (1, 2, 0, 3)).reshape(2, items, GROUP, row_count, short)
    taps = jnp.transpose(section2_taps.reshape(tap_count, short, GROUP), (0, 2, 1))
    running = jnp.zeros((2, items, GROUP, spectra, short), jnp.float32)
    for tap_index in range(tap_count):
        running = running + taps[tap_index][:, None, :] * lanes[
            :, :, :, tap_index : tap_index + spectra
        ].astype(jnp.float32)
    inner = radix_b // GROUP
    weighted = running.astype(jnp.bfloat16).reshape(2, items, GROUP, spectra, radix_a, inner)
    weighted = jnp.transpose(weighted, (0, 1, 3, 4, 2, 5)).reshape(
        2, items, spectra, radix_a, radix_b
    )
    order = (np.arange(GROUP)[:, None] + GROUP * np.arange(inner)[None, :]).reshape(-1)
    return weighted, order


def ordered_angles(rows, order, length):
    product = (np.arange(rows)[:, None] * order[None, :] % length).astype(np.float32)
    return jnp.asarray(product) * (2.0 * math.pi / length)


def fine_spectra(weighted, order, keep_len, edge_len):
    _, items, spectra, radix_a, radix_b = weighted.shape
    fine_len = radix_a * radix_b
    partial_value = jnp.einsum(
        "pqkm,qcfmb->pcfkb", rotation_block(radix_a), weighted, preferred_element_type=jnp.float32
    )
    angles = ordered_angles(radix_a, order, fine_len)
    cosine_tab = jnp.cos(angles)
    sine_tab = jnp.sin(angles)
    real_part = partial_value[0] * cosine_tab + partial_value[1] * sine_tab
    imag_part = partial_value[1] * cosine_tab - partial_value[0] * sine_tab
    twiddled = jnp.concatenate([real_part, imag_part], axis=-1).astype(jnp.bfloat16)
    turned = ordered_angles(radix_b, order, radix_b).T
    cosine_b = jnp.cos(turned).astype(jnp.bfloat16)
    sine_b = jnp.sin(turned).astype(jnp.bfloat16)
    table = jnp.concatenate(
        [jnp.stack([cosine_b, -sine_b], axis=1), jnp.stack([sine_b, cosine_b], axis=1)], axis=0
    )
    spectrum = jnp.einsum(
        "cfkm,mpq->pcfqk", twiddled, table, preferred_element_type=jnp.float32
    ).reshape(2, items, spectra, fine_len)
    first = (-(keep_len // 2) - edge_len) % fine_len
    rest = keep_len + 2 * edge_len - (fine_len - first)
    return jnp.concatenate([spectrum[..., first:], spectrum[..., :rest]], axis=-1)


def stitch_bands(extended, upper_rim, lower_rim, slot_ids, band_width, keep_len, edge_len):
    centre = extended[..., edge_len : edge_len + keep_len]
    live = (slot_ids < band_width).astype(jnp.float32)[None, :, None, None]
    upper_ok = (slot_ids + 1 < band_width).astype(jnp.float32)[None, :, None, None]
    lower_ok = ((slot_ids >= 1) & (slot_ids < band_width)).astype(jnp.float32)[None, :, None, None]
    ramp = (jnp.arange(edge_len, dtype=jnp.float32) + 0.5) / (2.0 * edge_len)
    upper_weight = ramp * upper_ok
    lower_weight = ramp[::-1] * lower_ok
    low_part = centre[..., :edge_len] * (1.0 - lower_weight) + lower_rim * lower_weight
    high_part = centre[..., keep_len - edge_len :] * (1.0 - upper_weight) + upper_rim * upper_weight
    joined = jnp.concatenate(
        [low_part, centre[..., edge_len : keep_len - edge_len], high_part], axis=-1
    )
    return joined * live


GROUP = 8
CHUNK = 1152


def bank_kernel(
    turns, per_row, pick_ref, x_ref, rim_ref, taps_ref, rot_ref, out_ref, tail_ref, data, bank, total, mix, turned
):
    step = pl.program_id(0)
    rows = x_ref.shape[1]
    halves = data.shape[1] // 2
    base = halves - rim_ref.shape[1]
    half = rot_ref.shape[1] // 2
    rot_len = rot_ref.shape[0]
    piece = 128

    @pl.when(step == 0)
    def _():
        total[...] = jnp.zeros_like(total)

    @pl.when(step < per_row)
    def _():
        for part in range(2):
            data[step, pl.ds(part * halves, rows), :] = x_ref[part]
            data[step, pl.ds(part * halves + base, halves - base), :] = rim_ref[part]

    @pl.loop(0, CHUNK // piece)
    def _(index):
        row = pl.multiple_of(index * piece, piece)
        turn = pl.multiple_of((step * CHUNK + row) % rot_len, piece)
        wide = jnp.transpose(jnp.tile(taps_ref[:, pl.ds(row, piece)], (piece // GROUP, 1)))
        for col in range(0, 2 * half, piece):
            bank[pl.ds(row, piece), pl.ds(col, piece)] = (
                wide * rot_ref[pl.ds(turn, piece), pl.ds(col, piece)]
            ).astype(jnp.bfloat16)

    total[step // per_row] += jnp.dot(
        data[step % per_row], bank[...], preferred_element_type=jnp.float32
    )

    @pl.when(step == pl.num_programs(0) - 1)
    def _():
        for shift in range(1, turns):
            for part in range(2):
                total[shift, pl.ds(part * halves + rows, shift), :] = total[
                    shift, pl.ds(part * halves + base, shift), :
                ]
        for part in range(2):
            whole = jnp.zeros((rows, half), jnp.float32)
            for shift in range(turns):
                upper = total[shift, pl.ds(shift, rows), pl.ds(part * half, half)]
                lower = total[shift, pl.ds(halves + shift, rows), pl.ds((1 - part) * half, half)]
                whole += upper + lower if part == 0 else lower - upper
            mix[pl.ds(0, rows), pl.ds(0, half)] = whole
            turned[part] = jnp.transpose(mix[...])[:half]
        dests, lines, main = out_ref.shape
        width = lines // (2 * GROUP)
        fill = -(-lines // 128) * 128 - lines

        @pl.loop(0, dests)
        def _(dest):
            blocks = []
            for part in range(2):
                for slot in range(width):
                    line = pl.multiple_of(pick_ref[dest * width + slot] * GROUP, GROUP)
                    blocks.append(turned[part, pl.ds(line, GROUP), :])
            block = jnp.concatenate(blocks, axis=0)
            out_ref[dest] = block[:, :main].astype(jnp.bfloat16)
            spare = jnp.zeros((fill, turned.shape[2] - main), jnp.float32)
            rest = jnp.transpose(jnp.concatenate([block[:, main:], spare], axis=0))
            tail_ref[dest] = rest[: tail_ref.shape[1], :lines].astype(jnp.bfloat16)


def slot_bank(signal, following, taps, channels, spectra, picks):
    tap_count, chan_len = taps.shape
    row_len = GROUP * HOP
    rows = spectra // GROUP
    reach = (GROUP - 1) * HOP + tap_count * chan_len
    steps = -(-reach // CHUNK)
    per_row = row_len // CHUNK
    turns = -(-steps // per_row)
    rim = 16
    halves = -(-rows // 16) * 16 + rim
    data = signal.reshape(2, rows, row_len)
    fill = rim * row_len - following.shape[1]
    edge = jnp.pad(following, ((0, 0), (0, fill))).reshape(2, rim, row_len)
    flat = taps.reshape(-1)
    spread = jnp.stack(
        [
            jnp.pad(flat, (phase * HOP, steps * CHUNK - flat.shape[0] - phase * HOP))
            for phase in range(GROUP)
        ]
    )
    chans = channels.shape[0]
    half = GROUP * chans
    places = (np.arange(chan_len)[:, None] - HOP * np.arange(GROUP)[None, :]) % chan_len
    places = jnp.asarray(places.astype(np.int32))
    turns_of = (places[:, None, :] * channels[None, :, None]).reshape(chan_len, half) % chan_len
    angles = turns_of.astype(jnp.float32) * (2.0 * math.pi / chan_len)
    rot = jnp.concatenate([jnp.cos(angles), jnp.sin(angles)], axis=1)
    rot = rot.astype(jnp.bfloat16).astype(jnp.float32)
    deep = -(-rows // 128) * 128
    wide = -(-half // 128) * 128
    main = rows // 128 * 128
    lines = 2 * picks.shape[1] * GROUP
    shape = (picks.shape[0], lines, main)
    tail = (picks.shape[0], -(-(rows - main) // 16) * 16, lines)
    return pl.pallas_call(
        functools.partial(bank_kernel, turns, per_row),
        out_shape=(
            jax.ShapeDtypeStruct(shape, jnp.bfloat16),
            jax.ShapeDtypeStruct(tail, jnp.bfloat16),
        ),
        grid_spec=pltpu.PrefetchScalarGridSpec(
            num_scalar_prefetch=1,
            grid=(steps,),
            in_specs=[
                pl.BlockSpec((2, rows, CHUNK), lambda i, p: (0, 0, jnp.minimum(i, per_row - 1))),
                pl.BlockSpec((2, rim, CHUNK), lambda i, p: (0, 0, jnp.minimum(i, per_row - 1))),
                pl.BlockSpec((GROUP, CHUNK), lambda i, p: (0, i)),
                pl.BlockSpec((chan_len, 2 * half), lambda i, p: (0, 0)),
            ],
            out_specs=(
                pl.BlockSpec(shape, lambda i, p: (0, 0, 0)),
                pl.BlockSpec(tail, lambda i, p: (0, 0, 0)),
            ),
            scratch_shapes=[
            pltpu.VMEM((per_row, 2 * halves, CHUNK), jnp.bfloat16),
            pltpu.VMEM((CHUNK, 2 * half), jnp.bfloat16),
            pltpu.VMEM((turns, 2 * halves, 2 * half), jnp.float32),
            pltpu.VMEM((deep, wide), jnp.float32),
            pltpu.VMEM((2, half, deep), jnp.float32),
            ],
        ),
        name="slot_bank",
    )(picks.reshape(-1), data, edge, spread, rot)


def swap_kernel(zooms, in_ref, in_tail, out_ref, out_tail, send_sems, recv_sems):
    count = in_ref.shape[0]
    me = lax.axis_index("tm") * zooms + lax.axis_index("zoom")
    barrier = pltpu.get_barrier_semaphore()

    def place(step):
        other = lax.rem(me + step, count)
        return other, {"tm": other // zooms, "zoom": lax.rem(other, zooms)}

    for step in range(1, count):
        pl.semaphore_signal(
            barrier, inc=1, device_id=place(step)[1], device_id_type=pl.DeviceIdType.MESH
        )
    pl.semaphore_wait(barrier, count - 1)
    copies = []
    for step in range(1, count):
        other, where = place(step)
        for which, (source, target) in enumerate(((in_ref, out_ref), (in_tail, out_tail))):
            copy = pltpu.make_async_remote_copy(
                src_ref=source.at[other],
                dst_ref=target.at[me],
                send_sem=send_sems.at[which, step],
                recv_sem=recv_sems.at[which, step],
                device_id=where,
                device_id_type=pl.DeviceIdType.MESH,
            )
            copy.start()
            copies.append(copy)
    out_ref[me] = in_ref[me]
    out_tail[me] = in_tail[me]
    for copy in copies:
        copy.wait()


def swapped(packed, tail, zooms, rows):
    count, lines, main = packed.shape
    body, rest = pl.pallas_call(
        functools.partial(swap_kernel, zooms),
        out_shape=tuple(jax.ShapeDtypeStruct(x.shape, x.dtype) for x in (packed, tail)),
        in_specs=[pl.BlockSpec(memory_space=pltpu.VMEM)] * 2,
        out_specs=(pl.BlockSpec(memory_space=pltpu.VMEM),) * 2,
        scratch_shapes=[
            pltpu.SemaphoreType.DMA((2, count)),
            pltpu.SemaphoreType.DMA((2, count)),
        ],
        compiler_params=pltpu.CompilerParams(collective_id=0, has_side_effects=True),
        name="swap_slots",
    )(packed, tail)
    rest = jnp.transpose(rest, (0, 2, 1))[:, :, : rows - main]
    return jnp.concatenate([body, rest], axis=2).reshape(count, 2, lines // 2, rows)


def on_device(voltages, section1_taps, section2_taps, band_starts, band_widths):
    signal = voltages[0]
    tap_count, chan_len = section1_taps.shape
    spectra = signal.shape[1] // HOP
    rim_len = tap_count * chan_len - HOP
    tm_count = lax.axis_size("tm")
    zoom_count = lax.axis_size("zoom")
    device_count = tm_count * zoom_count
    slot_count = tm_count * CH_DEV
    width = CH_DEV + 2
    following = shifted(signal[:, :rim_len], ("tm", "zoom"), -1)
    span = slot_count + 2
    band_slots = jnp.arange(-1, slot_count + 1, dtype=jnp.int32)
    channels = ((band_starts[:, None] + band_slots[None, :]) % chan_len).reshape(-1)
    picks = [tm * CH_DEV + zoom * span for tm in range(tm_count) for zoom in range(zoom_count)]
    live_count = LIVE_DEV * device_count
    ragged = spectra // GROUP % 128
    if live_count <= 48 and spectra % GROUP == 0 and spectra // GROUP > 128 and ragged:
        before = np.tri(band_widths.shape[0], dtype=np.int32)
        band_ends = jnp.sum(before * band_widths[None, :], axis=1)
        band_firsts = band_ends - band_widths
        live_ids = jnp.arange(live_count, dtype=jnp.int32)
        band_of = jnp.sum((band_ends[None, :] <= live_ids[:, None]).astype(jnp.int32), axis=1)
        member = band_of[:, None] == jnp.arange(zoom_count, dtype=jnp.int32)[None, :]
        shifts = jnp.where(member, (band_starts - band_firsts)[None, :], 0)
        channels = (jnp.sum(shifts, axis=1) + live_ids) % chan_len
        slots = np.arange(tm_count)[:, None, None] * CH_DEV + np.arange(-1, CH_DEV + 1)
        slots = jnp.asarray(slots.astype(np.int32)) + band_firsts[None, :, None]
        lines = jnp.clip(slots, 0, live_count - 1).reshape(device_count, width)
        packed, tail = slot_bank(signal, following, section1_taps, channels, spectra, lines)
        received = swapped(packed, tail, zoom_count, spectra // GROUP)
        weighted, order = phase_order(received, section2_taps, FA, FB)
    else:
        pieces = -(-chan_len // HOP)
        padded = jnp.concatenate(
            [signal, following, jnp.zeros((2, pieces * HOP), jnp.bfloat16)], axis=1
        )
        frames = weighted_frames(padded, section1_taps, spectra, HOP)
        coarse = jnp.einsum(
            "pqkn,qsn->pks", rotation_block(chan_len), frames, preferred_element_type=jnp.float32
        ).astype(jnp.bfloat16)
        wanted = np.arange(width)[:, None] + np.asarray(picks)[None, :]
        hot = channels[wanted.reshape(-1)][:, None] == jnp.arange(chan_len, dtype=jnp.int32)[None, :]
        packed = jnp.einsum(
            "lk,pks->pls", hot.astype(jnp.bfloat16), coarse, preferred_element_type=jnp.float32
        ).astype(jnp.bfloat16)
        packed = packed.reshape(2, width, device_count, spectra)
        received = lax.all_to_all(packed, ("tm", "zoom"), split_axis=2, concat_axis=2, tiled=True)
        series = received.reshape(2, width, -1)
        weighted, order = natural_order(series, section2_taps, FA, FB)
    spans = fine_spectra(weighted, order, KEEP, EDGE)
    slot_ids = lax.axis_index("tm") * CH_DEV + jnp.arange(CH_DEV, dtype=jnp.int32)
    band_ids = jnp.arange(band_widths.shape[0], dtype=jnp.int32)
    band_width = jnp.sum(jnp.where(band_ids == lax.axis_index("zoom"), band_widths, 0))
    upper_rim = spans[:, 2:, :, :EDGE]
    lower_rim = spans[:, :CH_DEV, :, KEEP + EDGE :]
    extended = spans[:, 1 : CH_DEV + 1]
    stitched = stitch_bands(extended, upper_rim, lower_rim, slot_ids, band_width, KEEP, EDGE)
    fine_count = stitched.shape[2]
    result = jnp.transpose(stitched, (0, 2, 1, 3)).reshape(2, fine_count, CH_DEV * KEEP)
    return result[None, None]


def solution(mesh):
    placed = (P("pol", "groups", ("tm", "zoom")), P(), P(), P("groups"), P("groups"))
    return jax.shard_map(
        on_device,
        mesh=mesh,
        in_specs=placed,
        out_specs=P("pol", "zoom", "groups", None, "tm"),
        check_vma=False,
    )
```

```python
import functools
import math

import jax
import jax.numpy as jnp
import numpy as np
from jax import lax
from jax.experimental import pallas as pl
from jax.experimental.pallas import tpu as pltpu
from jax.sharding import PartitionSpec as P

HOP = 432
FA = 27
FB = 128
KEEP = 2916
EDGE = 128
CH_DEV = 5
LIVE_DEV = 3


def shifted(value, axis, steps):
    count = lax.axis_size(axis)
    initial, last = (max(0, -steps), min(count, count - steps))
    return lax.ppermute(value, axis, [(source, source + steps) for source in range(initial, last)])


def angle_table(rows, cols, length):
    product = (
        jnp.arange(rows, dtype=jnp.int32)[:, None]
        * jnp.arange(cols, dtype=jnp.int32)[None, :]
        % length
    )
    return product.astype(jnp.float32) * (2.0 * math.pi / length)


def rotation_block(length):
    angles = angle_table(length, length, length)
    cosine_tab = jnp.cos(angles).astype(jnp.bfloat16)
    sine_tab = jnp.sin(angles).astype(jnp.bfloat16)
    return jnp.stack([jnp.stack([cosine_tab, sine_tab]), jnp.stack([-sine_tab, cosine_tab])])


def frame_view(segment, spectra, chan_len, hop_len):
    pieces = -(-chan_len // hop_len)
    framed = segment[:, : (spectra + pieces - 1) * hop_len].reshape(
        segment.shape[0], spectra + pieces - 1, hop_len
    )
    joined = jnp.concatenate(
        [framed[:, offset : offset + spectra] for offset in range(pieces)], axis=2
    )
    return joined[:, :, :chan_len]


def weighted_frames(signal, taps, spectra, hop_len):
    chan_len = taps.shape[1]
    running = jnp.zeros((2, spectra, chan_len), jnp.float32)
    for tap_index in range(taps.shape[0]):
        frames = frame_view(signal[:, tap_index * chan_len :], spectra, chan_len, hop_len)
        running = running + taps[tap_index][None, None, :] * frames.astype(jnp.float32)
    return running.astype(jnp.bfloat16)


def natural_order(series, section2_taps, radix_a, radix_b):
    tap_count, fine_len = section2_taps.shape
    items = series.shape[1]
    row_count = series.shape[2] // fine_len
    spectra = row_count - tap_count + 1
    row_blocks = series.reshape(2, items, row_count, fine_len)
    running = jnp.zeros((2, items, spectra, fine_len), jnp.float32)
    for tap_index in range(tap_count):
        running = running + section2_taps[tap_index] * row_blocks[
            :, :, tap_index : tap_index + spectra
        ].astype(jnp.float32)
    weighted = running.astype(jnp.bfloat16).reshape(2, items, spectra, radix_a, radix_b)
    return weighted, np.arange(radix_b)


def ordered_angles(rows, order, length):
    product = (np.arange(rows)[:, None] * order[None, :] % length).astype(np.float32)
    return jnp.asarray(product) * (2.0 * math.pi / length)


def fine_spectra(weighted, order, keep_len, edge_len):
    _, items, spectra, radix_a, radix_b = weighted.shape
    fine_len = radix_a * radix_b
    partial_value = jnp.einsum(
        "pqkm,qcfmb->pcfkb", rotation_block(radix_a), weighted, preferred_element_type=jnp.float32
    )
    angles = ordered_angles(radix_a, order, fine_len)
    cosine_tab = jnp.cos(angles)
    sine_tab = jnp.sin(angles)
    real_part = partial_value[0] * cosine_tab + partial_value[1] * sine_tab
    imag_part = partial_value[1] * cosine_tab - partial_value[0] * sine_tab
    twiddled = jnp.concatenate([real_part, imag_part], axis=-1).astype(jnp.bfloat16)
    turned = ordered_angles(radix_b, order, radix_b).T
    cosine_b = jnp.cos(turned).astype(jnp.bfloat16)
    sine_b = jnp.sin(turned).astype(jnp.bfloat16)
    table = jnp.concatenate(
        [jnp.stack([cosine_b, -sine_b], axis=1), jnp.stack([sine_b, cosine_b], axis=1)], axis=0
    )
    spectrum = jnp.einsum(
        "cfkm,mpq->pcfqk", twiddled, table, preferred_element_type=jnp.float32
    ).reshape(2, items, spectra, fine_len)
    first = (-(keep_len // 2) - edge_len) % fine_len
    rest = keep_len + 2 * edge_len - (fine_len - first)
    return jnp.concatenate([spectrum[..., first:], spectrum[..., :rest]], axis=-1)


def stitch_bands(extended, upper_rim, lower_rim, slot_ids, band_width, keep_len, edge_len):
    centre = extended[..., edge_len : edge_len + keep_len]
    live = (slot_ids < band_width).astype(jnp.float32)[None, :, None, None]
    upper_ok = (slot_ids + 1 < band_width).astype(jnp.float32)[None, :, None, None]
    lower_ok = ((slot_ids >= 1) & (slot_ids < band_width)).astype(jnp.float32)[None, :, None, None]
    ramp = (jnp.arange(edge_len, dtype=jnp.float32) + 0.5) / (2.0 * edge_len)
    upper_weight = ramp * upper_ok
    lower_weight = ramp[::-1] * lower_ok
    low_part = centre[..., :edge_len] * (1.0 - lower_weight) + lower_rim * lower_weight
    high_part = centre[..., keep_len - edge_len :] * (1.0 - upper_weight) + upper_rim * upper_weight
    joined = jnp.concatenate(
        [low_part, centre[..., edge_len : keep_len - edge_len], high_part], axis=-1
    )
    return joined * live


GROUP = 8
LANE = 128
SLOT = 64
PART = 32
FAST = 4


def sine(x):
    square = x * x
    total = jnp.full_like(x, -1.0 / 39916800.0)
    for factor in (1.0 / 362880.0, -1.0 / 5040.0, 1.0 / 120.0, -1.0 / 6.0, 1.0):
        total = total * square + factor
    return total * x


def fill_bank(starts_ref, widths_ref, taps_ref, rot_len, hop, lead, live, bank, spread):
    lanes = lax.broadcasted_iota(jnp.int32, (LANE, LANE), 1)
    upper = lanes // SLOT
    quarter = (lanes % SLOT) // PART
    member = lanes % PART
    channel = jnp.where(
        member < widths_ref[0], starts_ref[0] + member, starts_ref[1] + (live - 1) - member
    )
    rows_of = lax.broadcasted_iota(jnp.int32, (LANE, LANE), 0)
    steps = taps_ref.shape[0]
    rolled = pltpu.roll(taps_ref[...], hop, 1)
    down = pltpu.roll(rolled, 1, 0)
    behind = jnp.where(lax.broadcasted_iota(jnp.int32, rolled.shape, 1) < hop, down, rolled)
    spread[pl.ds(0, steps), :] = taps_ref[...]
    spread[pl.ds(steps, steps), :] = behind
    for block in range(rot_len // LANE):
        turned = jnp.transpose(spread[:, pl.ds(block * LANE, LANE)])
        place = rows_of + block * LANE - upper * hop
        turn = (place * channel - quarter * (rot_len // 4)) & (rot_len - 1)
        half = rot_len // 2
        angle = (jnp.abs(turn - half) - half // 2).astype(jnp.float32) * (2.0 * math.pi / rot_len)
        rot = sine(angle).astype(jnp.bfloat16).astype(jnp.float32)
        for tap in range(steps - 3):
            taken = jnp.take_along_axis(turned, upper * steps + tap, axis=1)
            bank[pl.ds(lead + tap * rot_len + block * LANE, LANE), :] = (taken * rot).astype(jnp.bfloat16)


def beam_kernel(
    cfg,
    starts_ref,
    widths_ref,
    taps_ref,
    tapw_ref,
    twist_ref,
    eight_ref,
    x_ref,
    table_ref,
    out_ref,
    data,
    bank,
    spread,
    total,
    turned,
    send_a,
    send_b,
    recv_a,
    recv_b,
    table,
    pair,
    gathered,
    flat,
    x_sems,
    table_sem,
    halo_sems,
    send_sems,
    recv_sems,
    out_sems,
    in_sems,
):
    tms, zooms, hop, rot_len, reach, slots, keep, edge, folded, homes, needs = cfg
    per = len(homes[0])
    live = per * len(homes)
    rows, blocks = x_ref.shape[0], x_ref.shape[1]
    row_len = blocks * LANE
    count = tms * zooms
    tm = lax.axis_index("tm")
    zoom = lax.axis_index("zoom")
    me = tm * zooms + zoom
    gathered[...] = jnp.zeros_like(gathered)
    barrier = pltpu.get_barrier_semaphore()

    def where_is(index):
        return {"tm": index // zooms, "zoom": lax.rem(index, zooms)}

    for step in range(1, count):
        pl.semaphore_signal(
            barrier,
            inc=1,
            device_id=where_is(lax.rem(me + step, count)),
            device_id_type=pl.DeviceIdType.MESH,
        )
    held = data.shape[1]
    cut = held // 2
    spans = ((0, cut), (cut, rows - cut))
    loads = []
    for which, (start, size) in enumerate(spans):
        loads.append([])
        for block in range(blocks):
            copy = pltpu.make_async_copy(
                x_ref.at[pl.ds(start, size), block],
                data.at[block, pl.ds(start, size)],
                x_sems.at[which, block],
            )
            copy.start()
            loads[which].append(copy)
    table_copy = pltpu.make_async_copy(table_ref, table, table_sem)
    table_copy.start()
    rest = -(-(reach - row_len) // LANE)
    data[pl.ds(rest, blocks - rest), pl.ds(rows + 1, 1)] = jnp.zeros(
        (blocks - rest, 1, 2, LANE), data.dtype
    )

    @pl.when(me == count - 1)
    def _():
        data[:, pl.ds(rows, 1)] = jnp.zeros((blocks, 1, 2, LANE), data.dtype)
        data[pl.ds(0, rest), pl.ds(rows + 1, 1)] = jnp.zeros((rest, 1, 2, LANE), data.dtype)

    columns = GROUP * SLOT
    wide = 2 * LANE
    tiles = columns // wide
    apart = 2 * hop
    lead = (columns // LANE - 1) * apart
    turns = total.shape[0]
    total[:, pl.ds(2 * held, total.shape[1] - 2 * held), :] = jnp.zeros(
        (turns, total.shape[1] - 2 * held, columns), jnp.float32
    )
    bank[pl.ds(0, lead), :] = jnp.zeros((lead, LANE), jnp.bfloat16)
    tail = lead + (taps_ref.shape[0] - 3) * rot_len
    bank[pl.ds(tail, bank.shape[0] - tail), :] = jnp.zeros((bank.shape[0] - tail, LANE), jnp.bfloat16)
    fill_bank(
        starts_ref, widths_ref, taps_ref, rot_len, hop, lead, live, bank, spread
    )
    pl.semaphore_wait(barrier, count - 1)
    before = lax.rem(me + count - 1, count)
    halo = [
        pltpu.make_async_remote_copy(
            src_ref=source,
            dst_ref=target,
            send_sem=halo_sems.at[0, index],
            recv_sem=halo_sems.at[1, index],
            device_id=where_is(before),
            device_id_type=pl.DeviceIdType.MESH,
        )
        for index, (source, target) in enumerate(
            (
                (x_ref.at[0], data.at[:, rows]),
                (x_ref.at[1, pl.ds(0, rest)], data.at[pl.ds(0, rest), rows + 1]),
            )
        )
    ]

    @pl.when(me > 0)
    def _():
        for copy in halo:
            copy.start()

    def multiply(start, size):
        for tile in range(tiles):
            low = tile * 2 * apart
            high = low + 3 * hop + reach + hop
            for turn in range(turns):
                one = max(turn * blocks, low // LANE)
                end = min((turn + 1) * blocks, -(-high // LANE))
                picks = range(one, end)
                left = jnp.concatenate(
                    [
                        data.at[block - turn * blocks, pl.ds(start, size)].reshape(2 * size, LANE)[...]
                        for block in picks
                    ],
                    axis=1,
                )
                right = jnp.concatenate(
                    [
                        bank[pl.ds(lead + one * LANE - (2 * tile + part) * apart, (end - one) * LANE), :]
                        for part in range(2)
                    ],
                    axis=1,
                )
                total[turn, pl.ds(2 * start, 2 * size), pl.ds(tile * wide, wide)] = jnp.dot(
                    left, right, preferred_element_type=jnp.float32
                )

    def turn_round(tile):
        row = tile * LANE
        for col in range(columns // LANE):
            whole = total[0, pl.ds(row, LANE), pl.ds(col * LANE, LANE)]
            for turn in range(1, turns):
                whole += total[turn, pl.ds(row + 2 * turn, LANE), pl.ds(col * LANE, LANE)]
            turned[tile, pl.ds(col * LANE, LANE), :] = jnp.transpose(whole)

    even = lax.broadcasted_iota(jnp.int32, (GROUP, LANE), 1) % 2 == 0

    def pack(out, first, tile_ids):
        for dest in range(count):
            for place in range(per):
                line = homes[dest][place]
                for tile in tile_ids:
                    cosine = turned[tile, pl.ds(line, GROUP, stride=SLOT), :]
                    sine_part = turned[tile, pl.ds(PART + line, GROUP, stride=SLOT), :]
                    swapped_part = jnp.where(
                        even, pltpu.roll(sine_part, LANE - 1, 1), -pltpu.roll(sine_part, 1, 1)
                    )
                    scaled = (cosine + swapped_part) * tapw_ref[:, pl.ds(tile * LANE, LANE)]
                    out[dest, pl.ds(place * GROUP, GROUP), pl.ds((tile - first) * LANE, LANE)] = (
                        scaled.astype(jnp.bfloat16)
                    )

    def exchange(which, source, target):
        copies = []
        for step in range(1, count):
            other = lax.rem(me + step, count)
            copy = pltpu.make_async_remote_copy(
                src_ref=source.at[other],
                dst_ref=target.at[me],
                send_sem=send_sems.at[which, step],
                recv_sem=recv_sems.at[which, step],
                device_id=where_is(other),
                device_id_type=pl.DeviceIdType.MESH,
            )
            copy.start()
            copies.append(copy)
        target[me] = source[me]
        return copies

    lane_tiles = turned.shape[0]
    near = 2 * cut // LANE
    for copy in loads[0]:
        copy.wait()
    multiply(0, cut)
    for tile in range(near):
        turn_round(tile)
    pack(send_a, 0, range(near))
    copies = exchange(0, send_a, recv_a)
    for copy in loads[1]:
        copy.wait()

    @pl.when(me > 0)
    def _():
        for copy in halo:
            copy.wait_send()

    @pl.when(me < count - 1)
    def _():
        for copy in halo:
            copy.wait_recv()

    multiply(cut, held - cut)
    for tile in range(near, lane_tiles):
        turn_round(tile)
    pack(send_b, near, range(near, lane_tiles))
    copies += exchange(1, send_b, recv_b)
    table_copy.wait()
    for copy in copies:
        copy.wait()

    lines = per * GROUP
    ring = -(-folded // LANE) + lane_tiles + 1
    sums = [None] * ring
    lane_ids = lax.broadcasted_iota(jnp.int32, (lines, LANE), 1)

    def put(tile, value):
        sums[tile] = value if sums[tile] is None else sums[tile] + value

    for source in range(count):
        offset = 2 * rows * source % folded
        base, shift = offset // LANE, offset % LANE
        for tile in range(lane_tiles):
            if tile < near:
                piece = recv_a[source, :, pl.ds(tile * LANE, LANE)]
            else:
                piece = recv_b[source, :, pl.ds((tile - near) * LANE, LANE)]
            piece = piece.astype(jnp.float32)
            if shift:
                piece = pltpu.roll(piece, shift, 1)
                put(base + tile, jnp.where(lane_ids >= shift, piece, 0.0))
                put(base + tile + 1, jnp.where(lane_ids < shift, piece, 0.0))
            else:
                put(base + tile, piece)
    base, shift = folded // LANE, folded % LANE
    for tile in range(base, ring):
        if sums[tile] is None:
            continue
        value = pltpu.roll(sums[tile], LANE - shift, 1) if shift else sums[tile]
        if shift and tile > base:
            put(tile - base - 1, jnp.where(lane_ids >= LANE - shift, value, 0.0))
        put(tile - base, jnp.where(lane_ids < LANE - shift, value, 0.0))
    used = -(-folded // LANE)
    weighted = jnp.concatenate(sums[:used], axis=1).astype(jnp.bfloat16)
    freq = table.shape[1] // 2
    partial_value = jnp.dot(weighted, table[...], preferred_element_type=jnp.float32)
    real, imag = partial_value[:, :freq], partial_value[:, freq:]
    cosine = jnp.concatenate([twist_ref[0]] * per, axis=0)
    sine_part = jnp.concatenate([twist_ref[1]] * per, axis=0)
    both = jnp.concatenate(
        [real * cosine + imag * sine_part, imag * cosine - real * sine_part], axis=0
    )
    spectrum = jnp.dot(
        eight_ref[...], both, preferred_element_type=jnp.float32, precision=lax.Precision.HIGHEST
    )
    pair[...] = spectrum.astype(jnp.bfloat16)
    high = 2 * GROUP

    def outward(source, target, index, device):
        return pltpu.make_async_remote_copy(
            src_ref=pair.at[pl.ds(source * high, high)],
            dst_ref=gathered.at[target],
            send_sem=out_sems.at[index],
            recv_sem=in_sems.at[target],
            device_id={"tm": device // zooms, "zoom": device % zooms},
            device_id_type=pl.DeviceIdType.MESH,
        )

    for device in range(count):
        sent = [
            (place, target, other)
            for place, line in enumerate(homes[device])
            for other in range(count)
            for target in range(slots + 2)
            if needs[other][target] == line and other != device
        ]
        kept = [
            (homes[device].index(line), target)
            for target, line in enumerate(needs[device])
            if line in homes[device]
        ]
        taken = [
            target
            for target, line in enumerate(needs[device])
            if line is not None and line not in homes[device]
        ]

        @pl.when(me == device)
        def _():
            copies = [
                outward(place, target, index, other)
                for index, (place, target, other) in enumerate(sent)
            ]
            for copy in copies:
                copy.start()
            for place, target in kept:
                gathered[target] = pair[pl.ds(place * high, high)]
            for copy in copies:
                copy.wait_send()
            for target in taken:
                outward(0, target, 0, (device + 1) % count).wait_recv()

    width = widths_ref[0] + zoom * (widths_ref[1] - widths_ref[0])
    for item in range(slots + 2):
        slot = tm * slots + item - 1
        real = ((slot >= 0) & (slot < width)).astype(jnp.int32)
        live_here = jnp.full((high, freq), real, jnp.int32) > 0
        value = jnp.where(live_here, gathered[item].astype(jnp.float32), 0.0)
        for tile in range(freq // LANE):
            flat[tile, pl.ds(item * high, high), :] = value[:, tile * LANE : (tile + 1) * LANE]
    stitch(flat, out_ref, width, tm * slots, slots, keep, edge, folded // 2)


def stitch(flat, out_ref, width, first, slots, keep, edge, freq):
    lines = 2 * GROUP
    pieces = [
        [flat[tile, pl.ds(turn, lines, stride=GROUP), :] for tile in range(flat.shape[0])]
        for turn in range(GROUP)
    ]
    span = jnp.concatenate([jnp.concatenate(row, axis=1)[:, :freq] for row in pieces], axis=1)
    full = GROUP * freq
    slot = lax.broadcasted_iota(jnp.int32, (lines, edge), 0) // 2 - 1 + first
    low_ok = jnp.where((slot >= 1) & (slot < width), 1.0, 0.0)
    high_ok = jnp.where(slot + 1 < width, 1.0, 0.0)
    place = lax.broadcasted_iota(jnp.int32, (lines, edge), 1).astype(jnp.float32)
    ramp = (place + 0.5) / (2.0 * edge)
    fall = (edge - place - 0.5) / (2.0 * edge)
    under = pltpu.roll(span[:, keep : keep + edge], 2, 0)
    over = pltpu.roll(span[:, full - edge :], lines - 2, 0)
    low_weight = fall * low_ok
    high_weight = ramp * high_ok
    head = span[:, :edge] * (1.0 - low_weight) + under * low_weight
    foot = span[:, keep - edge : keep] * (1.0 - high_weight) + over * high_weight
    kept = jnp.concatenate([head, span[:, edge : keep - edge], foot], axis=1)
    joined = jnp.concatenate([kept[2 * slot + 2 : 2 * slot + 4] for slot in range(slots)], axis=1)
    for part in range(2):
        out_ref[part] = joined[part : part + 1]


def beam(voltages, section1_taps, section2_taps, band_starts, band_widths):
    tap_count, chan_len = section1_taps.shape
    tms, zooms = lax.axis_size("tm"), lax.axis_size("zoom")
    count = tms * zooms
    row_len = GROUP * HOP
    rows = voltages.shape[2] // row_len
    blocks = row_len // LANE
    signal = voltages[0].reshape(2, rows, blocks, LANE).transpose(1, 2, 0, 3)
    fine_len = section2_taps.shape[1]
    freq_count = fine_len // GROUP
    freq = -(-freq_count // LANE) * LANE
    taps = jnp.pad(section1_taps, ((0, 4), (0, 0)))
    me = lax.axis_index("tm") * zooms + lax.axis_index("zoom")
    own = lax.dynamic_index_in_dim(section2_taps.reshape(count, rows, GROUP), me, keepdims=False)
    lane_tiles = -(-2 * rows // LANE)
    tapw = jnp.repeat(jnp.transpose(own), 2, axis=1)
    tapw = jnp.pad(tapw, ((0, 0), (0, lane_tiles * LANE - 2 * rows)))
    shift = KEEP // 2
    bins = np.arange(freq_count) - shift
    spot = np.arange(freq_count)
    angles = 2.0 * np.pi * ((spot[:, None] * bins[None, :]) % freq_count) / freq_count
    folded = 2 * freq_count
    table = np.zeros((-(-folded // (2 * LANE)) * LANE, 2, 2, freq))
    table[:freq_count, 0, 0, :freq_count] = np.cos(angles)
    table[:freq_count, 0, 1, :freq_count] = -np.sin(angles)
    table[:freq_count, 1, 0, :freq_count] = np.sin(angles)
    table[:freq_count, 1, 1, :freq_count] = np.cos(angles)
    table = table.reshape(-1, 2 * freq)[: -(-folded // LANE) * LANE]
    table = jnp.asarray(table.astype(np.float32).astype(jnp.bfloat16))
    phases = 2.0 * np.pi * ((np.arange(GROUP)[:, None] * bins[None, :]) % fine_len) / fine_len
    twist = np.zeros((2, GROUP, freq), np.float32)
    twist[0, :, :freq_count] = np.cos(phases)
    twist[1, :, :freq_count] = np.sin(phases)
    slots = CH_DEV
    per = LIVE_DEV
    live = per * count

    def owners(line):
        return [slot // slots for slot in (line, live - 1 - line) if slot < slots * tms]

    order = sorted(range(live), key=lambda line: (sum(owners(line)) / len(owners(line)), line))
    homes = [order[per * device : per * device + per] for device in range(count)]
    needs = []
    for device in range(count):
        needed = [device // zooms * slots + item - 1 for item in range(slots + 2)]
        needed = [slot if 0 <= slot < slots * tms else None for slot in needed]
        flip = device % zooms
        needs.append([live - 1 - slot if flip and slot is not None else slot for slot in needed])
    wheel = 2.0 * np.pi * ((np.arange(GROUP)[:, None] * np.arange(GROUP)[None, :]) % GROUP) / GROUP
    core = np.zeros((2, GROUP, 2, GROUP))
    core[0, :, 0] = np.cos(wheel)
    core[0, :, 1] = np.sin(wheel)
    core[1, :, 0] = -np.sin(wheel)
    core[1, :, 1] = np.cos(wheel)
    eight = np.zeros((per, 2, GROUP, 2, per, GROUP), np.float32)
    for place in range(per):
        eight[place, :, :, :, place] = core
    lines = per * GROUP
    eight = eight.reshape(2 * lines, 2 * lines)
    reach = tap_count * chan_len - HOP
    held = rows + 2
    columns = GROUP * SLOT
    cfg = (tms, zooms, HOP, chan_len, reach, slots, KEEP, EDGE, folded, homes, needs)
    near_lanes = held // LANE * LANE
    lead = (columns // LANE - 1) * 2 * HOP
    depth = lead + -(-(3 * HOP + tap_count * chan_len) // LANE) * LANE
    turns = -(-(row_len - HOP + tap_count * chan_len) // row_len)
    bf, f32 = jnp.bfloat16, jnp.float32
    any_space = pl.BlockSpec(memory_space=pl.ANY)
    vmem = pl.BlockSpec(memory_space=pltpu.VMEM)
    smem = pl.BlockSpec(memory_space=pltpu.SMEM)
    result = pl.pallas_call(
        functools.partial(beam_kernel, cfg),
        out_shape=jax.ShapeDtypeStruct((2, 1, slots * KEEP), f32),
        in_specs=[smem, smem, vmem, vmem, vmem, vmem, any_space, any_space],
        out_specs=vmem,
        scratch_shapes=[
            pltpu.VMEM((blocks, held, 2, LANE), bf),
            pltpu.VMEM((depth, LANE), bf),
            pltpu.VMEM((LANE, chan_len), f32),
            pltpu.VMEM((turns, lane_tiles * LANE + 16, columns), f32),
            pltpu.VMEM((lane_tiles, columns, LANE), f32),
            pltpu.VMEM((count, lines, near_lanes), bf),
            pltpu.VMEM((count, lines, lane_tiles * LANE - near_lanes), bf),
            pltpu.VMEM((count, lines, near_lanes), bf),
            pltpu.VMEM((count, lines, lane_tiles * LANE - near_lanes), bf),
            pltpu.VMEM(table.shape, bf),
            pltpu.VMEM((2 * lines, freq), bf),
            pltpu.VMEM((slots + 2, 2 * GROUP, freq), bf),
            pltpu.VMEM((freq // LANE, (slots + 3) * 2 * GROUP, LANE), f32),
            pltpu.SemaphoreType.DMA((2, blocks)),
            pltpu.SemaphoreType.DMA,
            pltpu.SemaphoreType.DMA((2, 2)),
            pltpu.SemaphoreType.DMA((2, count)),
            pltpu.SemaphoreType.DMA((2, count)),
            pltpu.SemaphoreType.DMA((4 * per,)),
            pltpu.SemaphoreType.DMA((slots + 2,)),
        ],
        compiler_params=pltpu.CompilerParams(
            collective_id=0, has_side_effects=True, vmem_limit_bytes=48 << 20
        ),
        name="beam",
    )(band_starts, band_widths, taps, tapw, twist, eight, signal, table)
    return result.reshape(1, 1, 2, 1, slots * KEEP)


def general(voltages, section1_taps, section2_taps, band_starts, band_widths):
    signal = voltages[0]
    tap_count, chan_len = section1_taps.shape
    spectra = signal.shape[1] // HOP
    rim_len = tap_count * chan_len - HOP
    tm_count = lax.axis_size("tm")
    zoom_count = lax.axis_size("zoom")
    device_count = tm_count * zoom_count
    slot_count = tm_count * CH_DEV
    width = CH_DEV + 2
    following = shifted(signal[:, :rim_len], ("tm", "zoom"), -1)
    span = slot_count + 2
    band_slots = jnp.arange(-1, slot_count + 1, dtype=jnp.int32)
    channels = ((band_starts[:, None] + band_slots[None, :]) % chan_len).reshape(-1)
    picks = [tm * CH_DEV + zoom * span for tm in range(tm_count) for zoom in range(zoom_count)]
    pieces = -(-chan_len // HOP)
    padded = jnp.concatenate(
        [signal, following, jnp.zeros((2, pieces * HOP), jnp.bfloat16)], axis=1
    )
    frames = weighted_frames(padded, section1_taps, spectra, HOP)
    coarse = jnp.einsum(
        "pqkn,qsn->pks", rotation_block(chan_len), frames, preferred_element_type=jnp.float32
    ).astype(jnp.bfloat16)
    wanted = np.arange(width)[:, None] + np.asarray(picks)[None, :]
    hot = channels[wanted.reshape(-1)][:, None] == jnp.arange(chan_len, dtype=jnp.int32)[None, :]
    packed = jnp.einsum(
        "lk,pks->pls", hot.astype(jnp.bfloat16), coarse, preferred_element_type=jnp.float32
    ).astype(jnp.bfloat16)
    packed = packed.reshape(2, width, device_count, spectra)
    received = lax.all_to_all(packed, ("tm", "zoom"), split_axis=2, concat_axis=2, tiled=True)
    series = received.reshape(2, width, -1)
    weighted, order = natural_order(series, section2_taps, FA, FB)
    spans = fine_spectra(weighted, order, KEEP, EDGE)
    slot_ids = lax.axis_index("tm") * CH_DEV + jnp.arange(CH_DEV, dtype=jnp.int32)
    band_ids = jnp.arange(band_widths.shape[0], dtype=jnp.int32)
    band_width = jnp.sum(jnp.where(band_ids == lax.axis_index("zoom"), band_widths, 0))
    upper_rim = spans[:, 2:, :, :EDGE]
    lower_rim = spans[:, :CH_DEV, :, KEEP + EDGE :]
    extended = spans[:, 1 : CH_DEV + 1]
    stitched = stitch_bands(extended, upper_rim, lower_rim, slot_ids, band_width, KEEP, EDGE)
    fine_count = stitched.shape[2]
    result = jnp.transpose(stitched, (0, 2, 1, 3)).reshape(2, fine_count, CH_DEV * KEEP)
    return result[None, None]


def on_device(voltages, section1_taps, section2_taps, band_starts, band_widths):
    chan_len = section1_taps.shape[1]
    tm_count, zoom_count = lax.axis_size("tm"), lax.axis_size("zoom")
    live = LIVE_DEV * tm_count * zoom_count
    row_len = GROUP * HOP
    fits = (
        zoom_count == 2
        and band_widths.shape[0] == 2
        and CH_DEV * tm_count <= live
        and live <= PART
        and chan_len & (chan_len - 1) == 0
        and voltages.shape[2] % row_len == 0
        and row_len % LANE == 0
        and voltages.shape[2] // row_len * tm_count * zoom_count * GROUP % section2_taps.shape[1] == 0
        and section1_taps.shape[0] * chan_len - HOP <= 2 * row_len
    )
    chosen = beam if fits else general
    return chosen(voltages, section1_taps, section2_taps, band_starts, band_widths)


def solution(mesh):
    placed = (P("pol", "groups", ("tm", "zoom")), P(), P(), P("groups"), P("groups"))
    return jax.shard_map(
        on_device,
        mesh=mesh,
        in_specs=placed,
        out_specs=P("pol", "zoom", "groups", None, "tm"),
        check_vma=False,
    )
```

```python
import functools
import math

import jax
import jax.numpy as jnp
import numpy as np
from jax import lax
from jax.experimental import pallas as pl
from jax.experimental.pallas import tpu as pltpu
from jax.sharding import PartitionSpec as P

HOP = 432
FA = 27
FB = 128
KEEP = 2916
EDGE = 128
CH_DEV = 5
LIVE_DEV = 3


def shifted(value, axis, steps):
    count = lax.axis_size(axis)
    initial, last = (max(0, -steps), min(count, count - steps))
    return lax.ppermute(value, axis, [(source, source + steps) for source in range(initial, last)])


def angle_table(rows, cols, length):
    product = (
        jnp.arange(rows, dtype=jnp.int32)[:, None]
        * jnp.arange(cols, dtype=jnp.int32)[None, :]
        % length
    )
    return product.astype(jnp.float32) * (2.0 * math.pi / length)


def rotation_block(length):
    angles = angle_table(length, length, length)
    cosine_tab = jnp.cos(angles).astype(jnp.bfloat16)
    sine_tab = jnp.sin(angles).astype(jnp.bfloat16)
    return jnp.stack([jnp.stack([cosine_tab, sine_tab]), jnp.stack([-sine_tab, cosine_tab])])


def frame_view(segment, spectra, chan_len, hop_len):
    pieces = -(-chan_len // hop_len)
    framed = segment[:, : (spectra + pieces - 1) * hop_len].reshape(
        segment.shape[0], spectra + pieces - 1, hop_len
    )
    joined = jnp.concatenate(
        [framed[:, offset : offset + spectra] for offset in range(pieces)], axis=2
    )
    return joined[:, :, :chan_len]


def weighted_frames(signal, taps, spectra, hop_len):
    chan_len = taps.shape[1]
    running = jnp.zeros((2, spectra, chan_len), jnp.float32)
    for tap_index in range(taps.shape[0]):
        frames = frame_view(signal[:, tap_index * chan_len :], spectra, chan_len, hop_len)
        running = running + taps[tap_index][None, None, :] * frames.astype(jnp.float32)
    return running.astype(jnp.bfloat16)


def natural_order(series, section2_taps, radix_a, radix_b):
    tap_count, fine_len = section2_taps.shape
    items = series.shape[1]
    row_count = series.shape[2] // fine_len
    spectra = row_count - tap_count + 1
    row_blocks = series.reshape(2, items, row_count, fine_len)
    running = jnp.zeros((2, items, spectra, fine_len), jnp.float32)
    for tap_index in range(tap_count):
        running = running + section2_taps[tap_index] * row_blocks[
            :, :, tap_index : tap_index + spectra
        ].astype(jnp.float32)
    weighted = running.astype(jnp.bfloat16).reshape(2, items, spectra, radix_a, radix_b)
    return weighted, np.arange(radix_b)


def ordered_angles(rows, order, length):
    product = (np.arange(rows)[:, None] * order[None, :] % length).astype(np.float32)
    return jnp.asarray(product) * (2.0 * math.pi / length)


def fine_spectra(weighted, order, keep_len, edge_len):
    _, items, spectra, radix_a, radix_b = weighted.shape
    fine_len = radix_a * radix_b
    partial_value = jnp.einsum(
        "pqkm,qcfmb->pcfkb", rotation_block(radix_a), weighted, preferred_element_type=jnp.float32
    )
    angles = ordered_angles(radix_a, order, fine_len)
    cosine_tab = jnp.cos(angles)
    sine_tab = jnp.sin(angles)
    real_part = partial_value[0] * cosine_tab + partial_value[1] * sine_tab
    imag_part = partial_value[1] * cosine_tab - partial_value[0] * sine_tab
    twiddled = jnp.concatenate([real_part, imag_part], axis=-1).astype(jnp.bfloat16)
    turned = ordered_angles(radix_b, order, radix_b).T
    cosine_b = jnp.cos(turned).astype(jnp.bfloat16)
    sine_b = jnp.sin(turned).astype(jnp.bfloat16)
    table = jnp.concatenate(
        [jnp.stack([cosine_b, -sine_b], axis=1), jnp.stack([sine_b, cosine_b], axis=1)], axis=0
    )
    spectrum = jnp.einsum(
        "cfkm,mpq->pcfqk", twiddled, table, preferred_element_type=jnp.float32
    ).reshape(2, items, spectra, fine_len)
    first = (-(keep_len // 2) - edge_len) % fine_len
    rest = keep_len + 2 * edge_len - (fine_len - first)
    return jnp.concatenate([spectrum[..., first:], spectrum[..., :rest]], axis=-1)


def stitch_bands(extended, upper_rim, lower_rim, slot_ids, band_width, keep_len, edge_len):
    centre = extended[..., edge_len : edge_len + keep_len]
    live = (slot_ids < band_width).astype(jnp.float32)[None, :, None, None]
    upper_ok = (slot_ids + 1 < band_width).astype(jnp.float32)[None, :, None, None]
    lower_ok = ((slot_ids >= 1) & (slot_ids < band_width)).astype(jnp.float32)[None, :, None, None]
    ramp = (jnp.arange(edge_len, dtype=jnp.float32) + 0.5) / (2.0 * edge_len)
    upper_weight = ramp * upper_ok
    lower_weight = ramp[::-1] * lower_ok
    low_part = centre[..., :edge_len] * (1.0 - lower_weight) + lower_rim * lower_weight
    high_part = centre[..., keep_len - edge_len :] * (1.0 - upper_weight) + upper_rim * upper_weight
    joined = jnp.concatenate(
        [low_part, centre[..., edge_len : keep_len - edge_len], high_part], axis=-1
    )
    return joined * live


GROUP = 8
LANE = 128
SLOT = 64
PART = 32
FAST = 4


def sine(x):
    square = x * x
    total = jnp.full_like(x, -1.0 / 39916800.0)
    for factor in (1.0 / 362880.0, -1.0 / 5040.0, 1.0 / 120.0, -1.0 / 6.0, 1.0):
        total = total * square + factor
    return total * x


def fill_bank(starts_ref, widths_ref, taps_ref, rot_len, hop, lead, live, bank, spread):
    lanes = lax.broadcasted_iota(jnp.int32, (LANE, LANE), 1)
    upper = lanes // SLOT
    quarter = (lanes % SLOT) // PART
    member = lanes % PART
    channel = jnp.where(
        member < widths_ref[0], starts_ref[0] + member, starts_ref[1] + (live - 1) - member
    )
    rows_of = lax.broadcasted_iota(jnp.int32, (LANE, LANE), 0)
    steps = -(-(taps_ref.shape[0] + 1) // GROUP) * GROUP
    filling = jnp.zeros((steps - taps_ref.shape[0], rot_len), jnp.float32)
    taps = jnp.concatenate([taps_ref[...], filling], axis=0)
    rolled = pltpu.roll(taps, hop, 1)
    down = pltpu.roll(rolled, 1, 0)
    behind = jnp.where(lax.broadcasted_iota(jnp.int32, rolled.shape, 1) < hop, down, rolled)
    spread[pl.ds(0, steps), :] = taps
    spread[pl.ds(steps, steps), :] = behind
    for block in range(rot_len // LANE):
        turned = jnp.transpose(spread[:, pl.ds(block * LANE, LANE)])
        place = rows_of + block * LANE - upper * hop
        turn = (place * channel - quarter * (rot_len // 4)) & (rot_len - 1)
        half = rot_len // 2
        angle = (jnp.abs(turn - half) - half // 2).astype(jnp.float32) * (2.0 * math.pi / rot_len)
        rot = sine(angle).astype(jnp.bfloat16).astype(jnp.float32)
        for tap in range(taps_ref.shape[0] + 1):
            taken = jnp.take_along_axis(turned, upper * steps + tap, axis=1)
            bank[pl.ds(lead + tap * rot_len + block * LANE, LANE), :] = (taken * rot).astype(jnp.bfloat16)


def fill_taps(taps_ref, me, count, length, ground, tapw):
    fine_len = taps_ref.shape[1]
    whole = ground.shape[1]
    for device in range(count):

        @pl.when(me == device)
        def _():
            place, stop, pieces = device * length, (device + 1) * length, []
            while place < stop:
                row, lane = divmod(place, fine_len)
                size = min(fine_len - lane, stop - place)
                pieces.append(taps_ref[pl.ds(row, 1), :][:, lane : lane + size])
                place += size
            pieces.append(jnp.zeros((1, whole - length), jnp.float32))
            ground[...] = jnp.broadcast_to(jnp.concatenate(pieces, axis=1), ground.shape)

    span = LANE * GROUP // 2
    lanes = lax.broadcasted_iota(jnp.int32, (GROUP, span), 1)
    chosen = lanes % GROUP == lax.broadcasted_iota(jnp.int32, (GROUP, span), 0)
    parts = []
    for tile in range(whole // span):
        value = jnp.where(chosen, ground[:, pl.ds(tile * span, span)], 0.0)
        for _ in range(3):
            head = value.astype(jnp.bfloat16)
            parts.append(head.astype(jnp.float32))
            value = value - head.astype(jnp.float32)
    source = lax.broadcasted_iota(jnp.int32, (span, LANE), 0) // GROUP
    target = lax.broadcasted_iota(jnp.int32, (span, LANE), 1) // 2
    moved = jnp.where(source == target, 1.0, 0.0).astype(jnp.bfloat16)
    placed = jnp.dot(
        jnp.concatenate(parts, axis=0).astype(jnp.bfloat16), moved, preferred_element_type=jnp.float32
    )
    for tile in range(whole // span):
        row = 3 * GROUP * tile
        tapw[:, pl.ds(tile * LANE, LANE)] = (
            placed[row : row + GROUP]
            + placed[row + GROUP : row + 2 * GROUP]
            + placed[row + 2 * GROUP : row + 3 * GROUP]
        )


def beam_kernel(
    cfg,
    starts_in,
    widths_in,
    taps_in,
    fine_taps_in,
    twist_in,
    eight_in,
    x_ref,
    table_ref,
    out_ref,
    starts_ref,
    widths_ref,
    taps_ref,
    fine_taps_ref,
    twist_ref,
    eight_ref,
    small_sems,
    data,
    bank,
    spread,
    tapw_ref,
    ground,
    native,
    total,
    turned,
    send_a,
    send_b,
    recv_a,
    recv_b,
    table,
    pair,
    gathered,
    flat,
    x_sems,
    table_sem,
    halo_sems,
    send_sems,
    recv_sems,
    out_sems,
    in_sems,
):
    tms, zooms, hop, rot_len, reach, slots, keep, edge, folded, homes, needs = cfg
    per = len(homes[0])
    live = per * len(homes)
    rows, blocks = x_ref.shape[0], x_ref.shape[1]
    row_len = blocks * LANE
    count = tms * zooms
    tm = lax.axis_index("tm")
    zoom = lax.axis_index("zoom")
    me = tm * zooms + zoom
    gathered[...] = jnp.zeros_like(gathered)
    barrier = pltpu.get_barrier_semaphore()

    def where_is(index):
        return {"tm": index // zooms, "zoom": lax.rem(index, zooms)}

    for step in range(1, count):
        pl.semaphore_signal(
            barrier,
            inc=1,
            device_id=where_is(lax.rem(me + step, count)),
            device_id_type=pl.DeviceIdType.MESH,
        )
    smalls = [
        pltpu.make_async_copy(source, target, small_sems.at[index])
        for index, (source, target) in enumerate(
            (
                (starts_in, starts_ref),
                (widths_in, widths_ref),
                (taps_in, taps_ref),
                (fine_taps_in, fine_taps_ref),
                (twist_in, twist_ref),
                (eight_in, eight_ref),
            )
        )
    ]
    for copy in smalls:
        copy.start()
    held = data.shape[1]
    cut = held // 2
    spans = ((0, cut), (cut, rows - cut))
    loads = []
    for which, (start, size) in enumerate(spans):
        loads.append([])
        for block in range(blocks):
            copy = pltpu.make_async_copy(
                x_ref.at[pl.ds(start, size), block],
                data.at[block, pl.ds(start, size)],
                x_sems.at[which, block],
            )
            copy.start()
            loads[which].append(copy)
    table_copy = pltpu.make_async_copy(table_ref, table, table_sem)
    table_copy.start()
    rest = -(-(reach - row_len) // LANE)
    data[pl.ds(rest, blocks - rest), pl.ds(rows + 1, 1)] = jnp.zeros(
        (blocks - rest, 1, 2, LANE), data.dtype
    )

    @pl.when(me == count - 1)
    def _():
        data[:, pl.ds(rows, 1)] = jnp.zeros((blocks, 1, 2, LANE), data.dtype)
        data[pl.ds(0, rest), pl.ds(rows + 1, 1)] = jnp.zeros((rest, 1, 2, LANE), data.dtype)

    columns = GROUP * SLOT
    wide = 2 * LANE
    tiles = columns // wide
    apart = 2 * hop
    lead = (columns // LANE - 1) * apart
    turns = total.shape[0]
    total[:, pl.ds(2 * held, total.shape[1] - 2 * held), :] = jnp.zeros(
        (turns, total.shape[1] - 2 * held, columns), jnp.float32
    )
    bank[pl.ds(0, lead), :] = jnp.zeros((lead, LANE), jnp.bfloat16)
    tail = lead + (taps_ref.shape[0] + 1) * rot_len
    bank[pl.ds(tail, bank.shape[0] - tail), :] = jnp.zeros((bank.shape[0] - tail, LANE), jnp.bfloat16)
    for copy in smalls:
        copy.wait()
    fill_bank(
        starts_ref, widths_ref, taps_ref, rot_len, hop, lead, live, bank, spread
    )
    fill_taps(fine_taps_ref, me, count, rows * GROUP, ground, tapw_ref)
    pl.semaphore_wait(barrier, count - 1)
    before = lax.rem(me + count - 1, count)
    halo = [
        pltpu.make_async_remote_copy(
            src_ref=source,
            dst_ref=target,
            send_sem=halo_sems.at[0, index],
            recv_sem=halo_sems.at[1, index],
            device_id=where_is(before),
            device_id_type=pl.DeviceIdType.MESH,
        )
        for index, (source, target) in enumerate(
            (
                (x_ref.at[0], data.at[:, rows]),
                (x_ref.at[1, pl.ds(0, rest)], data.at[pl.ds(0, rest), rows + 1]),
            )
        )
    ]

    @pl.when(me > 0)
    def _():
        for copy in halo:
            copy.start()

    def multiply(start, size):
        for block in range(blocks):
            native[block, pl.ds(2 * start, 2 * size), :] = data.at[block, pl.ds(start, size)].reshape(
                2 * size, LANE
            )[...]
        for tile in range(tiles):
            low = tile * 2 * apart
            high = low + 3 * hop + reach + hop
            for turn in range(turns):
                one = max(turn * blocks, low // LANE)
                end = min((turn + 1) * blocks, -(-high // LANE))
                picks = range(one, end)
                left = jnp.concatenate(
                    [
                        native[block - turn * blocks, pl.ds(2 * start, 2 * size), :]
                        for block in picks
                    ],
                    axis=1,
                )
                right = jnp.concatenate(
                    [
                        bank[pl.ds(lead + one * LANE - (2 * tile + part) * apart, (end - one) * LANE), :]
                        for part in range(2)
                    ],
                    axis=1,
                )
                total[turn, pl.ds(2 * start, 2 * size), pl.ds(tile * wide, wide)] = jnp.dot(
                    left, right, preferred_element_type=jnp.float32
                )

    def turn_round(tile):
        row = tile * LANE
        for col in range(columns // LANE):
            whole = total[0, pl.ds(row, LANE), pl.ds(col * LANE, LANE)]
            for turn in range(1, turns):
                whole += total[turn, pl.ds(row + 2 * turn, LANE), pl.ds(col * LANE, LANE)]
            turned[tile, pl.ds(col * LANE, LANE), :] = jnp.transpose(whole)

    even = lax.broadcasted_iota(jnp.int32, (GROUP, LANE), 1) % 2 == 0

    def line_of(tile, line):
        cosine = turned[tile, pl.ds(line, GROUP, stride=SLOT), :]
        sine_part = turned[tile, pl.ds(PART + line, GROUP, stride=SLOT), :]
        swapped_part = jnp.where(
            even, pltpu.roll(sine_part, LANE - 1, 1), -pltpu.roll(sine_part, 1, 1)
        )
        return (cosine + swapped_part) * tapw_ref[:, pl.ds(tile * LANE, LANE)]

    def pack(out, first, tile_ids, extra):
        for dest in range(count):
            for tile in tile_ids:
                values = [line_of(tile, line) for line in homes[dest]]
                if extra and tile == first:
                    value = line_of(lane_tiles - 1, homes[dest][0])
                    for place in range(1, per):
                        moved = line_of(lane_tiles - 1, homes[dest][place])
                        value += pltpu.roll(moved, place * last_width, 1)
                    values.append(value)
                elif extra:
                    values.append(jnp.zeros((GROUP, LANE), jnp.float32))
                value = jnp.concatenate(values, axis=0)
                out[dest, :, pl.ds((tile - first) * LANE, LANE)] = value.astype(jnp.bfloat16)

    def exchange(which, source, target):
        copies = []
        for step in range(1, count):
            other = lax.rem(me + step, count)
            copy = pltpu.make_async_remote_copy(
                src_ref=source.at[other],
                dst_ref=target.at[me],
                send_sem=send_sems.at[which, step],
                recv_sem=recv_sems.at[which, step],
                device_id=where_is(other),
                device_id_type=pl.DeviceIdType.MESH,
            )
            copy.start()
            copies.append(copy)
        target[me] = source[me]
        return copies

    lane_tiles = turned.shape[0]
    near = 2 * cut // LANE
    lines = per * GROUP
    last_width = LANE // (per + 1)
    for copy in loads[0]:
        copy.wait()
    multiply(0, cut)
    for tile in range(near):
        turn_round(tile)
    pack(send_a, 0, range(near), False)
    copies = exchange(0, send_a, recv_a)
    for copy in loads[1]:
        copy.wait()

    @pl.when(me > 0)
    def _():
        for copy in halo:
            copy.wait_send()

    @pl.when(me < count - 1)
    def _():
        for copy in halo:
            copy.wait_recv()

    multiply(cut, held - cut)
    for tile in range(near, lane_tiles):
        turn_round(tile)
    pack(send_b, near, range(near, lane_tiles - 1), True)
    copies += exchange(1, send_b, recv_b)
    table_copy.wait()
    for copy in copies:
        copy.wait()

    ring = -(-folded // LANE) + lane_tiles + 1
    sums = [None] * ring
    lane_ids = lax.broadcasted_iota(jnp.int32, (lines, LANE), 1)

    def put(tile, value):
        sums[tile] = value if sums[tile] is None else sums[tile] + value

    for source in range(count):
        offset = 2 * rows * source % folded
        base, shift = offset // LANE, offset % LANE
        for tile in range(lane_tiles):
            if tile < near:
                piece = recv_a[source, :, pl.ds(tile * LANE, LANE)].astype(jnp.float32)
            elif tile < lane_tiles - 1:
                piece = recv_b[source, :, pl.ds((tile - near) * LANE, LANE)]
                piece = piece.astype(jnp.float32)[:lines]
            else:
                piece = recv_b[source, :, pl.ds(0, LANE)].astype(jnp.float32)[lines:]
                piece = jnp.concatenate(
                    [piece] + [pltpu.roll(piece, LANE - place * last_width, 1) for place in range(1, per)],
                    axis=0,
                )
                piece = jnp.where(lane_ids < last_width, piece, 0.0)
            if shift:
                piece = pltpu.roll(piece, shift, 1)
                put(base + tile, jnp.where(lane_ids >= shift, piece, 0.0))
                put(base + tile + 1, jnp.where(lane_ids < shift, piece, 0.0))
            else:
                put(base + tile, piece)
    base, shift = folded // LANE, folded % LANE
    for tile in range(base, ring):
        if sums[tile] is None:
            continue
        value = pltpu.roll(sums[tile], LANE - shift, 1) if shift else sums[tile]
        if shift and tile > base:
            put(tile - base - 1, jnp.where(lane_ids >= LANE - shift, value, 0.0))
        put(tile - base, jnp.where(lane_ids < LANE - shift, value, 0.0))
    used = -(-folded // LANE)
    weighted = jnp.concatenate(sums[:used], axis=1).astype(jnp.bfloat16)
    freq = table.shape[1] // 2
    partial_value = jnp.dot(weighted, table[...], preferred_element_type=jnp.float32)
    real, imag = partial_value[:, :freq], partial_value[:, freq:]
    cosine = jnp.concatenate([twist_ref[0]] * per, axis=0)
    sine_part = jnp.concatenate([twist_ref[1]] * per, axis=0)
    both = jnp.concatenate(
        [real * cosine + imag * sine_part, imag * cosine - real * sine_part], axis=0
    )
    spectrum = jnp.dot(
        eight_ref[...], both, preferred_element_type=jnp.float32, precision=lax.Precision.HIGHEST
    )
    pair[...] = spectrum.astype(jnp.bfloat16)
    high = 2 * GROUP

    def outward(source, target, index, device):
        return pltpu.make_async_remote_copy(
            src_ref=pair.at[pl.ds(source * high, high)],
            dst_ref=gathered.at[target],
            send_sem=out_sems.at[index],
            recv_sem=in_sems.at[target],
            device_id={"tm": device // zooms, "zoom": device % zooms},
            device_id_type=pl.DeviceIdType.MESH,
        )

    for device in range(count):
        sent = [
            (place, target, other)
            for place, line in enumerate(homes[device])
            for other in range(count)
            for target in range(slots + 2)
            if needs[other][target] == line and other != device
        ]
        kept = [
            (homes[device].index(line), target)
            for target, line in enumerate(needs[device])
            if line in homes[device]
        ]
        taken = [
            target
            for target, line in enumerate(needs[device])
            if line is not None and line not in homes[device]
        ]

        @pl.when(me == device)
        def _():
            copies = [
                outward(place, target, index, other)
                for index, (place, target, other) in enumerate(sent)
            ]
            for copy in copies:
                copy.start()
            for place, target in kept:
                gathered[target] = pair[pl.ds(place * high, high)]
            for copy in copies:
                copy.wait_send()
            for target in taken:
                outward(0, target, 0, (device + 1) % count).wait_recv()

    width = widths_ref[0] + zoom * (widths_ref[1] - widths_ref[0])
    for item in range(slots + 2):
        slot = tm * slots + item - 1
        real = ((slot >= 0) & (slot < width)).astype(jnp.int32)
        live_here = jnp.full((high, freq), real, jnp.int32) > 0
        value = jnp.where(live_here, gathered[item].astype(jnp.float32), 0.0)
        for tile in range(freq // LANE):
            flat[tile, pl.ds(item * high, high), :] = value[:, tile * LANE : (tile + 1) * LANE]
    stitch(flat, out_ref, width, tm * slots, slots, keep, edge, folded // 2)


def stitch(flat, out_ref, width, first, slots, keep, edge, freq):
    lines = 2 * GROUP
    pieces = [
        [flat[tile, pl.ds(turn, lines, stride=GROUP), :] for tile in range(flat.shape[0])]
        for turn in range(GROUP)
    ]
    span = jnp.concatenate([jnp.concatenate(row, axis=1)[:, :freq] for row in pieces], axis=1)
    full = GROUP * freq
    slot = lax.broadcasted_iota(jnp.int32, (lines, edge), 0) // 2 - 1 + first
    low_ok = jnp.where((slot >= 1) & (slot < width), 1.0, 0.0)
    high_ok = jnp.where(slot + 1 < width, 1.0, 0.0)
    place = lax.broadcasted_iota(jnp.int32, (lines, edge), 1).astype(jnp.float32)
    ramp = (place + 0.5) / (2.0 * edge)
    fall = (edge - place - 0.5) / (2.0 * edge)
    under = pltpu.roll(span[:, keep : keep + edge], 2, 0)
    over = pltpu.roll(span[:, full - edge :], lines - 2, 0)
    low_weight = fall * low_ok
    high_weight = ramp * high_ok
    head = span[:, :edge] * (1.0 - low_weight) + under * low_weight
    foot = span[:, keep - edge : keep] * (1.0 - high_weight) + over * high_weight
    kept = jnp.concatenate([head, span[:, edge : keep - edge], foot], axis=1)
    joined = jnp.concatenate([kept[2 * slot + 2 : 2 * slot + 4] for slot in range(slots)], axis=1)
    for part in range(2):
        out_ref[part] = joined[part : part + 1]


def beam(voltages, section1_taps, section2_taps, band_starts, band_widths):
    tap_count, chan_len = section1_taps.shape
    tms, zooms = lax.axis_size("tm"), lax.axis_size("zoom")
    count = tms * zooms
    row_len = GROUP * HOP
    rows = voltages.shape[2] // row_len
    blocks = row_len // LANE
    signal = voltages[0].reshape(2, rows, blocks, LANE).transpose(1, 2, 0, 3)
    fine_len = section2_taps.shape[1]
    freq_count = fine_len // GROUP
    freq = -(-freq_count // LANE) * LANE
    lane_tiles = -(-2 * rows // LANE)
    shift = KEEP // 2
    bins = np.arange(freq_count) - shift
    spot = np.arange(freq_count)
    angles = 2.0 * np.pi * ((spot[:, None] * bins[None, :]) % freq_count) / freq_count
    folded = 2 * freq_count
    table = np.zeros((-(-folded // (2 * LANE)) * LANE, 2, 2, freq))
    table[:freq_count, 0, 0, :freq_count] = np.cos(angles)
    table[:freq_count, 0, 1, :freq_count] = -np.sin(angles)
    table[:freq_count, 1, 0, :freq_count] = np.sin(angles)
    table[:freq_count, 1, 1, :freq_count] = np.cos(angles)
    table = table.reshape(-1, 2 * freq)[: -(-folded // LANE) * LANE]
    table = jnp.asarray(table.astype(np.float32).astype(jnp.bfloat16))
    phases = 2.0 * np.pi * ((np.arange(GROUP)[:, None] * bins[None, :]) % fine_len) / fine_len
    twist = np.zeros((2, GROUP, freq), np.float32)
    twist[0, :, :freq_count] = np.cos(phases)
    twist[1, :, :freq_count] = np.sin(phases)
    slots = CH_DEV
    per = LIVE_DEV
    live = per * count

    def owners(line):
        return [slot // slots for slot in (line, live - 1 - line) if slot < slots * tms]

    order = sorted(range(live), key=lambda line: (sum(owners(line)) / len(owners(line)), line))
    homes = [order[per * device : per * device + per] for device in range(count)]
    needs = []
    for device in range(count):
        needed = [device // zooms * slots + item - 1 for item in range(slots + 2)]
        needed = [slot if 0 <= slot < slots * tms else None for slot in needed]
        flip = device % zooms
        needs.append([live - 1 - slot if flip and slot is not None else slot for slot in needed])
    wheel = 2.0 * np.pi * ((np.arange(GROUP)[:, None] * np.arange(GROUP)[None, :]) % GROUP) / GROUP
    core = np.zeros((2, GROUP, 2, GROUP))
    core[0, :, 0] = np.cos(wheel)
    core[0, :, 1] = np.sin(wheel)
    core[1, :, 0] = -np.sin(wheel)
    core[1, :, 1] = np.cos(wheel)
    eight = np.zeros((per, 2, GROUP, 2, per, GROUP), np.float32)
    for place in range(per):
        eight[place, :, :, :, place] = core
    lines = per * GROUP
    eight = eight.reshape(2 * lines, 2 * lines)
    reach = tap_count * chan_len - HOP
    held = rows + 2
    columns = GROUP * SLOT
    cfg = (tms, zooms, HOP, chan_len, reach, slots, KEEP, EDGE, folded, homes, needs)
    near_lanes = held // LANE * LANE
    lead = (columns // LANE - 1) * 2 * HOP
    depth = lead + -(-(3 * HOP + tap_count * chan_len) // LANE) * LANE
    turns = -(-(row_len - HOP + tap_count * chan_len) // row_len)
    bf, f32 = jnp.bfloat16, jnp.float32
    hbm = pl.BlockSpec(memory_space=pltpu.HBM)
    vmem = pl.BlockSpec(memory_space=pltpu.VMEM)
    result = pl.pallas_call(
        functools.partial(beam_kernel, cfg),
        out_shape=jax.ShapeDtypeStruct((2, 1, slots * KEEP), f32),
        in_specs=[hbm] * 8,
        out_specs=vmem,
        scratch_shapes=[
            pltpu.SMEM(band_starts.shape, jnp.int32),
            pltpu.SMEM(band_widths.shape, jnp.int32),
            pltpu.VMEM(section1_taps.shape, f32),
            pltpu.VMEM(section2_taps.shape, f32),
            pltpu.VMEM(twist.shape, f32),
            pltpu.VMEM(eight.shape, f32),
            pltpu.SemaphoreType.DMA((6,)),
            pltpu.VMEM((blocks, held, 2, LANE), bf),
            pltpu.VMEM((depth, LANE), bf),
            pltpu.VMEM((LANE, chan_len), f32),
            pltpu.VMEM((GROUP, lane_tiles * LANE), f32),
            pltpu.VMEM((GROUP, lane_tiles * LANE * GROUP // 2), f32),
            pltpu.VMEM((blocks, 2 * held, LANE), bf),
            pltpu.VMEM((turns, lane_tiles * LANE + 16, columns), f32),
            pltpu.VMEM((lane_tiles, columns, LANE), f32),
            pltpu.VMEM((count, lines, near_lanes), bf),
            pltpu.VMEM((count, lines + GROUP, (lane_tiles - 1) * LANE - near_lanes), bf),
            pltpu.VMEM((count, lines, near_lanes), bf),
            pltpu.VMEM((count, lines + GROUP, (lane_tiles - 1) * LANE - near_lanes), bf),
            pltpu.VMEM(table.shape, bf),
            pltpu.VMEM((2 * lines, freq), bf),
            pltpu.VMEM((slots + 2, 2 * GROUP, freq), bf),
            pltpu.VMEM((freq // LANE, (slots + 3) * 2 * GROUP, LANE), f32),
            pltpu.SemaphoreType.DMA((2, blocks)),
            pltpu.SemaphoreType.DMA,
            pltpu.SemaphoreType.DMA((2, 2)),
            pltpu.SemaphoreType.DMA((2, count)),
            pltpu.SemaphoreType.DMA((2, count)),
            pltpu.SemaphoreType.DMA((4 * per,)),
            pltpu.SemaphoreType.DMA((slots + 2,)),
        ],
        compiler_params=pltpu.CompilerParams(
            collective_id=0, has_side_effects=True, vmem_limit_bytes=64 << 20
        ),
        name="beam",
    )(band_starts, band_widths, section1_taps, section2_taps, twist, eight, signal, table)
    return result.reshape(1, 1, 2, 1, slots * KEEP)


def general(voltages, section1_taps, section2_taps, band_starts, band_widths):
    signal = voltages[0]
    tap_count, chan_len = section1_taps.shape
    spectra = signal.shape[1] // HOP
    rim_len = tap_count * chan_len - HOP
    tm_count = lax.axis_size("tm")
    zoom_count = lax.axis_size("zoom")
    device_count = tm_count * zoom_count
    slot_count = tm_count * CH_DEV
    width = CH_DEV + 2
    following = shifted(signal[:, :rim_len], ("tm", "zoom"), -1)
    span = slot_count + 2
    band_slots = jnp.arange(-1, slot_count + 1, dtype=jnp.int32)
    channels = ((band_starts[:, None] + band_slots[None, :]) % chan_len).reshape(-1)
    picks = [tm * CH_DEV + zoom * span for tm in range(tm_count) for zoom in range(zoom_count)]
    pieces = -(-chan_len // HOP)
    padded = jnp.concatenate(
        [signal, following, jnp.zeros((2, pieces * HOP), jnp.bfloat16)], axis=1
    )
    frames = weighted_frames(padded, section1_taps, spectra, HOP)
    coarse = jnp.einsum(
        "pqkn,qsn->pks", rotation_block(chan_len), frames, preferred_element_type=jnp.float32
    ).astype(jnp.bfloat16)
    wanted = np.arange(width)[:, None] + np.asarray(picks)[None, :]
    hot = channels[wanted.reshape(-1)][:, None] == jnp.arange(chan_len, dtype=jnp.int32)[None, :]
    packed = jnp.einsum(
        "lk,pks->pls", hot.astype(jnp.bfloat16), coarse, preferred_element_type=jnp.float32
    ).astype(jnp.bfloat16)
    packed = packed.reshape(2, width, device_count, spectra)
    received = lax.all_to_all(packed, ("tm", "zoom"), split_axis=2, concat_axis=2, tiled=True)
    series = received.reshape(2, width, -1)
    weighted, order = natural_order(series, section2_taps, FA, FB)
    spans = fine_spectra(weighted, order, KEEP, EDGE)
    slot_ids = lax.axis_index("tm") * CH_DEV + jnp.arange(CH_DEV, dtype=jnp.int32)
    band_ids = jnp.arange(band_widths.shape[0], dtype=jnp.int32)
    band_width = jnp.sum(jnp.where(band_ids == lax.axis_index("zoom"), band_widths, 0))
    upper_rim = spans[:, 2:, :, :EDGE]
    lower_rim = spans[:, :CH_DEV, :, KEEP + EDGE :]
    extended = spans[:, 1 : CH_DEV + 1]
    stitched = stitch_bands(extended, upper_rim, lower_rim, slot_ids, band_width, KEEP, EDGE)
    fine_count = stitched.shape[2]
    result = jnp.transpose(stitched, (0, 2, 1, 3)).reshape(2, fine_count, CH_DEV * KEEP)
    return result[None, None]


def on_device(voltages, section1_taps, section2_taps, band_starts, band_widths):
    chan_len = section1_taps.shape[1]
    tm_count, zoom_count = lax.axis_size("tm"), lax.axis_size("zoom")
    live = LIVE_DEV * tm_count * zoom_count
    row_len = GROUP * HOP
    fits = (
        zoom_count == 2
        and band_widths.shape[0] == 2
        and CH_DEV * tm_count <= live
        and live <= PART
        and chan_len & (chan_len - 1) == 0
        and voltages.shape[2] % row_len == 0
        and row_len % LANE == 0
        and voltages.shape[2] // row_len * tm_count * zoom_count * GROUP % section2_taps.shape[1] == 0
        and section1_taps.shape[0] * chan_len - HOP <= 2 * row_len
        and 2 * (voltages.shape[2] // row_len) % LANE <= LANE // (LIVE_DEV + 1)
        and voltages.shape[2] // row_len > LANE
    )
    chosen = beam if fits else general
    return chosen(voltages, section1_taps, section2_taps, band_starts, band_widths)


def solution(mesh):
    placed = (P("pol", "groups", ("tm", "zoom")), P(), P(), P("groups"), P("groups"))
    return jax.shard_map(
        on_device,
        mesh=mesh,
        in_specs=placed,
        out_specs=P("pol", "zoom", "groups", None, "tm"),
        check_vma=False,
    )
```

```python
import functools
import math

import jax
import jax.numpy as jnp
import numpy as np
from jax import lax
from jax.experimental import pallas as pl
from jax.experimental.pallas import tpu as pltpu
from jax.sharding import PartitionSpec as P

HOP = 432
FA = 27
FB = 128
KEEP = 2916
EDGE = 128
CH_DEV = 5
LIVE_DEV = 3


def shifted(value, axis, steps):
    count = lax.axis_size(axis)
    initial, last = (max(0, -steps), min(count, count - steps))
    return lax.ppermute(value, axis, [(source, source + steps) for source in range(initial, last)])


def angle_table(rows, cols, length):
    product = (
        jnp.arange(rows, dtype=jnp.int32)[:, None]
        * jnp.arange(cols, dtype=jnp.int32)[None, :]
        % length
    )
    return product.astype(jnp.float32) * (2.0 * math.pi / length)


def rotation_block(length):
    angles = angle_table(length, length, length)
    cosine_tab = jnp.cos(angles).astype(jnp.bfloat16)
    sine_tab = jnp.sin(angles).astype(jnp.bfloat16)
    return jnp.stack([jnp.stack([cosine_tab, sine_tab]), jnp.stack([-sine_tab, cosine_tab])])


def frame_view(segment, spectra, chan_len, hop_len):
    pieces = -(-chan_len // hop_len)
    framed = segment[:, : (spectra + pieces - 1) * hop_len].reshape(
        segment.shape[0], spectra + pieces - 1, hop_len
    )
    joined = jnp.concatenate(
        [framed[:, offset : offset + spectra] for offset in range(pieces)], axis=2
    )
    return joined[:, :, :chan_len]


def weighted_frames(signal, taps, spectra, hop_len):
    chan_len = taps.shape[1]
    running = jnp.zeros((2, spectra, chan_len), jnp.float32)
    for tap_index in range(taps.shape[0]):
        frames = frame_view(signal[:, tap_index * chan_len :], spectra, chan_len, hop_len)
        running = running + taps[tap_index][None, None, :] * frames.astype(jnp.float32)
    return running.astype(jnp.bfloat16)


def natural_order(series, section2_taps, radix_a, radix_b):
    tap_count, fine_len = section2_taps.shape
    items = series.shape[1]
    row_count = series.shape[2] // fine_len
    spectra = row_count - tap_count + 1
    row_blocks = series.reshape(2, items, row_count, fine_len)
    running = jnp.zeros((2, items, spectra, fine_len), jnp.float32)
    for tap_index in range(tap_count):
        running = running + section2_taps[tap_index] * row_blocks[
            :, :, tap_index : tap_index + spectra
        ].astype(jnp.float32)
    weighted = running.astype(jnp.bfloat16).reshape(2, items, spectra, radix_a, radix_b)
    return weighted, np.arange(radix_b)


def ordered_angles(rows, order, length):
    product = (np.arange(rows)[:, None] * order[None, :] % length).astype(np.float32)
    return jnp.asarray(product) * (2.0 * math.pi / length)


def fine_spectra(weighted, order, keep_len, edge_len):
    _, items, spectra, radix_a, radix_b = weighted.shape
    fine_len = radix_a * radix_b
    partial_value = jnp.einsum(
        "pqkm,qcfmb->pcfkb", rotation_block(radix_a), weighted, preferred_element_type=jnp.float32
    )
    angles = ordered_angles(radix_a, order, fine_len)
    cosine_tab = jnp.cos(angles)
    sine_tab = jnp.sin(angles)
    real_part = partial_value[0] * cosine_tab + partial_value[1] * sine_tab
    imag_part = partial_value[1] * cosine_tab - partial_value[0] * sine_tab
    twiddled = jnp.concatenate([real_part, imag_part], axis=-1).astype(jnp.bfloat16)
    turned = ordered_angles(radix_b, order, radix_b).T
    cosine_b = jnp.cos(turned).astype(jnp.bfloat16)
    sine_b = jnp.sin(turned).astype(jnp.bfloat16)
    table = jnp.concatenate(
        [jnp.stack([cosine_b, -sine_b], axis=1), jnp.stack([sine_b, cosine_b], axis=1)], axis=0
    )
    spectrum = jnp.einsum(
        "cfkm,mpq->pcfqk", twiddled, table, preferred_element_type=jnp.float32
    ).reshape(2, items, spectra, fine_len)
    first = (-(keep_len // 2) - edge_len) % fine_len
    rest = keep_len + 2 * edge_len - (fine_len - first)
    return jnp.concatenate([spectrum[..., first:], spectrum[..., :rest]], axis=-1)


def stitch_bands(extended, upper_rim, lower_rim, slot_ids, band_width, keep_len, edge_len):
    centre = extended[..., edge_len : edge_len + keep_len]
    live = (slot_ids < band_width).astype(jnp.float32)[None, :, None, None]
    upper_ok = (slot_ids + 1 < band_width).astype(jnp.float32)[None, :, None, None]
    lower_ok = ((slot_ids >= 1) & (slot_ids < band_width)).astype(jnp.float32)[None, :, None, None]
    ramp = (jnp.arange(edge_len, dtype=jnp.float32) + 0.5) / (2.0 * edge_len)
    upper_weight = ramp * upper_ok
    lower_weight = ramp[::-1] * lower_ok
    low_part = centre[..., :edge_len] * (1.0 - lower_weight) + lower_rim * lower_weight
    high_part = centre[..., keep_len - edge_len :] * (1.0 - upper_weight) + upper_rim * upper_weight
    joined = jnp.concatenate(
        [low_part, centre[..., edge_len : keep_len - edge_len], high_part], axis=-1
    )
    return joined * live


GROUP = 8
LANE = 128
SLOT = 64
PART = 32


def sine(x):
    square = x * x
    total = jnp.full_like(x, -1.0 / 39916800.0)
    for factor in (1.0 / 362880.0, -1.0 / 5040.0, 1.0 / 120.0, -1.0 / 6.0, 1.0):
        total = total * square + factor
    return total * x


def fill_bank(starts_ref, widths_ref, taps_ref, rot_len, hop, lead, live, bank, spread):
    lanes = lax.broadcasted_iota(jnp.int32, (LANE, LANE), 1)
    upper = lanes // SLOT
    quarter = (lanes % SLOT) // PART
    member = lanes % PART
    channel = jnp.where(
        member < widths_ref[0], starts_ref[0] + member, starts_ref[1] + (live - 1) - member
    )
    rows_of = lax.broadcasted_iota(jnp.int32, (LANE, LANE), 0)
    steps = -(-(taps_ref.shape[0] + 1) // GROUP) * GROUP
    filling = jnp.zeros((steps - taps_ref.shape[0], rot_len), jnp.float32)
    taps = jnp.concatenate([taps_ref[...], filling], axis=0)
    rolled = pltpu.roll(taps, hop, 1)
    down = pltpu.roll(rolled, 1, 0)
    behind = jnp.where(lax.broadcasted_iota(jnp.int32, rolled.shape, 1) < hop, down, rolled)
    spread[pl.ds(0, steps), :] = taps
    spread[pl.ds(steps, steps), :] = behind
    for block in range(rot_len // LANE):
        turned = jnp.transpose(spread[:, pl.ds(block * LANE, LANE)])
        place = rows_of + block * LANE - upper * hop
        turn = (place * channel - quarter * (rot_len // 4)) & (rot_len - 1)
        half = rot_len // 2
        angle = (jnp.abs(turn - half) - half // 2).astype(jnp.float32) * (2.0 * math.pi / rot_len)
        rot = sine(angle).astype(jnp.bfloat16).astype(jnp.float32)
        for tap in range(taps_ref.shape[0] + 1):
            taken = jnp.take_along_axis(turned, upper * steps + tap, axis=1)
            bank[pl.ds(lead + tap * rot_len + block * LANE, LANE), :] = (taken * rot).astype(jnp.bfloat16)


def fill_taps(taps_ref, me, count, length, ground, tapw):
    fine_len = taps_ref.shape[1]
    whole = ground.shape[1]
    for device in range(count):

        @pl.when(me == device)
        def _():
            place, stop, pieces = device * length, (device + 1) * length, []
            while place < stop:
                row, lane = divmod(place, fine_len)
                size = min(fine_len - lane, stop - place)
                pieces.append(taps_ref[pl.ds(row, 1), :][:, lane : lane + size])
                place += size
            pieces.append(jnp.zeros((1, whole - length), jnp.float32))
            ground[...] = jnp.broadcast_to(jnp.concatenate(pieces, axis=1), ground.shape)

    span = LANE * GROUP // 2
    lanes = lax.broadcasted_iota(jnp.int32, (GROUP, span), 1)
    chosen = lanes % GROUP == lax.broadcasted_iota(jnp.int32, (GROUP, span), 0)
    parts = []
    for tile in range(whole // span):
        value = jnp.where(chosen, ground[:, pl.ds(tile * span, span)], 0.0)
        for _ in range(3):
            head = value.astype(jnp.bfloat16)
            parts.append(head.astype(jnp.float32))
            value = value - head.astype(jnp.float32)
    source = lax.broadcasted_iota(jnp.int32, (span, LANE), 0) // GROUP
    target = lax.broadcasted_iota(jnp.int32, (span, LANE), 1) // 2
    moved = jnp.where(source == target, 1.0, 0.0).astype(jnp.bfloat16)
    placed = jnp.dot(
        jnp.concatenate(parts, axis=0).astype(jnp.bfloat16), moved, preferred_element_type=jnp.float32
    )
    for tile in range(whole // span):
        row = 3 * GROUP * tile
        tapw[:, pl.ds(tile * LANE, LANE)] = (
            placed[row : row + GROUP]
            + placed[row + GROUP : row + 2 * GROUP]
            + placed[row + 2 * GROUP : row + 3 * GROUP]
        )


def beam_kernel(
    cfg,
    starts_in,
    widths_in,
    taps_in,
    fine_taps_in,
    twist_in,
    eight_in,
    x_ref,
    table_ref,
    out_ref,
    starts_ref,
    widths_ref,
    taps_ref,
    fine_taps_ref,
    twist_ref,
    eight_ref,
    small_sems,
    data,
    bank,
    spread,
    tapw_ref,
    ground,
    native,
    total,
    turned,
    sends,
    recvs,
    table,
    pair,
    gathered,
    flat,
    x_sems,
    table_sem,
    halo_sems,
    send_sems,
    recv_sems,
    out_sems,
    in_sems,
):
    tms, zooms, hop, rot_len, reach, slots, keep, edge, folded, homes, needs, groups = cfg
    per = len(homes[0])
    live = per * len(homes)
    rows, blocks = x_ref.shape[0], x_ref.shape[1]
    row_len = blocks * LANE
    count = tms * zooms
    tm = lax.axis_index("tm")
    zoom = lax.axis_index("zoom")
    me = tm * zooms + zoom
    gathered[...] = jnp.zeros_like(gathered)
    barrier = pltpu.get_barrier_semaphore()

    def where_is(index):
        return {"tm": index // zooms, "zoom": lax.rem(index, zooms)}

    for step in range(1, count):
        pl.semaphore_signal(
            barrier,
            inc=1,
            device_id=where_is(lax.rem(me + step, count)),
            device_id_type=pl.DeviceIdType.MESH,
        )
    smalls = [
        pltpu.make_async_copy(source, target, small_sems.at[index])
        for index, (source, target) in enumerate(
            (
                (starts_in, starts_ref),
                (widths_in, widths_ref),
                (taps_in, taps_ref),
                (fine_taps_in, fine_taps_ref),
                (twist_in, twist_ref),
                (eight_in, eight_ref),
            )
        )
    ]
    for copy in smalls:
        copy.start()
    held = data.shape[1]
    cuts = [0] + [(group[-1] * LANE + LANE + 16) // 2 for group in groups[:-1]] + [held]
    spans = [(low, min(high, rows) - low) for low, high in zip(cuts[:-1], cuts[1:])]
    loads = []
    for which, (start, size) in enumerate(spans):
        loads.append([])
        for block in range(blocks):
            copy = pltpu.make_async_copy(
                x_ref.at[pl.ds(start, size), block],
                data.at[block, pl.ds(start, size)],
                x_sems.at[which, block],
            )
            loads[which].append(copy)
    for copy in loads[0]:
        copy.start()
    table_copy = pltpu.make_async_copy(table_ref, table, table_sem)
    table_copy.start()
    rest = -(-(reach - row_len) // LANE)
    data[pl.ds(rest, blocks - rest), pl.ds(rows + 1, 1)] = jnp.zeros(
        (blocks - rest, 1, 2, LANE), data.dtype
    )

    @pl.when(me == count - 1)
    def _():
        data[:, pl.ds(rows, 1)] = jnp.zeros((blocks, 1, 2, LANE), data.dtype)
        data[pl.ds(0, rest), pl.ds(rows + 1, 1)] = jnp.zeros((rest, 1, 2, LANE), data.dtype)

    columns = GROUP * SLOT
    wide = 2 * LANE
    tiles = columns // wide
    apart = 2 * hop
    lead = (columns // LANE - 1) * apart
    turns = total.shape[0]
    total[:, pl.ds(2 * held, total.shape[1] - 2 * held), :] = jnp.zeros(
        (turns, total.shape[1] - 2 * held, columns), jnp.float32
    )
    bank[pl.ds(0, lead), :] = jnp.zeros((lead, LANE), jnp.bfloat16)
    tail = lead + (taps_ref.shape[0] + 1) * rot_len
    bank[pl.ds(tail, bank.shape[0] - tail), :] = jnp.zeros((bank.shape[0] - tail, LANE), jnp.bfloat16)
    for copy in smalls:
        copy.wait()
    fill_bank(
        starts_ref, widths_ref, taps_ref, rot_len, hop, lead, live, bank, spread
    )
    fill_taps(fine_taps_ref, me, count, rows * GROUP, ground, tapw_ref)
    pl.semaphore_wait(barrier, count - 1)
    before = lax.rem(me + count - 1, count)
    halo = [
        pltpu.make_async_remote_copy(
            src_ref=source,
            dst_ref=target,
            send_sem=halo_sems.at[0, index],
            recv_sem=halo_sems.at[1, index],
            device_id=where_is(before),
            device_id_type=pl.DeviceIdType.MESH,
        )
        for index, (source, target) in enumerate(
            (
                (x_ref.at[0], data.at[:, rows]),
                (x_ref.at[1, pl.ds(0, rest)], data.at[pl.ds(0, rest), rows + 1]),
            )
        )
    ]

    @pl.when(me > 0)
    def _():
        for copy in halo:
            copy.start()

    def multiply(start, size):
        for block in range(blocks):
            native[block, pl.ds(2 * start, 2 * size), :] = data.at[block, pl.ds(start, size)].reshape(
                2 * size, LANE
            )[...]
        for tile in range(tiles):
            low = tile * 2 * apart
            high = low + 3 * hop + reach + hop
            for turn in range(turns):
                one = max(turn * blocks, low // LANE)
                end = min((turn + 1) * blocks, -(-high // LANE))
                picks = range(one, end)
                left = jnp.concatenate(
                    [
                        native[block - turn * blocks, pl.ds(2 * start, 2 * size), :]
                        for block in picks
                    ],
                    axis=1,
                )
                right = jnp.concatenate(
                    [
                        bank[pl.ds(lead + one * LANE - (2 * tile + part) * apart, (end - one) * LANE), :]
                        for part in range(2)
                    ],
                    axis=1,
                )
                total[turn, pl.ds(2 * start, 2 * size), pl.ds(tile * wide, wide)] = jnp.dot(
                    left, right, preferred_element_type=jnp.float32
                )

    def turn_round(tile):
        row = tile * LANE
        for col in range(columns // LANE):
            whole = total[0, pl.ds(row, LANE), pl.ds(col * LANE, LANE)]
            for turn in range(1, turns):
                whole += total[turn, pl.ds(row + 2 * turn, LANE), pl.ds(col * LANE, LANE)]
            turned[tile, pl.ds(col * LANE, LANE), :] = jnp.transpose(whole)

    even = lax.broadcasted_iota(jnp.int32, (GROUP, LANE), 1) % 2 == 0

    def line_of(tile, line):
        cosine = turned[tile, pl.ds(line, GROUP, stride=SLOT), :]
        sine_part = turned[tile, pl.ds(PART + line, GROUP, stride=SLOT), :]
        swapped_part = jnp.where(
            even, pltpu.roll(sine_part, LANE - 1, 1), -pltpu.roll(sine_part, 1, 1)
        )
        return (cosine + swapped_part) * tapw_ref[:, pl.ds(tile * LANE, LANE)]

    def pack(out, first, tile_ids, extra):
        for dest in range(count):
            for tile in tile_ids:
                values = [line_of(tile, line) for line in homes[dest]]
                if extra and tile == first:
                    value = line_of(lane_tiles - 1, homes[dest][0])
                    for place in range(1, per):
                        moved = line_of(lane_tiles - 1, homes[dest][place])
                        value += pltpu.roll(moved, place * last_width, 1)
                    values.append(value)
                elif extra:
                    values.append(jnp.zeros((GROUP, LANE), jnp.float32))
                value = jnp.concatenate(values, axis=0)
                out[dest, :, pl.ds((tile - first) * LANE, LANE)] = value.astype(jnp.bfloat16)

    def exchange(which, source, target):
        copies = []
        for step in range(1, count):
            other = lax.rem(me + step, count)
            copy = pltpu.make_async_remote_copy(
                src_ref=source.at[other],
                dst_ref=target.at[me],
                send_sem=send_sems.at[which, step],
                recv_sem=recv_sems.at[which, step],
                device_id=where_is(other),
                device_id_type=pl.DeviceIdType.MESH,
            )
            copy.start()
            copies.append(copy)
        target[me] = source[me]
        return copies

    lane_tiles = turned.shape[0]
    lines = per * GROUP
    last_width = LANE // (per + 1)
    copies = []
    for index, group in enumerate(groups):
        ending = index == len(groups) - 1
        for copy in loads[index]:
            copy.wait()
        if not ending:
            for copy in loads[index + 1]:
                copy.start()
        else:

            @pl.when(me > 0)
            def _():
                for copy in halo:
                    copy.wait_send()

            @pl.when(me < count - 1)
            def _():
                for copy in halo:
                    copy.wait_recv()

        multiply(cuts[index], cuts[index + 1] - cuts[index])
        for tile in group + [lane_tiles - 1] * ending:
            turn_round(tile)
        pack(sends[index], group[0], group, ending)
        copies += exchange(index, sends[index], recvs[index])
    table_copy.wait()
    for copy in copies:
        copy.wait()

    ring = -(-folded // LANE) + lane_tiles + 1
    sums = [None] * ring
    lane_ids = lax.broadcasted_iota(jnp.int32, (lines, LANE), 1)

    def put(tile, value):
        sums[tile] = value if sums[tile] is None else sums[tile] + value

    for source in range(count):
        offset = 2 * rows * source % folded
        base, shift = offset // LANE, offset % LANE
        for tile in range(lane_tiles):
            if tile < lane_tiles - 1:
                index = [tile in group for group in groups].index(True)
                piece = recvs[index][source, :, pl.ds((tile - groups[index][0]) * LANE, LANE)]
                piece = piece.astype(jnp.float32)[:lines]
            else:
                piece = recvs[-1][source, :, pl.ds(0, LANE)].astype(jnp.float32)[lines:]
                piece = jnp.concatenate(
                    [piece] + [pltpu.roll(piece, LANE - place * last_width, 1) for place in range(1, per)],
                    axis=0,
                )
                piece = jnp.where(lane_ids < last_width, piece, 0.0)
            if shift:
                piece = pltpu.roll(piece, shift, 1)
                put(base + tile, jnp.where(lane_ids >= shift, piece, 0.0))
                put(base + tile + 1, jnp.where(lane_ids < shift, piece, 0.0))
            else:
                put(base + tile, piece)
    base, shift = folded // LANE, folded % LANE
    for tile in range(base, ring):
        if sums[tile] is None:
            continue
        value = pltpu.roll(sums[tile], LANE - shift, 1) if shift else sums[tile]
        if shift and tile > base:
            put(tile - base - 1, jnp.where(lane_ids >= LANE - shift, value, 0.0))
        put(tile - base, jnp.where(lane_ids < LANE - shift, value, 0.0))
    used = -(-folded // LANE)
    weighted = jnp.concatenate(sums[:used], axis=1).astype(jnp.bfloat16)
    freq = table.shape[1] // 2
    partial_value = jnp.dot(weighted, table[...], preferred_element_type=jnp.float32)
    real, imag = partial_value[:, :freq], partial_value[:, freq:]
    cosine = jnp.concatenate([twist_ref[0]] * per, axis=0)
    sine_part = jnp.concatenate([twist_ref[1]] * per, axis=0)
    both = jnp.concatenate(
        [real * cosine + imag * sine_part, imag * cosine - real * sine_part], axis=0
    )
    spectrum = jnp.dot(
        eight_ref[...], both, preferred_element_type=jnp.float32, precision=lax.Precision.HIGHEST
    )
    pair[...] = spectrum.astype(jnp.bfloat16)
    high = 2 * GROUP

    sizes = [2 * LANE] + [freq] * slots + [LANE]

    def outward(source, target, index, device):
        return pltpu.make_async_remote_copy(
            src_ref=pair.at[pl.ds(source * high, high), pl.ds(0, sizes[target])],
            dst_ref=gathered.at[target, :, pl.ds(0, sizes[target])],
            send_sem=out_sems.at[index],
            recv_sem=in_sems.at[target],
            device_id={"tm": device // zooms, "zoom": device % zooms},
            device_id_type=pl.DeviceIdType.MESH,
        )

    for device in range(count):
        sent = [
            (place, target, other)
            for place, line in enumerate(homes[device])
            for other in range(count)
            for target in range(slots + 2)
            if needs[other][target] == line and other != device
        ]
        kept = [
            (homes[device].index(line), target)
            for target, line in enumerate(needs[device])
            if line in homes[device]
        ]
        taken = [
            target
            for target, line in enumerate(needs[device])
            if line is not None and line not in homes[device]
        ]

        @pl.when(me == device)
        def _():
            copies = [
                outward(place, target, index, other)
                for index, (place, target, other) in enumerate(sent)
            ]
            for copy in copies:
                copy.start()
            for place, target in kept:
                gathered[target] = pair[pl.ds(place * high, high)]
            for copy in copies:
                copy.wait_send()
            for target in taken:
                outward(0, target, 0, (device + 1) % count).wait_recv()

    width = widths_ref[0] + zoom * (widths_ref[1] - widths_ref[0])
    for item in range(slots + 2):
        slot = tm * slots + item - 1
        real = ((slot >= 0) & (slot < width)).astype(jnp.int32)
        live_here = jnp.full((high, freq), real, jnp.int32) > 0
        value = jnp.where(live_here, gathered[item].astype(jnp.float32), 0.0)
        for tile in range(freq // LANE):
            flat[tile, pl.ds(item * high, high), :] = value[:, tile * LANE : (tile + 1) * LANE]
    stitch(flat, out_ref, width, tm * slots, slots, keep, edge, folded // 2)


def stitch(flat, out_ref, width, first, slots, keep, edge, freq):
    lines = 2 * GROUP
    pieces = [
        [flat[tile, pl.ds(turn, lines, stride=GROUP), :] for tile in range(flat.shape[0])]
        for turn in range(GROUP)
    ]
    span = jnp.concatenate([jnp.concatenate(row, axis=1)[:, :freq] for row in pieces], axis=1)
    slot = lax.broadcasted_iota(jnp.int32, (lines, edge), 0) // 2 - 1 + first
    low_ok = jnp.where((slot >= 1) & (slot < width), 1.0, 0.0)
    high_ok = jnp.where(slot + 1 < width, 1.0, 0.0)
    place = lax.broadcasted_iota(jnp.int32, (lines, edge), 1).astype(jnp.float32)
    ramp = (place + 0.5) / (2.0 * edge)
    fall = (edge - place - 0.5) / (2.0 * edge)
    under = pltpu.roll(span[:, keep + edge : keep + 2 * edge], 2, 0)
    over = pltpu.roll(span[:, :edge], lines - 2, 0)
    low_weight = fall * low_ok
    high_weight = ramp * high_ok
    head = span[:, edge : 2 * edge] * (1.0 - low_weight) + under * low_weight
    foot = span[:, keep : keep + edge] * (1.0 - high_weight) + over * high_weight
    kept = jnp.concatenate([head, span[:, 2 * edge : keep], foot], axis=1)
    joined = jnp.concatenate([kept[2 * slot + 2 : 2 * slot + 4] for slot in range(slots)], axis=1)
    for part in range(2):
        out_ref[part] = joined[part : part + 1]


def beam(voltages, section1_taps, section2_taps, band_starts, band_widths):
    tap_count, chan_len = section1_taps.shape
    tms, zooms = lax.axis_size("tm"), lax.axis_size("zoom")
    count = tms * zooms
    row_len = GROUP * HOP
    rows = voltages.shape[2] // row_len
    blocks = row_len // LANE
    signal = voltages[0].reshape(2, rows, blocks, LANE).transpose(1, 2, 0, 3)
    fine_len = section2_taps.shape[1]
    freq_count = fine_len // GROUP
    freq = -(-freq_count // LANE) * LANE
    lane_tiles = -(-2 * rows // LANE)
    shift = KEEP // 2 + EDGE
    bins = np.arange(freq_count) - shift
    spot = np.arange(freq_count)
    angles = 2.0 * np.pi * ((spot[:, None] * bins[None, :]) % freq_count) / freq_count
    folded = 2 * freq_count
    table = np.zeros((-(-folded // (2 * LANE)) * LANE, 2, 2, freq))
    table[:freq_count, 0, 0, :freq_count] = np.cos(angles)
    table[:freq_count, 0, 1, :freq_count] = -np.sin(angles)
    table[:freq_count, 1, 0, :freq_count] = np.sin(angles)
    table[:freq_count, 1, 1, :freq_count] = np.cos(angles)
    table = table.reshape(-1, 2 * freq)[: -(-folded // LANE) * LANE]
    table = jnp.asarray(table.astype(np.float32).astype(jnp.bfloat16))
    phases = 2.0 * np.pi * ((np.arange(GROUP)[:, None] * bins[None, :]) % fine_len) / fine_len
    twist = np.zeros((2, GROUP, freq), np.float32)
    twist[0, :, :freq_count] = np.cos(phases)
    twist[1, :, :freq_count] = np.sin(phases)
    slots = CH_DEV
    per = LIVE_DEV
    live = per * count

    def owners(line):
        return [slot // slots for slot in (line, live - 1 - line) if slot < slots * tms]

    order = sorted(range(live), key=lambda line: (sum(owners(line)) / len(owners(line)), line))
    homes = [order[per * device : per * device + per] for device in range(count)]
    needs = []
    for device in range(count):
        needed = [device // zooms * slots + item - 1 for item in range(slots + 2)]
        needed = [slot if 0 <= slot < slots * tms else None for slot in needed]
        flip = device % zooms
        needs.append([live - 1 - slot if flip and slot is not None else slot for slot in needed])
    wheel = 2.0 * np.pi * ((np.arange(GROUP)[:, None] * np.arange(GROUP)[None, :]) % GROUP) / GROUP
    core = np.zeros((2, GROUP, 2, GROUP))
    core[0, :, 0] = np.cos(wheel)
    core[0, :, 1] = np.sin(wheel)
    core[1, :, 0] = -np.sin(wheel)
    core[1, :, 1] = np.cos(wheel)
    eight = np.zeros((per, 2, GROUP, 2, per, GROUP), np.float32)
    for place in range(per):
        eight[place, :, :, :, place] = core
    lines = per * GROUP
    eight = eight.reshape(2 * lines, 2 * lines)
    reach = tap_count * chan_len - HOP
    held = rows + 2
    columns = GROUP * SLOT
    groups = [[0], list(range(1, lane_tiles - 2)), [lane_tiles - 2]]
    parcels = [
        pltpu.VMEM((count, lines + GROUP * (group == groups[-1]), len(group) * LANE), jnp.bfloat16)
        for group in groups
    ]
    cfg = (tms, zooms, HOP, chan_len, reach, slots, KEEP, EDGE, folded, homes, needs, groups)
    lead = (columns // LANE - 1) * 2 * HOP
    depth = lead + -(-(3 * HOP + tap_count * chan_len) // LANE) * LANE
    turns = -(-(row_len - HOP + tap_count * chan_len) // row_len)
    bf, f32 = jnp.bfloat16, jnp.float32
    hbm = pl.BlockSpec(memory_space=pltpu.HBM)
    vmem = pl.BlockSpec(memory_space=pltpu.VMEM)
    result = pl.pallas_call(
        functools.partial(beam_kernel, cfg),
        out_shape=jax.ShapeDtypeStruct((2, 1, slots * KEEP), f32),
        in_specs=[hbm] * 8,
        out_specs=vmem,
        scratch_shapes=[
            pltpu.SMEM(band_starts.shape, jnp.int32),
            pltpu.SMEM(band_widths.shape, jnp.int32),
            pltpu.VMEM(section1_taps.shape, f32),
            pltpu.VMEM(section2_taps.shape, f32),
            pltpu.VMEM(twist.shape, f32),
            pltpu.VMEM(eight.shape, f32),
            pltpu.SemaphoreType.DMA((6,)),
            pltpu.VMEM((blocks, held, 2, LANE), bf),
            pltpu.VMEM((depth, LANE), bf),
            pltpu.VMEM((LANE, chan_len), f32),
            pltpu.VMEM((GROUP, lane_tiles * LANE), f32),
            pltpu.VMEM((GROUP, lane_tiles * LANE * GROUP // 2), f32),
            pltpu.VMEM((blocks, 2 * held, LANE), bf),
            pltpu.VMEM((turns, lane_tiles * LANE + 16, columns), f32),
            pltpu.VMEM((lane_tiles, columns, LANE), f32),
            parcels,
            parcels,
            pltpu.VMEM(table.shape, bf),
            pltpu.VMEM((2 * lines, freq), bf),
            pltpu.VMEM((slots + 2, 2 * GROUP, freq), bf),
            pltpu.VMEM((freq // LANE, (slots + 3) * 2 * GROUP, LANE), f32),
            pltpu.SemaphoreType.DMA((len(groups), blocks)),
            pltpu.SemaphoreType.DMA,
            pltpu.SemaphoreType.DMA((2, 2)),
            pltpu.SemaphoreType.DMA((len(groups), count)),
            pltpu.SemaphoreType.DMA((len(groups), count)),
            pltpu.SemaphoreType.DMA((4 * per,)),
            pltpu.SemaphoreType.DMA((slots + 2,)),
        ],
        compiler_params=pltpu.CompilerParams(
            collective_id=0, has_side_effects=True, vmem_limit_bytes=48 << 20
        ),
        name="beam",
    )(*[
        pltpu.with_memory_space_constraint(operand, pltpu.HBM)
        for operand in (band_starts, band_widths, section1_taps, section2_taps, twist, eight, signal, table)
    ])
    return result.reshape(1, 1, 2, 1, slots * KEEP)


def general(voltages, section1_taps, section2_taps, band_starts, band_widths):
    signal = voltages[0]
    tap_count, chan_len = section1_taps.shape
    spectra = signal.shape[1] // HOP
    rim_len = tap_count * chan_len - HOP
    tm_count = lax.axis_size("tm")
    zoom_count = lax.axis_size("zoom")
    device_count = tm_count * zoom_count
    slot_count = tm_count * CH_DEV
    width = CH_DEV + 2
    following = shifted(signal[:, :rim_len], ("tm", "zoom"), -1)
    span = slot_count + 2
    band_slots = jnp.arange(-1, slot_count + 1, dtype=jnp.int32)
    channels = ((band_starts[:, None] + band_slots[None, :]) % chan_len).reshape(-1)
    picks = [tm * CH_DEV + zoom * span for tm in range(tm_count) for zoom in range(zoom_count)]
    pieces = -(-chan_len // HOP)
    padded = jnp.concatenate(
        [signal, following, jnp.zeros((2, pieces * HOP), jnp.bfloat16)], axis=1
    )
    frames = weighted_frames(padded, section1_taps, spectra, HOP)
    coarse = jnp.einsum(
        "pqkn,qsn->pks", rotation_block(chan_len), frames, preferred_element_type=jnp.float32
    ).astype(jnp.bfloat16)
    wanted = np.arange(width)[:, None] + np.asarray(picks)[None, :]
    hot = channels[wanted.reshape(-1)][:, None] == jnp.arange(chan_len, dtype=jnp.int32)[None, :]
    packed = jnp.einsum(
        "lk,pks->pls", hot.astype(jnp.bfloat16), coarse, preferred_element_type=jnp.float32
    ).astype(jnp.bfloat16)
    packed = packed.reshape(2, width, device_count, spectra)
    received = lax.all_to_all(packed, ("tm", "zoom"), split_axis=2, concat_axis=2, tiled=True)
    series = received.reshape(2, width, -1)
    weighted, order = natural_order(series, section2_taps, FA, FB)
    spans = fine_spectra(weighted, order, KEEP, EDGE)
    slot_ids = lax.axis_index("tm") * CH_DEV + jnp.arange(CH_DEV, dtype=jnp.int32)
    band_ids = jnp.arange(band_widths.shape[0], dtype=jnp.int32)
    band_width = jnp.sum(jnp.where(band_ids == lax.axis_index("zoom"), band_widths, 0))
    upper_rim = spans[:, 2:, :, :EDGE]
    lower_rim = spans[:, :CH_DEV, :, KEEP + EDGE :]
    extended = spans[:, 1 : CH_DEV + 1]
    stitched = stitch_bands(extended, upper_rim, lower_rim, slot_ids, band_width, KEEP, EDGE)
    fine_count = stitched.shape[2]
    result = jnp.transpose(stitched, (0, 2, 1, 3)).reshape(2, fine_count, CH_DEV * KEEP)
    return result[None, None]


def on_device(voltages, section1_taps, section2_taps, band_starts, band_widths):
    chan_len = section1_taps.shape[1]
    tm_count, zoom_count = lax.axis_size("tm"), lax.axis_size("zoom")
    live = LIVE_DEV * tm_count * zoom_count
    row_len = GROUP * HOP
    fits = (
        zoom_count == 2
        and band_widths.shape[0] == 2
        and CH_DEV * tm_count <= live
        and live <= PART
        and chan_len & (chan_len - 1) == 0
        and voltages.shape[2] % row_len == 0
        and row_len % LANE == 0
        and voltages.shape[2] // row_len * tm_count * zoom_count * GROUP % section2_taps.shape[1] == 0
        and section1_taps.shape[0] * chan_len - HOP <= 2 * row_len
        and 0 < 2 * (voltages.shape[2] // row_len) % LANE <= LANE // (LIVE_DEV + 1)
        and 2 * (voltages.shape[2] // row_len) > 3 * LANE
        and section2_taps.shape[1] == FA * FB
    )
    chosen = beam if fits else general
    return chosen(voltages, section1_taps, section2_taps, band_starts, band_widths)


def solution(mesh):
    placed = (P("pol", "groups", ("tm", "zoom")), P(), P(), P("groups"), P("groups"))
    return jax.shard_map(
        on_device,
        mesh=mesh,
        in_specs=placed,
        out_specs=P("pol", "zoom", "groups", None, "tm"),
        check_vma=False,
    )
```

```python
import functools
import math

import jax
import jax.numpy as jnp
import numpy as np
from jax import lax
from jax.experimental import pallas as pl
from jax.experimental.pallas import tpu as pltpu
from jax.sharding import PartitionSpec as P

HOP = 432
FA = 27
FB = 128
KEEP = 2916
EDGE = 128
CH_DEV = 5
LIVE_DEV = 3


def shifted(value, axis, steps):
    count = lax.axis_size(axis)
    initial, last = (max(0, -steps), min(count, count - steps))
    return lax.ppermute(value, axis, [(source, source + steps) for source in range(initial, last)])


def angle_table(rows, cols, length):
    product = (
        jnp.arange(rows, dtype=jnp.int32)[:, None]
        * jnp.arange(cols, dtype=jnp.int32)[None, :]
        % length
    )
    return product.astype(jnp.float32) * (2.0 * math.pi / length)


def rotation_block(length):
    angles = angle_table(length, length, length)
    cosine_tab = jnp.cos(angles).astype(jnp.bfloat16)
    sine_tab = jnp.sin(angles).astype(jnp.bfloat16)
    return jnp.stack([jnp.stack([cosine_tab, sine_tab]), jnp.stack([-sine_tab, cosine_tab])])


def frame_view(segment, spectra, chan_len, hop_len):
    pieces = -(-chan_len // hop_len)
    framed = segment[:, : (spectra + pieces - 1) * hop_len].reshape(
        segment.shape[0], spectra + pieces - 1, hop_len
    )
    joined = jnp.concatenate(
        [framed[:, offset : offset + spectra] for offset in range(pieces)], axis=2
    )
    return joined[:, :, :chan_len]


def weighted_frames(signal, taps, spectra, hop_len):
    chan_len = taps.shape[1]
    running = jnp.zeros((2, spectra, chan_len), jnp.float32)
    for tap_index in range(taps.shape[0]):
        frames = frame_view(signal[:, tap_index * chan_len :], spectra, chan_len, hop_len)
        running = running + taps[tap_index][None, None, :] * frames.astype(jnp.float32)
    return running.astype(jnp.bfloat16)


def natural_order(series, section2_taps, radix_a, radix_b):
    tap_count, fine_len = section2_taps.shape
    items = series.shape[1]
    row_count = series.shape[2] // fine_len
    spectra = row_count - tap_count + 1
    row_blocks = series.reshape(2, items, row_count, fine_len)
    running = jnp.zeros((2, items, spectra, fine_len), jnp.float32)
    for tap_index in range(tap_count):
        running = running + section2_taps[tap_index] * row_blocks[
            :, :, tap_index : tap_index + spectra
        ].astype(jnp.float32)
    weighted = running.astype(jnp.bfloat16).reshape(2, items, spectra, radix_a, radix_b)
    return weighted, np.arange(radix_b)


def ordered_angles(rows, order, length):
    product = (np.arange(rows)[:, None] * order[None, :] % length).astype(np.float32)
    return jnp.asarray(product) * (2.0 * math.pi / length)


def fine_spectra(weighted, order, keep_len, edge_len):
    _, items, spectra, radix_a, radix_b = weighted.shape
    fine_len = radix_a * radix_b
    partial_value = jnp.einsum(
        "pqkm,qcfmb->pcfkb", rotation_block(radix_a), weighted, preferred_element_type=jnp.float32
    )
    angles = ordered_angles(radix_a, order, fine_len)
    cosine_tab = jnp.cos(angles)
    sine_tab = jnp.sin(angles)
    real_part = partial_value[0] * cosine_tab + partial_value[1] * sine_tab
    imag_part = partial_value[1] * cosine_tab - partial_value[0] * sine_tab
    twiddled = jnp.concatenate([real_part, imag_part], axis=-1).astype(jnp.bfloat16)
    turned = ordered_angles(radix_b, order, radix_b).T
    cosine_b = jnp.cos(turned).astype(jnp.bfloat16)
    sine_b = jnp.sin(turned).astype(jnp.bfloat16)
    table = jnp.concatenate(
        [jnp.stack([cosine_b, -sine_b], axis=1), jnp.stack([sine_b, cosine_b], axis=1)], axis=0
    )
    spectrum = jnp.einsum(
        "cfkm,mpq->pcfqk", twiddled, table, preferred_element_type=jnp.float32
    ).reshape(2, items, spectra, fine_len)
    first = (-(keep_len // 2) - edge_len) % fine_len
    rest = keep_len + 2 * edge_len - (fine_len - first)
    return jnp.concatenate([spectrum[..., first:], spectrum[..., :rest]], axis=-1)


def stitch_bands(extended, upper_rim, lower_rim, slot_ids, band_width, keep_len, edge_len):
    centre = extended[..., edge_len : edge_len + keep_len]
    live = (slot_ids < band_width).astype(jnp.float32)[None, :, None, None]
    upper_ok = (slot_ids + 1 < band_width).astype(jnp.float32)[None, :, None, None]
    lower_ok = ((slot_ids >= 1) & (slot_ids < band_width)).astype(jnp.float32)[None, :, None, None]
    ramp = (jnp.arange(edge_len, dtype=jnp.float32) + 0.5) / (2.0 * edge_len)
    upper_weight = ramp * upper_ok
    lower_weight = ramp[::-1] * lower_ok
    low_part = centre[..., :edge_len] * (1.0 - lower_weight) + lower_rim * lower_weight
    high_part = centre[..., keep_len - edge_len :] * (1.0 - upper_weight) + upper_rim * upper_weight
    joined = jnp.concatenate(
        [low_part, centre[..., edge_len : keep_len - edge_len], high_part], axis=-1
    )
    return joined * live


GROUP = 8
LANE = 128
SLOT = 64
PART = 32


def sine(x):
    square = x * x
    total = jnp.full_like(x, -1.0 / 39916800.0)
    for factor in (1.0 / 362880.0, -1.0 / 5040.0, 1.0 / 120.0, -1.0 / 6.0, 1.0):
        total = total * square + factor
    return total * x


def fill_bank(starts_ref, widths_ref, taps_ref, rot_len, hop, lead, live, bank, spread):
    lanes = lax.broadcasted_iota(jnp.int32, (LANE, LANE), 1)
    upper = lanes // SLOT
    quarter = (lanes % SLOT) // PART
    member = lanes % PART
    channel = jnp.where(
        member < widths_ref[0], starts_ref[0] + member, starts_ref[1] + (live - 1) - member
    )
    rows_of = lax.broadcasted_iota(jnp.int32, (LANE, LANE), 0)
    steps = -(-(taps_ref.shape[0] + 1) // GROUP) * GROUP
    filling = jnp.zeros((steps - taps_ref.shape[0], rot_len), jnp.float32)
    taps = jnp.concatenate([taps_ref[...], filling], axis=0)
    rolled = pltpu.roll(taps, hop, 1)
    down = pltpu.roll(rolled, 1, 0)
    behind = jnp.where(lax.broadcasted_iota(jnp.int32, rolled.shape, 1) < hop, down, rolled)
    value = jnp.concatenate([taps, behind], axis=0)
    parts = 3
    for part in range(parts):
        head = value.astype(jnp.bfloat16).astype(jnp.float32)
        spread[pl.ds(part * 2 * steps, 2 * steps), :] = head
        value = value - head
    spent = parts * 2 * steps
    spread[pl.ds(spent, LANE - spent), :] = jnp.zeros((LANE - spent, rot_len), jnp.float32)
    half = rot_len // 2
    turned, rots = [], []
    for block in range(rot_len // LANE):
        turned.append(jnp.transpose(spread[:, pl.ds(block * LANE, LANE)]))
        place = rows_of + block * LANE - upper * hop
        turn = (place * channel - quarter * (rot_len // 4)) & (rot_len - 1)
        angle = (jnp.abs(turn - half) - half // 2).astype(jnp.float32) * (2.0 * math.pi / rot_len)
        rots.append(sine(angle).astype(jnp.bfloat16).astype(jnp.float32))
    left = jnp.concatenate(turned, axis=0).astype(jnp.bfloat16)
    rot = jnp.concatenate(rots, axis=0)
    count = taps_ref.shape[0] + 1
    for tap in range(0, count, 2):
        group = range(tap, min(tap + 2, count))
        picks = [
            jnp.where((rows_of % (2 * steps) == one + upper * steps) & (rows_of < spent), 1.0, 0.0)
            for one in group
        ]
        taken = jnp.dot(
            left, jnp.concatenate(picks, axis=1).astype(jnp.bfloat16), preferred_element_type=jnp.float32
        )
        for index, one in enumerate(group):
            piece = taken[:, index * LANE : (index + 1) * LANE]
            bank[pl.ds(lead + one * rot_len, rot_len), :] = (piece * rot).astype(jnp.bfloat16)


def fill_taps(taps_ref, me, count, length, ground, tapw):
    fine_len = taps_ref.shape[1]
    whole = ground.shape[1]
    for device in range(count):

        @pl.when(me == device)
        def _():
            place, stop, pieces = device * length, (device + 1) * length, []
            while place < stop:
                row, lane = divmod(place, fine_len)
                size = min(fine_len - lane, stop - place)
                pieces.append(taps_ref[pl.ds(row, 1), :][:, lane : lane + size])
                place += size
            pieces.append(jnp.zeros((1, whole - length), jnp.float32))
            ground[...] = jnp.broadcast_to(jnp.concatenate(pieces, axis=1), ground.shape)

    span = LANE * GROUP // 2
    lanes = lax.broadcasted_iota(jnp.int32, (GROUP, span), 1)
    chosen = lanes % GROUP == lax.broadcasted_iota(jnp.int32, (GROUP, span), 0)
    parts = []
    for tile in range(whole // span):
        value = jnp.where(chosen, ground[:, pl.ds(tile * span, span)], 0.0)
        for _ in range(3):
            head = value.astype(jnp.bfloat16)
            parts.append(head.astype(jnp.float32))
            value = value - head.astype(jnp.float32)
    source = lax.broadcasted_iota(jnp.int32, (span, LANE), 0) // GROUP
    target = lax.broadcasted_iota(jnp.int32, (span, LANE), 1) // 2
    moved = jnp.where(source == target, 1.0, 0.0).astype(jnp.bfloat16)
    placed = jnp.dot(
        jnp.concatenate(parts, axis=0).astype(jnp.bfloat16), moved, preferred_element_type=jnp.float32
    )
    for tile in range(whole // span):
        row = 3 * GROUP * tile
        tapw[:, pl.ds(tile * LANE, LANE)] = (
            placed[row : row + GROUP]
            + placed[row + GROUP : row + 2 * GROUP]
            + placed[row + 2 * GROUP : row + 3 * GROUP]
        )


def beam_kernel(
    cfg,
    starts_in,
    widths_in,
    taps_in,
    fine_taps_in,
    twist_in,
    eight_in,
    x_ref,
    table_ref,
    out_ref,
    starts_ref,
    widths_ref,
    taps_ref,
    fine_taps_ref,
    twist_ref,
    eight_ref,
    small_sems,
    data,
    bank,
    spread,
    tapw_ref,
    ground,
    native,
    total,
    turned,
    sends,
    recvs,
    table,
    pair,
    gathered,
    flat,
    x_sems,
    table_sem,
    halo_sems,
    send_sems,
    recv_sems,
    out_sems,
    in_sems,
):
    tms, zooms, hop, rot_len, reach, slots, keep, edge, folded, homes, needs, groups = cfg
    per = len(homes[0])
    live = per * len(homes)
    rows, blocks = x_ref.shape[0], x_ref.shape[1]
    row_len = blocks * LANE
    count = tms * zooms
    tm = lax.axis_index("tm")
    zoom = lax.axis_index("zoom")
    me = tm * zooms + zoom
    gathered[...] = jnp.zeros_like(gathered)
    barrier = pltpu.get_barrier_semaphore()

    def where_is(index):
        return {"tm": index // zooms, "zoom": lax.rem(index, zooms)}

    for step in range(1, count):
        pl.semaphore_signal(
            barrier,
            inc=1,
            device_id=where_is(lax.rem(me + step, count)),
            device_id_type=pl.DeviceIdType.MESH,
        )
    smalls = [
        pltpu.make_async_copy(source, target, small_sems.at[index])
        for index, (source, target) in enumerate(
            (
                (starts_in, starts_ref),
                (widths_in, widths_ref),
                (taps_in, taps_ref),
                (fine_taps_in, fine_taps_ref),
                (twist_in, twist_ref),
                (eight_in, eight_ref),
            )
        )
    ]
    for copy in smalls:
        copy.start()
    held = data.shape[1]
    cuts = [0] + [(group[-1] * LANE + LANE + 16) // 2 for group in groups[:-1]] + [held]
    spans = [(low, min(high, rows) - low) for low, high in zip(cuts[:-1], cuts[1:])]
    loads = []
    for which, (start, size) in enumerate(spans):
        loads.append([])
        for block in range(blocks):
            copy = pltpu.make_async_copy(
                x_ref.at[pl.ds(start, size), block],
                data.at[block, pl.ds(start, size)],
                x_sems.at[which, block],
            )
            loads[which].append(copy)
    for copy in loads[0]:
        copy.start()
    table_copy = pltpu.make_async_copy(table_ref, table, table_sem)
    table_copy.start()
    rest = -(-(reach - row_len) // LANE)
    data[pl.ds(rest, blocks - rest), pl.ds(rows + 1, 1)] = jnp.zeros(
        (blocks - rest, 1, 2, LANE), data.dtype
    )

    @pl.when(me == count - 1)
    def _():
        data[:, pl.ds(rows, 1)] = jnp.zeros((blocks, 1, 2, LANE), data.dtype)
        data[pl.ds(0, rest), pl.ds(rows + 1, 1)] = jnp.zeros((rest, 1, 2, LANE), data.dtype)

    columns = GROUP * SLOT
    wide = 2 * LANE
    tiles = columns // wide
    apart = 2 * hop
    lead = (columns // LANE - 1) * apart
    turns = total.shape[0]
    total[:, pl.ds(2 * held, total.shape[1] - 2 * held), :] = jnp.zeros(
        (turns, total.shape[1] - 2 * held, columns), jnp.float32
    )
    bank[pl.ds(0, lead), :] = jnp.zeros((lead, LANE), jnp.bfloat16)
    tail = lead + (taps_ref.shape[0] + 1) * rot_len
    bank[pl.ds(tail, bank.shape[0] - tail), :] = jnp.zeros((bank.shape[0] - tail, LANE), jnp.bfloat16)
    for copy in smalls:
        copy.wait()
    fill_bank(
        starts_ref, widths_ref, taps_ref, rot_len, hop, lead, live, bank, spread
    )
    fill_taps(fine_taps_ref, me, count, rows * GROUP, ground, tapw_ref)
    pl.semaphore_wait(barrier, count - 1)
    before = lax.rem(me + count - 1, count)
    halo = [
        pltpu.make_async_remote_copy(
            src_ref=source,
            dst_ref=target,
            send_sem=halo_sems.at[0, index],
            recv_sem=halo_sems.at[1, index],
            device_id=where_is(before),
            device_id_type=pl.DeviceIdType.MESH,
        )
        for index, (source, target) in enumerate(
            (
                (x_ref.at[0], data.at[:, rows]),
                (x_ref.at[1, pl.ds(0, rest)], data.at[pl.ds(0, rest), rows + 1]),
            )
        )
    ]

    @pl.when(me > 0)
    def _():
        for copy in halo:
            copy.start()

    def multiply(start, size):
        for block in range(blocks):
            native[block, pl.ds(2 * start, 2 * size), :] = data.at[block, pl.ds(start, size)].reshape(
                2 * size, LANE
            )[...]
        for tile in range(tiles):
            low = tile * 2 * apart
            high = low + 3 * hop + reach + hop
            for turn in range(turns):
                one = max(turn * blocks, low // LANE)
                end = min((turn + 1) * blocks, -(-high // LANE))
                picks = range(one, end)
                left = jnp.concatenate(
                    [
                        native[block - turn * blocks, pl.ds(2 * start, 2 * size), :]
                        for block in picks
                    ],
                    axis=1,
                )
                right = jnp.concatenate(
                    [
                        bank[pl.ds(lead + one * LANE - (2 * tile + part) * apart, (end - one) * LANE), :]
                        for part in range(2)
                    ],
                    axis=1,
                )
                total[turn, pl.ds(2 * start, 2 * size), pl.ds(tile * wide, wide)] = jnp.dot(
                    left, right, preferred_element_type=jnp.float32
                )

    def turn_round(tile):
        row = tile * LANE
        for col in range(columns // LANE):
            whole = total[0, pl.ds(row, LANE), pl.ds(col * LANE, LANE)]
            for turn in range(1, turns):
                whole += total[turn, pl.ds(row + 2 * turn, LANE), pl.ds(col * LANE, LANE)]
            turned[tile, pl.ds(col * LANE, LANE), :] = jnp.transpose(whole)

    even = lax.broadcasted_iota(jnp.int32, (GROUP, LANE), 1) % 2 == 0

    def line_of(tile, line):
        cosine = turned[tile, pl.ds(line, GROUP, stride=SLOT), :]
        sine_part = turned[tile, pl.ds(PART + line, GROUP, stride=SLOT), :]
        swapped_part = jnp.where(
            even, pltpu.roll(sine_part, LANE - 1, 1), -pltpu.roll(sine_part, 1, 1)
        )
        return (cosine + swapped_part) * tapw_ref[:, pl.ds(tile * LANE, LANE)]

    def pack(out, first, tile_ids, extra):
        for dest in range(count):
            for tile in tile_ids:
                values = [line_of(tile, line) for line in homes[dest]]
                if extra and tile == first:
                    value = line_of(lane_tiles - 1, homes[dest][0])
                    for place in range(1, per):
                        moved = line_of(lane_tiles - 1, homes[dest][place])
                        value += pltpu.roll(moved, place * last_width, 1)
                    values.append(value)
                elif extra:
                    values.append(jnp.zeros((GROUP, LANE), jnp.float32))
                value = jnp.concatenate(values, axis=0)
                out[dest, :, pl.ds((tile - first) * LANE, LANE)] = value.astype(jnp.bfloat16)

    def exchange(which, source, target):
        copies = []
        for step in sorted(range(1, count), key=lambda step: abs(2 * step - count)):
            other = lax.rem(me + step, count)
            copy = pltpu.make_async_remote_copy(
                src_ref=source.at[other],
                dst_ref=target.at[me],
                send_sem=send_sems.at[which, step],
                recv_sem=recv_sems.at[which, step],
                device_id=where_is(other),
                device_id_type=pl.DeviceIdType.MESH,
            )
            copy.start()
            copies.append(copy)
        target[me] = source[me]
        return copies

    lane_tiles = turned.shape[0]
    lines = per * GROUP
    last_width = LANE // (per + 1)
    copies = []
    for index, group in enumerate(groups):
        ending = index == len(groups) - 1
        for copy in loads[index]:
            copy.wait()
        if not ending:
            for copy in loads[index + 1]:
                copy.start()
        else:

            @pl.when(me > 0)
            def _():
                for copy in halo:
                    copy.wait_send()

            @pl.when(me < count - 1)
            def _():
                for copy in halo:
                    copy.wait_recv()

        multiply(cuts[index], cuts[index + 1] - cuts[index])
        for tile in group + [lane_tiles - 1] * ending:
            turn_round(tile)
        pack(sends[index], group[0], group, ending)
        copies += exchange(index, sends[index], recvs[index])
    table_copy.wait()
    for copy in copies:
        copy.wait_recv()

    ring = -(-folded // LANE) + lane_tiles + 1
    sums = [None] * ring
    lane_ids = lax.broadcasted_iota(jnp.int32, (lines, LANE), 1)

    def put(tile, value):
        sums[tile] = value if sums[tile] is None else sums[tile] + value

    for source in range(count):
        offset = 2 * rows * source % folded
        base, shift = offset // LANE, offset % LANE
        for tile in range(lane_tiles):
            if tile < lane_tiles - 1:
                index = [tile in group for group in groups].index(True)
                piece = recvs[index][source, :, pl.ds((tile - groups[index][0]) * LANE, LANE)]
                piece = piece.astype(jnp.float32)[:lines]
            else:
                piece = recvs[-1][source, :, pl.ds(0, LANE)].astype(jnp.float32)[lines:]
                piece = jnp.concatenate(
                    [piece] + [pltpu.roll(piece, LANE - place * last_width, 1) for place in range(1, per)],
                    axis=0,
                )
                piece = jnp.where(lane_ids < last_width, piece, 0.0)
            if shift:
                piece = pltpu.roll(piece, shift, 1)
                put(base + tile, jnp.where(lane_ids >= shift, piece, 0.0))
                put(base + tile + 1, jnp.where(lane_ids < shift, piece, 0.0))
            else:
                put(base + tile, piece)
    base, shift = folded // LANE, folded % LANE
    for tile in range(base, ring):
        if sums[tile] is None:
            continue
        value = pltpu.roll(sums[tile], LANE - shift, 1) if shift else sums[tile]
        if shift and tile > base:
            put(tile - base - 1, jnp.where(lane_ids >= LANE - shift, value, 0.0))
        put(tile - base, jnp.where(lane_ids < LANE - shift, value, 0.0))
    used = -(-folded // LANE)
    weighted = jnp.concatenate(sums[:used], axis=1).astype(jnp.bfloat16)
    freq = table.shape[1] // 2
    partial_value = jnp.dot(weighted, table[...], preferred_element_type=jnp.float32)
    real, imag = partial_value[:, :freq], partial_value[:, freq:]
    cosine = jnp.concatenate([twist_ref[0]] * per, axis=0)
    sine_part = jnp.concatenate([twist_ref[1]] * per, axis=0)
    both = jnp.concatenate(
        [real * cosine + imag * sine_part, imag * cosine - real * sine_part], axis=0
    )
    spectrum = jnp.dot(
        eight_ref[...], both, preferred_element_type=jnp.float32, precision=lax.Precision.HIGHEST
    )
    pair[...] = spectrum.astype(jnp.bfloat16)
    high = 2 * GROUP

    sizes = [2 * LANE] + [freq] * slots + [LANE]

    def outward(source, target, index, device):
        return pltpu.make_async_remote_copy(
            src_ref=pair.at[pl.ds(source * high, high), pl.ds(0, sizes[target])],
            dst_ref=gathered.at[target, :, pl.ds(0, sizes[target])],
            send_sem=out_sems.at[index],
            recv_sem=in_sems.at[target],
            device_id={"tm": device // zooms, "zoom": device % zooms},
            device_id_type=pl.DeviceIdType.MESH,
        )

    for device in range(count):
        sent = [
            (place, target, other)
            for place, line in enumerate(homes[device])
            for other in range(count)
            for target in range(slots + 2)
            if needs[other][target] == line and other != device
        ]
        sent.sort(key=lambda item: -abs(item[2] // zooms - device // zooms))
        kept = [
            (homes[device].index(line), target)
            for target, line in enumerate(needs[device])
            if line in homes[device]
        ]
        taken = [
            target
            for target, line in enumerate(needs[device])
            if line is not None and line not in homes[device]
        ]

        @pl.when(me == device)
        def _():
            leaving = [
                outward(place, target, index, other)
                for index, (place, target, other) in enumerate(sent)
            ]
            for copy in leaving:
                copy.start()
            for place, target in kept:
                gathered[target] = pair[pl.ds(place * high, high)]
            for target in taken:
                outward(0, target, 0, (device + 1) % count).wait_recv()
            for copy in leaving:
                copy.wait_send()

    width = widths_ref[0] + zoom * (widths_ref[1] - widths_ref[0])
    for item in range(slots + 2):
        slot = tm * slots + item - 1
        real = ((slot >= 0) & (slot < width)).astype(jnp.int32)
        live_here = jnp.full((high, freq), real, jnp.int32) > 0
        value = jnp.where(live_here, gathered[item].astype(jnp.float32), 0.0)
        for tile in range(freq // LANE):
            flat[tile, pl.ds(item * high, high), :] = value[:, tile * LANE : (tile + 1) * LANE]
    for copy in copies:
        copy.wait_send()
    stitch(flat, out_ref, width, tm * slots, slots, keep, edge, folded // 2)


def stitch(flat, out_ref, width, first, slots, keep, edge, freq):
    lines = 2 * GROUP
    pieces = [
        [flat[tile, pl.ds(turn, lines, stride=GROUP), :] for tile in range(flat.shape[0])]
        for turn in range(GROUP)
    ]
    span = jnp.concatenate([jnp.concatenate(row, axis=1)[:, :freq] for row in pieces], axis=1)
    slot = lax.broadcasted_iota(jnp.int32, (lines, edge), 0) // 2 - 1 + first
    low_ok = jnp.where((slot >= 1) & (slot < width), 1.0, 0.0)
    high_ok = jnp.where(slot + 1 < width, 1.0, 0.0)
    place = lax.broadcasted_iota(jnp.int32, (lines, edge), 1).astype(jnp.float32)
    ramp = (place + 0.5) / (2.0 * edge)
    fall = (edge - place - 0.5) / (2.0 * edge)
    under = pltpu.roll(span[:, keep + edge : keep + 2 * edge], 2, 0)
    over = pltpu.roll(span[:, :edge], lines - 2, 0)
    low_weight = fall * low_ok
    high_weight = ramp * high_ok
    head = span[:, edge : 2 * edge] * (1.0 - low_weight) + under * low_weight
    foot = span[:, keep : keep + edge] * (1.0 - high_weight) + over * high_weight
    kept = jnp.concatenate([head, span[:, 2 * edge : keep], foot], axis=1)
    joined = jnp.concatenate([kept[2 * slot + 2 : 2 * slot + 4] for slot in range(slots)], axis=1)
    for part in range(2):
        out_ref[part] = joined[part : part + 1]


def beam(voltages, section1_taps, section2_taps, band_starts, band_widths):
    tap_count, chan_len = section1_taps.shape
    tms, zooms = lax.axis_size("tm"), lax.axis_size("zoom")
    count = tms * zooms
    row_len = GROUP * HOP
    rows = voltages.shape[2] // row_len
    blocks = row_len // LANE
    signal = voltages[0].reshape(2, rows, blocks, LANE).transpose(1, 2, 0, 3)
    fine_len = section2_taps.shape[1]
    freq_count = fine_len // GROUP
    freq = -(-freq_count // LANE) * LANE
    lane_tiles = -(-2 * rows // LANE)
    shift = KEEP // 2 + EDGE
    bins = np.arange(freq_count) - shift
    spot = np.arange(freq_count)
    angles = 2.0 * np.pi * ((spot[:, None] * bins[None, :]) % freq_count) / freq_count
    folded = 2 * freq_count
    table = np.zeros((-(-folded // (2 * LANE)) * LANE, 2, 2, freq))
    table[:freq_count, 0, 0, :freq_count] = np.cos(angles)
    table[:freq_count, 0, 1, :freq_count] = -np.sin(angles)
    table[:freq_count, 1, 0, :freq_count] = np.sin(angles)
    table[:freq_count, 1, 1, :freq_count] = np.cos(angles)
    table = table.reshape(-1, 2 * freq)[: -(-folded // LANE) * LANE]
    table = jnp.asarray(table.astype(np.float32).astype(jnp.bfloat16))
    phases = 2.0 * np.pi * ((np.arange(GROUP)[:, None] * bins[None, :]) % fine_len) / fine_len
    twist = np.zeros((2, GROUP, freq), np.float32)
    twist[0, :, :freq_count] = np.cos(phases)
    twist[1, :, :freq_count] = np.sin(phases)
    slots = CH_DEV
    per = LIVE_DEV
    live = per * count

    def owners(line):
        return [slot // slots for slot in (line, live - 1 - line) if slot < slots * tms]

    order = sorted(range(live), key=lambda line: (sum(owners(line)) / len(owners(line)), line))
    homes = [order[per * device : per * device + per] for device in range(count)]
    needs = []
    for device in range(count):
        needed = [device // zooms * slots + item - 1 for item in range(slots + 2)]
        needed = [slot if 0 <= slot < slots * tms else None for slot in needed]
        flip = device % zooms
        needs.append([live - 1 - slot if flip and slot is not None else slot for slot in needed])
    wheel = 2.0 * np.pi * ((np.arange(GROUP)[:, None] * np.arange(GROUP)[None, :]) % GROUP) / GROUP
    core = np.zeros((2, GROUP, 2, GROUP))
    core[0, :, 0] = np.cos(wheel)
    core[0, :, 1] = np.sin(wheel)
    core[1, :, 0] = -np.sin(wheel)
    core[1, :, 1] = np.cos(wheel)
    eight = np.zeros((per, 2, GROUP, 2, per, GROUP), np.float32)
    for place in range(per):
        eight[place, :, :, :, place] = core
    lines = per * GROUP
    eight = eight.reshape(2 * lines, 2 * lines)
    reach = tap_count * chan_len - HOP
    held = rows + 2
    columns = GROUP * SLOT
    groups = [[0], list(range(1, lane_tiles - 2)), [lane_tiles - 2]]
    parcels = [
        pltpu.VMEM((count, lines + GROUP * (group == groups[-1]), len(group) * LANE), jnp.bfloat16)
        for group in groups
    ]
    cfg = (tms, zooms, HOP, chan_len, reach, slots, KEEP, EDGE, folded, homes, needs, groups)
    lead = (columns // LANE - 1) * 2 * HOP
    depth = lead + -(-(3 * HOP + tap_count * chan_len) // LANE) * LANE
    turns = -(-(row_len - HOP + tap_count * chan_len) // row_len)
    bf, f32 = jnp.bfloat16, jnp.float32
    hbm = pl.BlockSpec(memory_space=pltpu.HBM)
    vmem = pl.BlockSpec(memory_space=pltpu.VMEM)
    result = pl.pallas_call(
        functools.partial(beam_kernel, cfg),
        out_shape=jax.ShapeDtypeStruct((2, 1, slots * KEEP), f32),
        in_specs=[hbm] * 8,
        out_specs=vmem,
        scratch_shapes=[
            pltpu.SMEM(band_starts.shape, jnp.int32),
            pltpu.SMEM(band_widths.shape, jnp.int32),
            pltpu.VMEM(section1_taps.shape, f32),
            pltpu.VMEM(section2_taps.shape, f32),
            pltpu.VMEM(twist.shape, f32),
            pltpu.VMEM(eight.shape, f32),
            pltpu.SemaphoreType.DMA((6,)),
            pltpu.VMEM((blocks, held, 2, LANE), bf),
            pltpu.VMEM((depth, LANE), bf),
            pltpu.VMEM((LANE, chan_len), f32),
            pltpu.VMEM((GROUP, lane_tiles * LANE), f32),
            pltpu.VMEM((GROUP, lane_tiles * LANE * GROUP // 2), f32),
            pltpu.VMEM((blocks, 2 * held, LANE), bf),
            pltpu.VMEM((turns, lane_tiles * LANE + 16, columns), f32),
            pltpu.VMEM((lane_tiles, columns, LANE), f32),
            parcels,
            parcels,
            pltpu.VMEM(table.shape, bf),
            pltpu.VMEM((2 * lines, freq), bf),
            pltpu.VMEM((slots + 2, 2 * GROUP, freq), bf),
            pltpu.VMEM((freq // LANE, (slots + 3) * 2 * GROUP, LANE), f32),
            pltpu.SemaphoreType.DMA((len(groups), blocks)),
            pltpu.SemaphoreType.DMA,
            pltpu.SemaphoreType.DMA((2, 2)),
            pltpu.SemaphoreType.DMA((len(groups), count)),
            pltpu.SemaphoreType.DMA((len(groups), count)),
            pltpu.SemaphoreType.DMA((4 * per,)),
            pltpu.SemaphoreType.DMA((slots + 2,)),
        ],
        compiler_params=pltpu.CompilerParams(
            collective_id=0, has_side_effects=True, vmem_limit_bytes=48 << 20
        ),
        name="beam",
    )(*[
        pltpu.with_memory_space_constraint(operand, pltpu.HBM)
        for operand in (band_starts, band_widths, section1_taps, section2_taps, twist, eight, signal, table)
    ])
    return result.reshape(1, 1, 2, 1, slots * KEEP)


def general(voltages, section1_taps, section2_taps, band_starts, band_widths):
    signal = voltages[0]
    tap_count, chan_len = section1_taps.shape
    spectra = signal.shape[1] // HOP
    rim_len = tap_count * chan_len - HOP
    tm_count = lax.axis_size("tm")
    zoom_count = lax.axis_size("zoom")
    device_count = tm_count * zoom_count
    slot_count = tm_count * CH_DEV
    width = CH_DEV + 2
    following = shifted(signal[:, :rim_len], ("tm", "zoom"), -1)
    span = slot_count + 2
    band_slots = jnp.arange(-1, slot_count + 1, dtype=jnp.int32)
    channels = ((band_starts[:, None] + band_slots[None, :]) % chan_len).reshape(-1)
    picks = [tm * CH_DEV + zoom * span for tm in range(tm_count) for zoom in range(zoom_count)]
    pieces = -(-chan_len // HOP)
    padded = jnp.concatenate(
        [signal, following, jnp.zeros((2, pieces * HOP), jnp.bfloat16)], axis=1
    )
    frames = weighted_frames(padded, section1_taps, spectra, HOP)
    coarse = jnp.einsum(
        "pqkn,qsn->pks", rotation_block(chan_len), frames, preferred_element_type=jnp.float32
    ).astype(jnp.bfloat16)
    wanted = np.arange(width)[:, None] + np.asarray(picks)[None, :]
    hot = channels[wanted.reshape(-1)][:, None] == jnp.arange(chan_len, dtype=jnp.int32)[None, :]
    packed = jnp.einsum(
        "lk,pks->pls", hot.astype(jnp.bfloat16), coarse, preferred_element_type=jnp.float32
    ).astype(jnp.bfloat16)
    packed = packed.reshape(2, width, device_count, spectra)
    received = lax.all_to_all(packed, ("tm", "zoom"), split_axis=2, concat_axis=2, tiled=True)
    series = received.reshape(2, width, -1)
    weighted, order = natural_order(series, section2_taps, FA, FB)
    spans = fine_spectra(weighted, order, KEEP, EDGE)
    slot_ids = lax.axis_index("tm") * CH_DEV + jnp.arange(CH_DEV, dtype=jnp.int32)
    band_ids = jnp.arange(band_widths.shape[0], dtype=jnp.int32)
    band_width = jnp.sum(jnp.where(band_ids == lax.axis_index("zoom"), band_widths, 0))
    upper_rim = spans[:, 2:, :, :EDGE]
    lower_rim = spans[:, :CH_DEV, :, KEEP + EDGE :]
    extended = spans[:, 1 : CH_DEV + 1]
    stitched = stitch_bands(extended, upper_rim, lower_rim, slot_ids, band_width, KEEP, EDGE)
    fine_count = stitched.shape[2]
    result = jnp.transpose(stitched, (0, 2, 1, 3)).reshape(2, fine_count, CH_DEV * KEEP)
    return result[None, None]


def on_device(voltages, section1_taps, section2_taps, band_starts, band_widths):
    chan_len = section1_taps.shape[1]
    tm_count, zoom_count = lax.axis_size("tm"), lax.axis_size("zoom")
    live = LIVE_DEV * tm_count * zoom_count
    row_len = GROUP * HOP
    fits = (
        zoom_count == 2
        and band_widths.shape[0] == 2
        and CH_DEV * tm_count <= live
        and live <= PART
        and chan_len & (chan_len - 1) == 0
        and voltages.shape[2] % row_len == 0
        and row_len % LANE == 0
        and voltages.shape[2] // row_len * tm_count * zoom_count * GROUP % section2_taps.shape[1] == 0
        and section1_taps.shape[0] * chan_len - HOP <= 2 * row_len
        and 0 < 2 * (voltages.shape[2] // row_len) % LANE <= LANE // (LIVE_DEV + 1)
        and 2 * (voltages.shape[2] // row_len) > 3 * LANE
        and section2_taps.shape[1] == FA * FB
        and section1_taps.shape[0] < 2 * GROUP
    )
    chosen = beam if fits else general
    return chosen(voltages, section1_taps, section2_taps, band_starts, band_widths)


def solution(mesh):
    placed = (P("pol", "groups", ("tm", "zoom")), P(), P(), P("groups"), P("groups"))
    return jax.shard_map(
        on_device,
        mesh=mesh,
        in_specs=placed,
        out_specs=P("pol", "zoom", "groups", None, "tm"),
        check_vma=False,
    )
```

```python
import functools
import math

import jax
import jax.numpy as jnp
import numpy as np
from jax import lax
from jax.experimental import pallas as pl
from jax.experimental.pallas import tpu as pltpu
from jax.sharding import PartitionSpec as P

HOP = 432
FA = 27
FB = 128
KEEP = 2916
EDGE = 128
CH_DEV = 5
LIVE_DEV = 3


def shifted(value, axis, steps):
    count = lax.axis_size(axis)
    initial, last = (max(0, -steps), min(count, count - steps))
    return lax.ppermute(value, axis, [(source, source + steps) for source in range(initial, last)])


def angle_table(rows, cols, length):
    product = (
        jnp.arange(rows, dtype=jnp.int32)[:, None]
        * jnp.arange(cols, dtype=jnp.int32)[None, :]
        % length
    )
    return product.astype(jnp.float32) * (2.0 * math.pi / length)


def rotation_block(length):
    angles = angle_table(length, length, length)
    cosine_tab = jnp.cos(angles).astype(jnp.bfloat16)
    sine_tab = jnp.sin(angles).astype(jnp.bfloat16)
    return jnp.stack([jnp.stack([cosine_tab, sine_tab]), jnp.stack([-sine_tab, cosine_tab])])


def frame_view(segment, spectra, chan_len, hop_len):
    pieces = -(-chan_len // hop_len)
    framed = segment[:, : (spectra + pieces - 1) * hop_len].reshape(
        segment.shape[0], spectra + pieces - 1, hop_len
    )
    joined = jnp.concatenate(
        [framed[:, offset : offset + spectra] for offset in range(pieces)], axis=2
    )
    return joined[:, :, :chan_len]


def weighted_frames(signal, taps, spectra, hop_len):
    chan_len = taps.shape[1]
    running = jnp.zeros((2, spectra, chan_len), jnp.float32)
    for tap_index in range(taps.shape[0]):
        frames = frame_view(signal[:, tap_index * chan_len :], spectra, chan_len, hop_len)
        running = running + taps[tap_index][None, None, :] * frames.astype(jnp.float32)
    return running.astype(jnp.bfloat16)


def natural_order(series, section2_taps, radix_a, radix_b):
    tap_count, fine_len = section2_taps.shape
    items = series.shape[1]
    row_count = series.shape[2] // fine_len
    spectra = row_count - tap_count + 1
    row_blocks = series.reshape(2, items, row_count, fine_len)
    running = jnp.zeros((2, items, spectra, fine_len), jnp.float32)
    for tap_index in range(tap_count):
        running = running + section2_taps[tap_index] * row_blocks[
            :, :, tap_index : tap_index + spectra
        ].astype(jnp.float32)
    weighted = running.astype(jnp.bfloat16).reshape(2, items, spectra, radix_a, radix_b)
    return weighted, np.arange(radix_b)


def ordered_angles(rows, order, length):
    product = (np.arange(rows)[:, None] * order[None, :] % length).astype(np.float32)
    return jnp.asarray(product) * (2.0 * math.pi / length)


def fine_spectra(weighted, order, keep_len, edge_len):
    _, items, spectra, radix_a, radix_b = weighted.shape
    fine_len = radix_a * radix_b
    partial_value = jnp.einsum(
        "pqkm,qcfmb->pcfkb", rotation_block(radix_a), weighted, preferred_element_type=jnp.float32
    )
    angles = ordered_angles(radix_a, order, fine_len)
    cosine_tab = jnp.cos(angles)
    sine_tab = jnp.sin(angles)
    real_part = partial_value[0] * cosine_tab + partial_value[1] * sine_tab
    imag_part = partial_value[1] * cosine_tab - partial_value[0] * sine_tab
    twiddled = jnp.concatenate([real_part, imag_part], axis=-1).astype(jnp.bfloat16)
    turned = ordered_angles(radix_b, order, radix_b).T
    cosine_b = jnp.cos(turned).astype(jnp.bfloat16)
    sine_b = jnp.sin(turned).astype(jnp.bfloat16)
    table = jnp.concatenate(
        [jnp.stack([cosine_b, -sine_b], axis=1), jnp.stack([sine_b, cosine_b], axis=1)], axis=0
    )
    spectrum = jnp.einsum(
        "cfkm,mpq->pcfqk", twiddled, table, preferred_element_type=jnp.float32
    ).reshape(2, items, spectra, fine_len)
    first = (-(keep_len // 2) - edge_len) % fine_len
    rest = keep_len + 2 * edge_len - (fine_len - first)
    return jnp.concatenate([spectrum[..., first:], spectrum[..., :rest]], axis=-1)


def stitch_bands(extended, upper_rim, lower_rim, slot_ids, band_width, keep_len, edge_len):
    centre = extended[..., edge_len : edge_len + keep_len]
    live = (slot_ids < band_width).astype(jnp.float32)[None, :, None, None]
    upper_ok = (slot_ids + 1 < band_width).astype(jnp.float32)[None, :, None, None]
    lower_ok = ((slot_ids >= 1) & (slot_ids < band_width)).astype(jnp.float32)[None, :, None, None]
    ramp = (jnp.arange(edge_len, dtype=jnp.float32) + 0.5) / (2.0 * edge_len)
    upper_weight = ramp * upper_ok
    lower_weight = ramp[::-1] * lower_ok
    low_part = centre[..., :edge_len] * (1.0 - lower_weight) + lower_rim * lower_weight
    high_part = centre[..., keep_len - edge_len :] * (1.0 - upper_weight) + upper_rim * upper_weight
    joined = jnp.concatenate(
        [low_part, centre[..., edge_len : keep_len - edge_len], high_part], axis=-1
    )
    return joined * live


GROUP = 8
LANE = 128
SLOT = 64
PART = 32


def sine(x):
    square = x * x
    total = jnp.full_like(x, -1.0 / 39916800.0)
    for factor in (1.0 / 362880.0, -1.0 / 5040.0, 1.0 / 120.0, -1.0 / 6.0, 1.0):
        total = total * square + factor
    return total * x


def fill_bank(starts_ref, widths_ref, taps_ref, rot_len, hop, lead, live, bank, spread):
    lanes = lax.broadcasted_iota(jnp.int32, (LANE, LANE), 1)
    upper = lanes // SLOT
    quarter = (lanes % SLOT) // PART
    member = lanes % PART
    channel = jnp.where(
        member < widths_ref[0], starts_ref[0] + member, starts_ref[1] + (live - 1) - member
    )
    rows_of = lax.broadcasted_iota(jnp.int32, (LANE, LANE), 0)
    steps = -(-(taps_ref.shape[0] + 1) // GROUP) * GROUP
    filling = jnp.zeros((steps - taps_ref.shape[0], rot_len), jnp.float32)
    taps = jnp.concatenate([taps_ref[...], filling], axis=0)
    rolled = pltpu.roll(taps, hop, 1)
    down = pltpu.roll(rolled, 1, 0)
    behind = jnp.where(lax.broadcasted_iota(jnp.int32, rolled.shape, 1) < hop, down, rolled)
    value = jnp.concatenate([taps, behind], axis=0)
    parts = 3
    for part in range(parts):
        head = value.astype(jnp.bfloat16).astype(jnp.float32)
        spread[pl.ds(part * 2 * steps, 2 * steps), :] = head
        value = value - head
    spent = parts * 2 * steps
    spread[pl.ds(spent, LANE - spent), :] = jnp.zeros((LANE - spent, rot_len), jnp.float32)
    half = rot_len // 2
    turned, rots = [], []
    for block in range(rot_len // LANE):
        turned.append(jnp.transpose(spread[:, pl.ds(block * LANE, LANE)]))
        place = rows_of + block * LANE - upper * hop
        turn = (place * channel - quarter * (rot_len // 4)) & (rot_len - 1)
        angle = (jnp.abs(turn - half) - half // 2).astype(jnp.float32) * (2.0 * math.pi / rot_len)
        rots.append(sine(angle).astype(jnp.bfloat16).astype(jnp.float32))
    left = jnp.concatenate(turned, axis=0).astype(jnp.bfloat16)
    rot = jnp.concatenate(rots, axis=0)
    count = taps_ref.shape[0] + 1
    for tap in range(0, count, 2):
        group = range(tap, min(tap + 2, count))
        picks = [
            jnp.where((rows_of % (2 * steps) == one + upper * steps) & (rows_of < spent), 1.0, 0.0)
            for one in group
        ]
        taken = jnp.dot(
            left, jnp.concatenate(picks, axis=1).astype(jnp.bfloat16), preferred_element_type=jnp.float32
        )
        for index, one in enumerate(group):
            piece = taken[:, index * LANE : (index + 1) * LANE]
            bank[pl.ds(lead + one * rot_len, rot_len), :] = (piece * rot).astype(jnp.bfloat16)


def fill_taps(taps_ref, me, count, length, ground, tapw):
    fine_len = taps_ref.shape[1]
    whole = ground.shape[1]
    for device in range(count):

        @pl.when(me == device)
        def _():
            place, stop, pieces = device * length, (device + 1) * length, []
            while place < stop:
                row, lane = divmod(place, fine_len)
                size = min(fine_len - lane, stop - place)
                pieces.append(taps_ref[pl.ds(row, 1), :][:, lane : lane + size])
                place += size
            pieces.append(jnp.zeros((1, whole - length), jnp.float32))
            ground[...] = jnp.broadcast_to(jnp.concatenate(pieces, axis=1), ground.shape)

    span = LANE * GROUP // 2
    lanes = lax.broadcasted_iota(jnp.int32, (GROUP, span), 1)
    chosen = lanes % GROUP == lax.broadcasted_iota(jnp.int32, (GROUP, span), 0)
    parts = []
    for tile in range(whole // span):
        value = jnp.where(chosen, ground[:, pl.ds(tile * span, span)], 0.0)
        for _ in range(3):
            head = value.astype(jnp.bfloat16)
            parts.append(head.astype(jnp.float32))
            value = value - head.astype(jnp.float32)
    source = lax.broadcasted_iota(jnp.int32, (span, LANE), 0) // GROUP
    target = lax.broadcasted_iota(jnp.int32, (span, LANE), 1) // 2
    moved = jnp.where(source == target, 1.0, 0.0).astype(jnp.bfloat16)
    placed = jnp.dot(
        jnp.concatenate(parts, axis=0).astype(jnp.bfloat16), moved, preferred_element_type=jnp.float32
    )
    for tile in range(whole // span):
        row = 3 * GROUP * tile
        tapw[:, pl.ds(tile * LANE, LANE)] = (
            placed[row : row + GROUP]
            + placed[row + GROUP : row + 2 * GROUP]
            + placed[row + 2 * GROUP : row + 3 * GROUP]
        )


def beam_kernel(
    cfg,
    starts_in,
    widths_in,
    taps_in,
    fine_taps_in,
    twist_in,
    eight_in,
    x_ref,
    table_ref,
    out_ref,
    starts_ref,
    widths_ref,
    taps_ref,
    fine_taps_ref,
    twist_ref,
    eight_ref,
    small_sems,
    data,
    bank,
    spread,
    tapw_ref,
    ground,
    native,
    total,
    turned,
    sends,
    recvs,
    table,
    pair,
    gathered,
    flat,
    x_sems,
    table_sem,
    halo_sems,
    send_sems,
    recv_sems,
    out_sems,
    in_sems,
):
    tms, zooms, hop, rot_len, reach, slots, keep, edge, folded, homes, needs, groups = cfg
    per = len(homes[0])
    live = per * len(homes)
    rows, blocks = x_ref.shape[0], x_ref.shape[1]
    row_len = blocks * LANE
    count = tms * zooms
    tm = lax.axis_index("tm")
    zoom = lax.axis_index("zoom")
    me = tm * zooms + zoom
    gathered[...] = jnp.zeros_like(gathered)
    barrier = pltpu.get_barrier_semaphore()

    def where_is(index):
        return {"tm": index // zooms, "zoom": lax.rem(index, zooms)}

    for step in range(1, count):
        pl.semaphore_signal(
            barrier,
            inc=1,
            device_id=where_is(lax.rem(me + step, count)),
            device_id_type=pl.DeviceIdType.MESH,
        )
    smalls = [
        pltpu.make_async_copy(source, target, small_sems.at[index])
        for index, (source, target) in enumerate(
            (
                (starts_in, starts_ref),
                (widths_in, widths_ref),
                (taps_in, taps_ref),
                (fine_taps_in, fine_taps_ref),
                (twist_in, twist_ref),
                (eight_in, eight_ref),
            )
        )
    ]
    for copy in smalls:
        copy.start()
    held = data.shape[1]
    cuts = [0] + [(group[-1] * LANE + LANE + 16) // 2 for group in groups[:-1]] + [held]
    spans = [(low, min(high, rows) - low) for low, high in zip(cuts[:-1], cuts[1:])]
    loads = []
    for which, (start, size) in enumerate(spans):
        loads.append([])
        for block in range(blocks):
            copy = pltpu.make_async_copy(
                x_ref.at[pl.ds(start, size), block],
                data.at[block, pl.ds(start, size)],
                x_sems.at[which, block],
            )
            loads[which].append(copy)
    for copy in loads[0]:
        copy.start()
    table_copy = pltpu.make_async_copy(table_ref, table, table_sem)
    table_copy.start()
    rest = -(-(reach - row_len) // LANE)
    data[pl.ds(rest, blocks - rest), pl.ds(rows + 1, 1)] = jnp.zeros(
        (blocks - rest, 1, 2, LANE), data.dtype
    )

    @pl.when(me == count - 1)
    def _():
        data[:, pl.ds(rows, 1)] = jnp.zeros((blocks, 1, 2, LANE), data.dtype)
        data[pl.ds(0, rest), pl.ds(rows + 1, 1)] = jnp.zeros((rest, 1, 2, LANE), data.dtype)

    columns = GROUP * SLOT
    wide = 2 * LANE
    tiles = columns // wide
    apart = 2 * hop
    lead = (columns // LANE - 1) * apart
    turns = total.shape[0]
    total[:, pl.ds(2 * held, total.shape[1] - 2 * held), :] = jnp.zeros(
        (turns, total.shape[1] - 2 * held, columns), jnp.float32
    )
    bank[pl.ds(0, lead), :] = jnp.zeros((lead, LANE), jnp.bfloat16)
    tail = lead + (taps_ref.shape[0] + 1) * rot_len
    bank[pl.ds(tail, bank.shape[0] - tail), :] = jnp.zeros((bank.shape[0] - tail, LANE), jnp.bfloat16)
    for copy in smalls:
        copy.wait()
    fill_bank(
        starts_ref, widths_ref, taps_ref, rot_len, hop, lead, live, bank, spread
    )
    pl.semaphore_wait(barrier, count - 1)
    before = lax.rem(me + count - 1, count)
    halo = [
        pltpu.make_async_remote_copy(
            src_ref=source,
            dst_ref=target,
            send_sem=halo_sems.at[0, index],
            recv_sem=halo_sems.at[1, index],
            device_id=where_is(before),
            device_id_type=pl.DeviceIdType.MESH,
        )
        for index, (source, target) in enumerate(
            (
                (x_ref.at[0], data.at[:, rows]),
                (x_ref.at[1, pl.ds(0, rest)], data.at[pl.ds(0, rest), rows + 1]),
            )
        )
    ]

    @pl.when(me > 0)
    def _():
        for copy in halo:
            copy.start()

    def multiply(start, size):
        for block in range(blocks):
            native[block, pl.ds(2 * start, 2 * size), :] = data.at[block, pl.ds(start, size)].reshape(
                2 * size, LANE
            )[...]
        for tile in range(tiles):
            low = tile * 2 * apart
            high = low + 3 * hop + reach + hop
            for turn in range(turns):
                one = max(turn * blocks, low // LANE)
                end = min((turn + 1) * blocks, -(-high // LANE))
                picks = range(one, end)
                left = jnp.concatenate(
                    [
                        native[block - turn * blocks, pl.ds(2 * start, 2 * size), :]
                        for block in picks
                    ],
                    axis=1,
                )
                right = jnp.concatenate(
                    [
                        bank[pl.ds(lead + one * LANE - (2 * tile + part) * apart, (end - one) * LANE), :]
                        for part in range(2)
                    ],
                    axis=1,
                )
                total[turn, pl.ds(2 * start, 2 * size), pl.ds(tile * wide, wide)] = jnp.dot(
                    left, right, preferred_element_type=jnp.float32
                )

    def turn_round(tile):
        row = tile * LANE
        for col in range(columns // LANE):
            whole = total[0, pl.ds(row, LANE), pl.ds(col * LANE, LANE)]
            for turn in range(1, turns):
                whole += total[turn, pl.ds(row + 2 * turn, LANE), pl.ds(col * LANE, LANE)]
            turned[tile, pl.ds(col * LANE, LANE), :] = jnp.transpose(whole)

    even = lax.broadcasted_iota(jnp.int32, (GROUP, LANE), 1) % 2 == 0

    def line_of(tile, line):
        cosine = turned[tile, pl.ds(line, GROUP, stride=SLOT), :]
        sine_part = turned[tile, pl.ds(PART + line, GROUP, stride=SLOT), :]
        swapped_part = jnp.where(
            even, pltpu.roll(sine_part, LANE - 1, 1), -pltpu.roll(sine_part, 1, 1)
        )
        return (cosine + swapped_part) * tapw_ref[:, pl.ds(tile * LANE, LANE)]

    def pack(out, first, tile_ids, extra):
        for dest in range(count):
            for tile in tile_ids:
                values = [line_of(tile, line) for line in homes[dest]]
                if extra and tile == first:
                    value = line_of(lane_tiles - 1, homes[dest][0])
                    for place in range(1, per):
                        moved = line_of(lane_tiles - 1, homes[dest][place])
                        value += pltpu.roll(moved, place * last_width, 1)
                    values.append(value)
                elif extra:
                    values.append(jnp.zeros((GROUP, LANE), jnp.float32))
                value = jnp.concatenate(values, axis=0)
                out[dest, :, pl.ds((tile - first) * LANE, LANE)] = value.astype(jnp.bfloat16)

    def exchange(which, source, target):
        copies = []
        for step in sorted(range(1, count), key=lambda step: abs(2 * step - count)):
            other = lax.rem(me + step, count)
            copy = pltpu.make_async_remote_copy(
                src_ref=source.at[other],
                dst_ref=target.at[me],
                send_sem=send_sems.at[which, step],
                recv_sem=recv_sems.at[which, step],
                device_id=where_is(other),
                device_id_type=pl.DeviceIdType.MESH,
            )
            copy.start()
            copies.append(copy)
        target[me] = source[me]
        return copies

    lane_tiles = turned.shape[0]
    lines = per * GROUP
    last_width = LANE // (per + 1)
    copies = []
    for index, group in enumerate(groups):
        ending = index == len(groups) - 1
        for copy in loads[index]:
            copy.wait()
        if not ending:
            for copy in loads[index + 1]:
                copy.start()
        else:

            @pl.when(me > 0)
            def _():
                for copy in halo:
                    copy.wait_send()

            @pl.when(me < count - 1)
            def _():
                for copy in halo:
                    copy.wait_recv()

        multiply(cuts[index], cuts[index + 1] - cuts[index])
        if index == 0:
            fill_taps(fine_taps_ref, me, count, rows * GROUP, ground, tapw_ref)
        for tile in group + [lane_tiles - 1] * ending:
            turn_round(tile)
        pack(sends[index], group[0], group, ending)
        copies += exchange(index, sends[index], recvs[index])
    table_copy.wait()
    for copy in copies:
        copy.wait_recv()

    ring = -(-folded // LANE) + lane_tiles + 1
    sums = [None] * ring
    lane_ids = lax.broadcasted_iota(jnp.int32, (lines, LANE), 1)

    def put(tile, value):
        sums[tile] = value if sums[tile] is None else sums[tile] + value

    for source in range(count):
        offset = 2 * rows * source % folded
        base, shift = offset // LANE, offset % LANE
        for tile in range(lane_tiles):
            if tile < lane_tiles - 1:
                index = [tile in group for group in groups].index(True)
                piece = recvs[index][source, :, pl.ds((tile - groups[index][0]) * LANE, LANE)]
                piece = piece.astype(jnp.float32)[:lines]
            else:
                piece = recvs[-1][source, :, pl.ds(0, LANE)].astype(jnp.float32)[lines:]
                piece = jnp.concatenate(
                    [piece] + [pltpu.roll(piece, LANE - place * last_width, 1) for place in range(1, per)],
                    axis=0,
                )
                piece = jnp.where(lane_ids < last_width, piece, 0.0)
            if shift:
                piece = pltpu.roll(piece, shift, 1)
                put(base + tile, jnp.where(lane_ids >= shift, piece, 0.0))
                put(base + tile + 1, jnp.where(lane_ids < shift, piece, 0.0))
            else:
                put(base + tile, piece)
    base, shift = folded // LANE, folded % LANE
    for tile in range(base, ring):
        if sums[tile] is None:
            continue
        value = pltpu.roll(sums[tile], LANE - shift, 1) if shift else sums[tile]
        if shift and tile > base:
            put(tile - base - 1, jnp.where(lane_ids >= LANE - shift, value, 0.0))
        put(tile - base, jnp.where(lane_ids < LANE - shift, value, 0.0))
    used = -(-folded // LANE)
    weighted = jnp.concatenate(sums[:used], axis=1).astype(jnp.bfloat16)
    freq = table.shape[1] // 2
    partial_value = jnp.dot(weighted, table[...], preferred_element_type=jnp.float32)
    real, imag = partial_value[:, :freq], partial_value[:, freq:]
    cosine = jnp.concatenate([twist_ref[0]] * per, axis=0)
    sine_part = jnp.concatenate([twist_ref[1]] * per, axis=0)
    both = jnp.concatenate(
        [real * cosine + imag * sine_part, imag * cosine - real * sine_part], axis=0
    )
    spectrum = jnp.dot(
        eight_ref[...], both, preferred_element_type=jnp.float32, precision=lax.Precision.HIGHEST
    )
    pair[...] = spectrum.astype(jnp.bfloat16)
    high = 2 * GROUP

    sizes = [2 * LANE] + [freq] * slots + [LANE]

    def outward(source, target, index, device):
        return pltpu.make_async_remote_copy(
            src_ref=pair.at[pl.ds(source * high, high), pl.ds(0, sizes[target])],
            dst_ref=gathered.at[target, :, pl.ds(0, sizes[target])],
            send_sem=out_sems.at[index],
            recv_sem=in_sems.at[target],
            device_id={"tm": device // zooms, "zoom": device % zooms},
            device_id_type=pl.DeviceIdType.MESH,
        )

    for device in range(count):
        sent = [
            (place, target, other)
            for place, line in enumerate(homes[device])
            for other in range(count)
            for target in range(slots + 2)
            if needs[other][target] == line and other != device
        ]
        sent.sort(key=lambda item: -abs(item[2] // zooms - device // zooms))
        kept = [
            (homes[device].index(line), target)
            for target, line in enumerate(needs[device])
            if line in homes[device]
        ]
        taken = [
            target
            for target, line in enumerate(needs[device])
            if line is not None and line not in homes[device]
        ]

        @pl.when(me == device)
        def _():
            leaving = [
                outward(place, target, index, other)
                for index, (place, target, other) in enumerate(sent)
            ]
            for copy in leaving:
                copy.start()
            for place, target in kept:
                gathered[target] = pair[pl.ds(place * high, high)]
            for target in taken:
                outward(0, target, 0, (device + 1) % count).wait_recv()
            for copy in leaving:
                copy.wait_send()

    width = widths_ref[0] + zoom * (widths_ref[1] - widths_ref[0])
    for item in range(slots + 2):
        slot = tm * slots + item - 1
        real = ((slot >= 0) & (slot < width)).astype(jnp.int32)
        live_here = jnp.full((high, freq), real, jnp.int32) > 0
        value = jnp.where(live_here, gathered[item].astype(jnp.float32), 0.0)
        for tile in range(freq // LANE):
            flat[tile, pl.ds(item * high, high), :] = value[:, tile * LANE : (tile + 1) * LANE]
    for copy in copies:
        copy.wait_send()
    stitch(flat, out_ref, width, tm * slots, slots, keep, edge, folded // 2)


def stitch(flat, out_ref, width, first, slots, keep, edge, freq):
    lines = 2 * GROUP
    pieces = [
        [flat[tile, pl.ds(turn, lines, stride=GROUP), :] for tile in range(flat.shape[0])]
        for turn in range(GROUP)
    ]
    span = jnp.concatenate([jnp.concatenate(row, axis=1)[:, :freq] for row in pieces], axis=1)
    slot = lax.broadcasted_iota(jnp.int32, (lines, edge), 0) // 2 - 1 + first
    low_ok = jnp.where((slot >= 1) & (slot < width), 1.0, 0.0)
    high_ok = jnp.where(slot + 1 < width, 1.0, 0.0)
    place = lax.broadcasted_iota(jnp.int32, (lines, edge), 1).astype(jnp.float32)
    ramp = (place + 0.5) / (2.0 * edge)
    fall = (edge - place - 0.5) / (2.0 * edge)
    under = pltpu.roll(span[:, keep + edge : keep + 2 * edge], 2, 0)
    over = pltpu.roll(span[:, :edge], lines - 2, 0)
    low_weight = fall * low_ok
    high_weight = ramp * high_ok
    head = span[:, edge : 2 * edge] * (1.0 - low_weight) + under * low_weight
    foot = span[:, keep : keep + edge] * (1.0 - high_weight) + over * high_weight
    kept = jnp.concatenate([head, span[:, 2 * edge : keep], foot], axis=1)
    joined = jnp.concatenate([kept[2 * slot + 2 : 2 * slot + 4] for slot in range(slots)], axis=1)
    for part in range(2):
        out_ref[part] = joined[part : part + 1]


def beam(voltages, section1_taps, section2_taps, band_starts, band_widths):
    tap_count, chan_len = section1_taps.shape
    tms, zooms = lax.axis_size("tm"), lax.axis_size("zoom")
    count = tms * zooms
    row_len = GROUP * HOP
    rows = voltages.shape[2] // row_len
    blocks = row_len // LANE
    signal = voltages[0].reshape(2, rows, blocks, LANE).transpose(1, 2, 0, 3)
    fine_len = section2_taps.shape[1]
    freq_count = fine_len // GROUP
    freq = -(-freq_count // LANE) * LANE
    lane_tiles = -(-2 * rows // LANE)
    shift = KEEP // 2 + EDGE
    bins = np.arange(freq_count) - shift
    spot = np.arange(freq_count)
    angles = 2.0 * np.pi * ((spot[:, None] * bins[None, :]) % freq_count) / freq_count
    folded = 2 * freq_count
    table = np.zeros((-(-folded // (2 * LANE)) * LANE, 2, 2, freq))
    table[:freq_count, 0, 0, :freq_count] = np.cos(angles)
    table[:freq_count, 0, 1, :freq_count] = -np.sin(angles)
    table[:freq_count, 1, 0, :freq_count] = np.sin(angles)
    table[:freq_count, 1, 1, :freq_count] = np.cos(angles)
    table = table.reshape(-1, 2 * freq)[: -(-folded // LANE) * LANE]
    table = jnp.asarray(table.astype(np.float32).astype(jnp.bfloat16))
    phases = 2.0 * np.pi * ((np.arange(GROUP)[:, None] * bins[None, :]) % fine_len) / fine_len
    twist = np.zeros((2, GROUP, freq), np.float32)
    twist[0, :, :freq_count] = np.cos(phases)
    twist[1, :, :freq_count] = np.sin(phases)
    slots = CH_DEV
    per = LIVE_DEV
    live = per * count

    def owners(line):
        return [slot // slots for slot in (line, live - 1 - line) if slot < slots * tms]

    order = sorted(range(live), key=lambda line: (sum(owners(line)) / len(owners(line)), line))
    homes = [order[per * device : per * device + per] for device in range(count)]
    needs = []
    for device in range(count):
        needed = [device // zooms * slots + item - 1 for item in range(slots + 2)]
        needed = [slot if 0 <= slot < slots * tms else None for slot in needed]
        flip = device % zooms
        needs.append([live - 1 - slot if flip and slot is not None else slot for slot in needed])
    wheel = 2.0 * np.pi * ((np.arange(GROUP)[:, None] * np.arange(GROUP)[None, :]) % GROUP) / GROUP
    core = np.zeros((2, GROUP, 2, GROUP))
    core[0, :, 0] = np.cos(wheel)
    core[0, :, 1] = np.sin(wheel)
    core[1, :, 0] = -np.sin(wheel)
    core[1, :, 1] = np.cos(wheel)
    eight = np.zeros((per, 2, GROUP, 2, per, GROUP), np.float32)
    for place in range(per):
        eight[place, :, :, :, place] = core
    lines = per * GROUP
    eight = eight.reshape(2 * lines, 2 * lines)
    reach = tap_count * chan_len - HOP
    held = rows + 2
    columns = GROUP * SLOT
    groups = [[0, 1], list(range(2, lane_tiles - 1))]
    parcels = [
        pltpu.VMEM((count, lines + GROUP * (group == groups[-1]), len(group) * LANE), jnp.bfloat16)
        for group in groups
    ]
    cfg = (tms, zooms, HOP, chan_len, reach, slots, KEEP, EDGE, folded, homes, needs, groups)
    lead = (columns // LANE - 1) * 2 * HOP
    depth = lead + -(-(3 * HOP + tap_count * chan_len) // LANE) * LANE
    turns = -(-(row_len - HOP + tap_count * chan_len) // row_len)
    bf, f32 = jnp.bfloat16, jnp.float32
    hbm = pl.BlockSpec(memory_space=pltpu.HBM)
    vmem = pl.BlockSpec(memory_space=pltpu.VMEM)
    result = pl.pallas_call(
        functools.partial(beam_kernel, cfg),
        out_shape=jax.ShapeDtypeStruct((2, 1, slots * KEEP), f32),
        in_specs=[hbm] * 8,
        out_specs=vmem,
        scratch_shapes=[
            pltpu.SMEM(band_starts.shape, jnp.int32),
            pltpu.SMEM(band_widths.shape, jnp.int32),
            pltpu.VMEM(section1_taps.shape, f32),
            pltpu.VMEM(section2_taps.shape, f32),
            pltpu.VMEM(twist.shape, f32),
            pltpu.VMEM(eight.shape, f32),
            pltpu.SemaphoreType.DMA((6,)),
            pltpu.VMEM((blocks, held, 2, LANE), bf),
            pltpu.VMEM((depth, LANE), bf),
            pltpu.VMEM((LANE, chan_len), f32),
            pltpu.VMEM((GROUP, lane_tiles * LANE), f32),
            pltpu.VMEM((GROUP, lane_tiles * LANE * GROUP // 2), f32),
            pltpu.VMEM((blocks, 2 * held, LANE), bf),
            pltpu.VMEM((turns, lane_tiles * LANE + 16, columns), f32),
            pltpu.VMEM((lane_tiles, columns, LANE), f32),
            parcels,
            parcels,
            pltpu.VMEM(table.shape, bf),
            pltpu.VMEM((2 * lines, freq), bf),
            pltpu.VMEM((slots + 2, 2 * GROUP, freq), bf),
            pltpu.VMEM((freq // LANE, (slots + 3) * 2 * GROUP, LANE), f32),
            pltpu.SemaphoreType.DMA((len(groups), blocks)),
            pltpu.SemaphoreType.DMA,
            pltpu.SemaphoreType.DMA((2, 2)),
            pltpu.SemaphoreType.DMA((len(groups), count)),
            pltpu.SemaphoreType.DMA((len(groups), count)),
            pltpu.SemaphoreType.DMA((4 * per,)),
            pltpu.SemaphoreType.DMA((slots + 2,)),
        ],
        compiler_params=pltpu.CompilerParams(
            collective_id=0, has_side_effects=True, vmem_limit_bytes=48 << 20
        ),
        name="beam",
    )(*[
        pltpu.with_memory_space_constraint(operand, pltpu.HBM)
        for operand in (band_starts, band_widths, section1_taps, section2_taps, twist, eight, signal, table)
    ])
    return result.reshape(1, 1, 2, 1, slots * KEEP)


def general(voltages, section1_taps, section2_taps, band_starts, band_widths):
    signal = voltages[0]
    tap_count, chan_len = section1_taps.shape
    spectra = signal.shape[1] // HOP
    rim_len = tap_count * chan_len - HOP
    tm_count = lax.axis_size("tm")
    zoom_count = lax.axis_size("zoom")
    device_count = tm_count * zoom_count
    slot_count = tm_count * CH_DEV
    width = CH_DEV + 2
    following = shifted(signal[:, :rim_len], ("tm", "zoom"), -1)
    span = slot_count + 2
    band_slots = jnp.arange(-1, slot_count + 1, dtype=jnp.int32)
    channels = ((band_starts[:, None] + band_slots[None, :]) % chan_len).reshape(-1)
    picks = [tm * CH_DEV + zoom * span for tm in range(tm_count) for zoom in range(zoom_count)]
    pieces = -(-chan_len // HOP)
    padded = jnp.concatenate(
        [signal, following, jnp.zeros((2, pieces * HOP), jnp.bfloat16)], axis=1
    )
    frames = weighted_frames(padded, section1_taps, spectra, HOP)
    coarse = jnp.einsum(
        "pqkn,qsn->pks", rotation_block(chan_len), frames, preferred_element_type=jnp.float32
    ).astype(jnp.bfloat16)
    wanted = np.arange(width)[:, None] + np.asarray(picks)[None, :]
    hot = channels[wanted.reshape(-1)][:, None] == jnp.arange(chan_len, dtype=jnp.int32)[None, :]
    packed = jnp.einsum(
        "lk,pks->pls", hot.astype(jnp.bfloat16), coarse, preferred_element_type=jnp.float32
    ).astype(jnp.bfloat16)
    packed = packed.reshape(2, width, device_count, spectra)
    received = lax.all_to_all(packed, ("tm", "zoom"), split_axis=2, concat_axis=2, tiled=True)
    series = received.reshape(2, width, -1)
    weighted, order = natural_order(series, section2_taps, FA, FB)
    spans = fine_spectra(weighted, order, KEEP, EDGE)
    slot_ids = lax.axis_index("tm") * CH_DEV + jnp.arange(CH_DEV, dtype=jnp.int32)
    band_ids = jnp.arange(band_widths.shape[0], dtype=jnp.int32)
    band_width = jnp.sum(jnp.where(band_ids == lax.axis_index("zoom"), band_widths, 0))
    upper_rim = spans[:, 2:, :, :EDGE]
    lower_rim = spans[:, :CH_DEV, :, KEEP + EDGE :]
    extended = spans[:, 1 : CH_DEV + 1]
    stitched = stitch_bands(extended, upper_rim, lower_rim, slot_ids, band_width, KEEP, EDGE)
    fine_count = stitched.shape[2]
    result = jnp.transpose(stitched, (0, 2, 1, 3)).reshape(2, fine_count, CH_DEV * KEEP)
    return result[None, None]


def on_device(voltages, section1_taps, section2_taps, band_starts, band_widths):
    chan_len = section1_taps.shape[1]
    tm_count, zoom_count = lax.axis_size("tm"), lax.axis_size("zoom")
    live = LIVE_DEV * tm_count * zoom_count
    row_len = GROUP * HOP
    fits = (
        zoom_count == 2
        and band_widths.shape[0] == 2
        and CH_DEV * tm_count <= live
        and live <= PART
        and chan_len & (chan_len - 1) == 0
        and voltages.shape[2] % row_len == 0
        and row_len % LANE == 0
        and voltages.shape[2] // row_len * tm_count * zoom_count * GROUP % section2_taps.shape[1] == 0
        and section1_taps.shape[0] * chan_len - HOP <= 2 * row_len
        and 0 < 2 * (voltages.shape[2] // row_len) % LANE <= LANE // (LIVE_DEV + 1)
        and 2 * (voltages.shape[2] // row_len) > 3 * LANE
        and section2_taps.shape[1] == FA * FB
        and section1_taps.shape[0] < 2 * GROUP
    )
    chosen = beam if fits else general
    return chosen(voltages, section1_taps, section2_taps, band_starts, band_widths)


def solution(mesh):
    placed = (P("pol", "groups", ("tm", "zoom")), P(), P(), P("groups"), P("groups"))
    return jax.shard_map(
        on_device,
        mesh=mesh,
        in_specs=placed,
        out_specs=P("pol", "zoom", "groups", None, "tm"),
        check_vma=False,
    )
```
